32 devices in a mesh: dp: 16 (over z, y, core), tensor: 2 (over x).
Axes of the slice: x: 2, y: 2, z: 4, core: 2. Of those that a mesh axis runs over, the one named last changes fastest.
Arguments:
- inputs: bfloat16 [2, 16, 512, 768], P(None, 'dp'), may hold values from -6 to 6
- lengths: int32 [2, 16], P(None, 'dp'), may hold values from 1 to 512, as said below
- buckets: int32 [512, 512], replicated, may hold values from 0 to 255
- w_query: bfloat16 [768, 768], P(None, 'tensor'), may hold values from -0.21875 to 0.21875
- b_query: float32 [768], P('tensor'), may hold values from -3 to 3
- w_key: bfloat16 [768, 768], P(None, 'tensor'), may hold values from -0.21875 to 0.21875
- w_value: bfloat16 [768, 768], P(None, 'tensor'), may hold values from -0.21875 to 0.21875
- b_value: float32 [768], P('tensor'), may hold values from -3 to 3
- w_out: bfloat16 [768, 768], P('tensor'), may hold values from -1.25 to 1.25
- b_out: float32 [768], replicated, may hold values from -2 to 2
- norm1_gain: float32 [768], replicated, may hold values from 0.5 to 1.5
- norm1_shift: float32 [768], replicated, may hold values from -2 to 2
- w_up: bfloat16 [768, 3072], P(None, 'tensor'), may hold values from -0.21875 to 0.21875
- b_up: float32 [3072], P('tensor'), may hold values from -3 to 3
- w_down: bfloat16 [3072, 768], P('tensor'), may hold values from -0.109375 to 0.109375
- b_down: float32 [768], replicated, may hold values from -2 to 2
- norm2_gain: float32 [768], replicated, may hold values from 0.5 to 1.5
- norm2_shift: float32 [768], replicated, may hold values from -2 to 2
- position_table: float32 [256, 12], P(None, 'tensor'), may hold values from -4 to 4
- cotangent: bfloat16 [2, 16, 512, 768], P(None, 'dp'), may hold values from -6 to 6
Outputs:
- layer_output: bfloat16 [2, 16, 512, 768], P(None, 'dp')
- grad_inputs: float32 [2, 16, 512, 768], P(None, 'dp')
- grad_w_query: float32 [768, 768], P(None, 'tensor')
- grad_b_query: float32 [768], P('tensor')
- grad_w_key: float32 [768, 768], P(None, 'tensor')
- grad_w_value: float32 [768, 768], P(None, 'tensor')
- grad_b_value: float32 [768], P('tensor')
- grad_w_out: float32 [768, 768], P('tensor')
- grad_b_out: float32 [768], replicated
- grad_norm1_gain: float32 [768], replicated
- grad_norm1_shift: float32 [768], replicated
- grad_w_up: float32 [768, 3072], P(None, 'tensor')
- grad_b_up: float32 [3072], P('tensor')
- grad_w_down: float32 [3072, 768], P('tensor')
- grad_b_down: float32 [768], replicated
- grad_norm2_gain: float32 [768], replicated
- grad_norm2_shift: float32 [768], replicated
- grad_position_table: float32 [256, 12], P(None, 'tensor')
The draws below stay inside these ranges and needn't reach their ends.
Inputs may be any that keep to these rules, and one draw needn't show every extreme that they name: `lengths`: A sequence's live tokens are its first ones. Most sequences have at most max(150, 2) live tokens; in every draw at least one sequence is 512 long.
All inputs are finite; a program needn't handle non-finite values.
Results may differ from the reference program's by a relative error of at most 0.018.
The reference program's roundings to bfloat16 on the way count: a program that leaves them out, or rounds other values in their place, can miss the bound.
Values may be sent and summed in bfloat16 or wider, within the bound.
No kernel may reach another device: no remote copies, remote signals or barrier semaphores. Data moves between devices by JAX's collectives and lax.ppermute only.
A program may use at most 192 MiB of HBM per device.

```python
import math
import jax
import jax.numpy as jnp
from jax import lax

D = 768
H = 12
HD = 64
FF = 3072
BUCKETS = 256
SEQ = 512
MICRO = 2
SEQS = 16
N_TENSOR = 2


def draw_lengths(key, part):
    short_top = max(SEQ * 150 // 512, 2)
    sequence_total = MICRO * SEQS
    key_short, key_full, key_chosen = jax.random.split(key, 3)
    short_lengths = jax.random.randint(key_short, (sequence_total,), 1, short_top + 1)
    is_full = jax.random.randint(key_full, (sequence_total,), 0, 16) == 0
    chosen = jax.random.randint(key_chosen, (), 0, sequence_total)
    forced = jnp.arange(sequence_total) == chosen
    lengths = jnp.where(is_full | forced, SEQ, short_lengths)
    return lengths.reshape(MICRO, SEQS).astype(jnp.int32)


def with_ends(values, own_key, low, top_value):
    dims = values.shape
    place = [jax.random.randint(jax.random.fold_in(own_key, axis), (), 0, dims[axis]) for axis in range(len(dims))]
    values = values.at[tuple(place)].set(low)
    longest = dims.index(max(dims))
    place[longest] = (place[longest] + 1) % dims[longest]
    return values.at[tuple(place)].set(top_value)


def block_scale(rng, extent, shards, smallest, top_value):
    loudness = 1.0
    for position, shards_of in shards:
        heights = jax.random.uniform(jax.random.fold_in(jax.random.fold_in(rng, 6), position), (shards_of,), jnp.float32, smallest / len(shards), top_value / len(shards))
        loudness = loudness * jnp.repeat(jnp.exp(heights), extent[position] // shards_of).reshape((-1,) + (1,) * (len(extent) - 1 - position))
    return loudness


def gaussian(rng, shape, width, most, shards=(), kind=jnp.bfloat16):
    factor_of = block_scale(rng, shape, shards, -0.22, 0.18) if shards else 1.0
    values = jax.random.normal(rng, shape, jnp.float32) * width * factor_of
    return jnp.minimum(jnp.maximum(values, -most), most).astype(kind)


def setup_inputs(seed: int = 0) -> dict:
    key_of = jax.random.split(jax.random.key(seed), 21)
    return {
        "inputs": gaussian(key_of[0], (MICRO, SEQS, SEQ, D), 1.0, 6.0, ((1, 16),)),
        "lengths": draw_lengths(jax.random.fold_in(key_of[20], 71), 0),
        "buckets": with_ends(jax.random.randint(key_of[2], (SEQ, SEQ), 0, BUCKETS), jax.random.fold_in(key_of[2], 1), 0, BUCKETS - 1).astype(jnp.int32),
        "w_query": gaussian(key_of[3], (D, H * HD), D ** -0.5, 0.21875, ((1, 2),)),
        "b_query": gaussian(key_of[4], (H * HD,), 0.5, 3.0, ((0, 2),), jnp.float32),
        "w_key": gaussian(key_of[5], (D, H * HD), D ** -0.5, 0.21875, ((1, 2),)),
        "w_value": gaussian(key_of[6], (D, H * HD), D ** -0.5, 0.21875, ((1, 2),)),
        "b_value": gaussian(key_of[7], (H * HD,), 0.5, 3.0, ((0, 2),), jnp.float32),
        "w_out": gaussian(key_of[8], (H * HD, D), (H * HD // 32) ** -0.5, 1.25, ((0, 2),)),
        "b_out": gaussian(key_of[9], (D,), 0.3, 2.0, (), jnp.float32),
        "norm1_gain": jnp.clip(1.0 + 0.1 * jax.random.normal(key_of[10], (D,), jnp.float32), 0.5, 1.5),
        "norm1_shift": gaussian(key_of[11], (D,), 0.3, 2.0, (), jnp.float32),
        "w_up": gaussian(key_of[12], (D, FF), D ** -0.5, 0.21875, ((1, 2),)),
        "b_up": gaussian(key_of[13], (FF,), 0.5, 3.0, ((0, 2),), jnp.float32),
        "w_down": gaussian(key_of[14], (FF, D), FF ** -0.5, 0.109375, ((0, 2),)),
        "b_down": gaussian(key_of[15], (D,), 0.3, 2.0, (), jnp.float32),
        "norm2_gain": jnp.clip(1.0 + 0.1 * jax.random.normal(key_of[16], (D,), jnp.float32), 0.5, 1.5),
        "norm2_shift": gaussian(key_of[17], (D,), 0.3, 2.0, (), jnp.float32),
        "position_table": gaussian(key_of[18], (BUCKETS, H), 1.0, 4.0, ((1, 2),), jnp.float32),
        "cotangent": gaussian(key_of[19], (MICRO, SEQS, SEQ, D), 1.0, 6.0, ((1, 16),)),
    }


@jax.custom_vjp
def low(v):
    return lax.optimization_barrier(v.astype(jnp.bfloat16)).astype(jnp.float32)

@jax.custom_vjp
def low_back(v):
    return v

def low_keep(v):
    return (low(v), None)

def low_pass(kept, grad):
    return (grad,)

def back_keep(v):
    return (v, None)

def back_low(kept, grad):
    return (low(grad),)
low.defvjp(low_keep, low_pass)
low_back.defvjp(back_keep, back_low)
highest = lax.Precision.HIGHEST
epsilon = 1e-05
masked_value = -1e+30

def both_round(value):
    return low_back(low(value))

def layer_norm(flat_rows, gain, shift):
    centre = flat_rows - lax.optimization_barrier(jnp.mean(flat_rows, axis=-1, keepdims=True))
    variance = lax.optimization_barrier(jnp.mean(centre * centre, axis=-1, keepdims=True))
    return centre * lax.rsqrt(variance + epsilon) * gain + shift

def group_forward(params, bias_heads, grouped_inputs, grouped_lengths):
    w_query, b_query, w_key, w_value, b_value, w_out, b_out, norm1_gain, norm1_shift, w_up, b_up, w_down, b_down, norm2_gain, norm2_shift = params
    group_size = grouped_inputs.shape[0]
    flat_rows = grouped_inputs.reshape(-1, D)
    queries = both_round(jnp.dot(flat_rows, w_query, precision=highest) + b_query).reshape(group_size, SEQ, H, HD)
    key_rows = both_round(jnp.dot(flat_rows, w_key, precision=highest)).reshape(group_size, SEQ, H, HD)
    value_rows = both_round(jnp.dot(flat_rows, w_value, precision=highest) + b_value).reshape(group_size, SEQ, H, HD)
    scores = low_back(HD ** (-0.5) * jnp.einsum('gqhd,gkhd->ghqk', queries, key_rows, precision=highest) + bias_heads[None])
    live_keys = jnp.arange(SEQ, dtype=jnp.int32)[None, :] < grouped_lengths[:, None]
    scores = jnp.where(live_keys[:, None, None, :], scores, masked_value)
    probabilities = low(jnp.exp(scores - jax.nn.logsumexp(scores, axis=-1, keepdims=True)))
    attended = both_round(jnp.einsum('ghqk,gkhd->gqhd', probabilities, value_rows, precision=highest))
    attended = attended.reshape(-1, N_TENSOR, H * HD // N_TENSOR)
    head_parts = jnp.einsum('rtc,tcd->trd', attended, w_out.reshape(N_TENSOR, H * HD // N_TENSOR, D), precision=highest)
    branch = low_back(lax.optimization_barrier(jnp.sum(low(head_parts), axis=0)) + b_out)
    hidden_one = layer_norm(flat_rows + branch, norm1_gain, norm1_shift)
    upper_pre = low_back(jnp.dot(low(hidden_one), w_up, precision=highest) + b_up)
    activated = low(jax.nn.gelu(upper_pre, approximate=False)).reshape(-1, N_TENSOR, FF // N_TENSOR)
    unit_parts = jnp.einsum('rtc,tcd->trd', activated, w_down.reshape(N_TENSOR, FF // N_TENSOR, D), precision=highest)
    ffn_out = low_back(lax.optimization_barrier(jnp.sum(low(unit_parts), axis=0)) + b_down)
    result = layer_norm(hidden_one + ffn_out, norm2_gain, norm2_shift)
    row_mask = live_keys.reshape(-1, 1).astype(result.dtype)
    return (result * row_mask).reshape(group_size, SEQ, D)

def reference(inputs, lengths, buckets, w_query, b_query, w_key, w_value, b_value, w_out, b_out, norm1_gain, norm1_shift, w_up, b_up, w_down, b_down, norm2_gain, norm2_shift, position_table, cotangent):
    params = tuple((array.astype(jnp.float32) for array in (w_query, b_query, w_key, w_value, b_value, w_out, b_out, norm1_gain, norm1_shift, w_up, b_up, w_down, b_down, norm2_gain, norm2_shift)))
    table = position_table.astype(jnp.float32)
    sequence_total = MICRO * SEQS
    per_group = math.gcd(sequence_total, max(1, 4096 // SEQ))
    checked_forward = jax.checkpoint(group_forward)

    def forward(inputs_wide, params, table):
        bias_heads = jnp.transpose(jnp.take(table, buckets, axis=0), (2, 0, 1))
        grouped = inputs_wide.reshape(sequence_total // per_group, per_group, SEQ, D)
        grouped_lengths = lengths.reshape(sequence_total // per_group, per_group)
        outputs = lax.map(lambda packed: checked_forward(params, bias_heads, packed[0], packed[1]), (grouped, grouped_lengths))
        return outputs.reshape(MICRO, SEQS, SEQ, D)
    result, pullback = jax.vjp(forward, inputs.astype(jnp.float32), params, table)
    grad_inputs, grad_params, grad_table = pullback(cotangent.astype(jnp.float32))
    return (result.astype(jnp.bfloat16), grad_inputs, grad_params[0], grad_params[1], grad_params[2], grad_params[3], grad_params[4], grad_params[5], grad_params[6], grad_params[7], grad_params[8], grad_params[9], grad_params[10], grad_params[11], grad_params[12], grad_params[13], grad_params[14], grad_table)
```

```python
import jax
import jax.numpy as jnp
from jax import lax
from jax.experimental import pallas as pl
from jax.experimental.pallas import tpu as pltpu
from jax.sharding import PartitionSpec as P

epsilon = 1e-05
masked_value = -1e30
inv_root_two = 0.7071067811865476
inv_root_tau = 0.3989422804014327

BLOCK = 128
CAPS = (2, 5, 8)
bf16 = jnp.bfloat16
f32 = jnp.float32
shape_of = jax.ShapeDtypeStruct

in_vmem = pl.BlockSpec(memory_space=pltpu.VMEM)
in_smem = pl.BlockSpec(memory_space=pltpu.SMEM)
in_any = pl.BlockSpec(memory_space=pl.ANY)


def rows_at(block, count=1):
    return pl.ds(pl.multiple_of(block * BLOCK, BLOCK), count * BLOCK)


def dot_nn(left, right):
    return lax.dot_general(left, right, (((1,), (0,)), ((), ())), preferred_element_type=f32)


def dot_nt(left, right):
    return lax.dot_general(left, right, (((1,), (1,)), ((), ())), preferred_element_type=f32)


def dot_tn(left, right):
    return lax.dot_general(left, right, (((0,), (0,)), ((), ())), preferred_element_type=f32)


def place_of(meta, block):
    second = (block >= meta[0]).astype(jnp.int32)
    return second, pl.multiple_of((block - second * meta[0]) * BLOCK, BLOCK)


def live_rows(meta, second, first_row):
    rows = lax.broadcasted_iota(jnp.int32, (BLOCK, 1), 0) + first_row
    return rows < meta[2 + second]


def zero_tail(meta, ref):
    def clear(block, unused):
        ref[rows_at(block), :] = jnp.zeros((BLOCK, ref.shape[1]), ref.dtype)
        return unused

    lax.fori_loop(meta[4], meta[5], clear, 0)


def piece_copies(meta, pieces, whole, sems, to_pieces):
    start = 0
    made = []
    for index, piece in enumerate(pieces):
        rows = piece.shape[0]
        part = whole.at[pl.ds(start, rows), :]
        pair = (part, piece) if to_pieces else (piece, part)
        made.append((start // BLOCK, pltpu.make_async_copy(pair[0], pair[1], sems.at[index])))
        start += rows
    return made


def start_copies(meta, made):
    for first, copy in made:
        @pl.when(meta[5] > first)
        def _():
            copy.start()


def wait_copies(meta, made):
    for first, copy in made:
        @pl.when(meta[5] > first)
        def _():
            copy.wait()


def by_length(meta, second, body):
    for blocks in (1, 2, 4):
        @pl.when(meta[second] == blocks)
        def _():
            body(blocks)


def by_cap(meta, body):
    for blocks in CAPS:
        @pl.when(meta[5] == blocks)
        def _():
            body(blocks * BLOCK)


def norm_forward(rows, gain, shift):
    centre = rows - jnp.mean(rows, axis=-1, keepdims=True)
    inverse = lax.rsqrt(jnp.mean(centre * centre, axis=-1, keepdims=True) + epsilon)
    normed = centre * inverse
    return normed, normed * gain + shift, inverse


def norm_back(grad_rows, normed, inverse, gain):
    scaled = grad_rows * gain
    first_mean = jnp.mean(scaled, axis=-1, keepdims=True)
    second_mean = jnp.mean(scaled * normed, axis=-1, keepdims=True)
    return inverse * (scaled - first_mean - normed * second_mean)


def attention_forward(
    meta, x, w_query, b_query, w_key, w_value, b_value, buckets, table,
    packed_x, query3, key3, value3, key_t, probs_t, piece0, piece1, piece2,
    bias, value_t, attended_t, attended, sems,
):
    heads = probs_t.shape[0]
    pairs = heads // 2
    scale = 0.125
    seq_len = x.shape[1]
    columns = seq_len // BLOCK

    def bias_rows(group, unused):
        rows = pl.ds(pl.multiple_of(group * 8, 8), 8)
        for column in range(columns):
            lanes = slice(column * BLOCK, (column + 1) * BLOCK)
            bucket = buckets[rows, lanes]
            low = bucket & 127
            upper = bucket >= 128
            for head in range(heads):
                first = jnp.broadcast_to(table[head : head + 1, :128], (8, 128))
                second = jnp.broadcast_to(table[head : head + 1, 128:], (8, 128))
                bias[head, rows, lanes] = jnp.where(
                    upper,
                    jnp.take_along_axis(second, low, axis=1, mode="promise_in_bounds"),
                    jnp.take_along_axis(first, low, axis=1, mode="promise_in_bounds"),
                )
        return unused

    lax.fori_loop(0, jnp.maximum(meta[0], meta[1]) * (BLOCK // 8), bias_rows, 0)

    def project(block, unused):
        second, first_row = place_of(meta, block)
        rows = rows_at(block)
        part = x[second, pl.ds(first_row, BLOCK), :]
        packed_x[rows, :] = part
        query = ((dot_nn(part, w_query[...]) + b_query[...]).astype(bf16).astype(f32) * scale).astype(bf16)
        key = dot_nn(part, w_key[...])
        value = dot_nn(part, w_value[...]) + b_value[...]
        key_t[:, rows] = key.T.astype(bf16)
        value_t[:, rows] = value.T.astype(bf16)
        key = key.astype(bf16)
        value = value.astype(bf16)
        for pair in range(pairs):
            lanes = slice(pair * 128, (pair + 1) * 128)
            query3[pair, rows, :] = query[:, lanes]
            key3[pair, rows, :] = key[:, lanes]
            value3[pair, rows, :] = value[:, lanes]
        return unused

    lax.fori_loop(0, meta[4], project, 0)

    def one_sequence(second, unused):
        offset = second * meta[0]
        length = meta[2 + second]

        def sized(blocks):
            count = blocks * BLOCK
            wide = min(count, 256)

            def one_head(head, unused):
                pair = head // 2
                lane = lax.broadcasted_iota(jnp.int32, (count, 128), 1)
                mine = (lane >= 64) == (head % 2 == 1)
                keys = jnp.where(mine, key3[pair, rows_at(offset, blocks), :], jnp.zeros((), bf16))
                values = value_t[pl.ds(pl.multiple_of(head * 64, 64), 64), rows_at(offset, blocks)]
                live = lax.broadcasted_iota(jnp.int32, (count, wide), 0) < length
                for column in range(count // wide):
                    lanes = slice(column * wide, (column + 1) * wide)
                    places = rows_at(offset + column * (wide // BLOCK), wide // BLOCK)
                    scores = dot_nt(keys, query3[pair, places, :]) + bias[head, :count, lanes]
                    scores = jnp.where(live, scores, masked_value)
                    top = jnp.max(scores, axis=0, keepdims=True)
                    powers = jnp.exp(scores - top)
                    total = jnp.sum(powers, axis=0, keepdims=True)
                    probs = (powers * (1.0 / total)).astype(bf16)
                    probs_t[head, rows_at(offset, blocks), lanes] = probs
                    attended_t[pl.ds(pl.multiple_of(head * 64, 64), 64), places] = dot_nn(values, probs)
                return unused

            lax.fori_loop(0, heads, one_head, 0)

        by_length(meta, second, sized)
        return unused

    lax.fori_loop(0, 2, one_sequence, 0)

    def turn(block, unused):
        attended[rows_at(block), :] = attended_t[:, rows_at(block)].T.astype(bf16)
        return unused

    lax.fori_loop(0, meta[4], turn, 0)
    zero_tail(meta, attended)
    zero_tail(meta, packed_x)
    made = piece_copies(meta, (piece0, piece1, piece2), attended, sems, True)
    start_copies(meta, made)
    wait_copies(meta, made)


def feed_forward(
    meta, x, own0, own1, own2, got0, got1, got2, w_out_own, w_out_got, b_out, gain, shift,
    w_up, b_up, w_down,
    normed1, inverse1, hidden_low, activated, slope, piece0, piece1, piece2,
    own, got, part, sems,
):
    own_copies = piece_copies(meta, (own0, own1, own2), own, sems.at[0], False)
    got_copies = piece_copies(meta, (got0, got1, got2), got, sems.at[1], False)
    start_copies(meta, own_copies)
    start_copies(meta, got_copies)
    wait_copies(meta, own_copies)
    wait_copies(meta, got_copies)
    width = w_up.shape[1]

    def one_block(block, unused):
        second, first_row = place_of(meta, block)
        rows = rows_at(block)
        head_own = dot_nn(own[rows, :], w_out_own[...]).astype(bf16).astype(f32)
        head_got = dot_nn(got[rows, :], w_out_got[...]).astype(bf16).astype(f32)
        branch = (head_own + head_got) + b_out[...]
        base = x[second, pl.ds(first_row, BLOCK), :].astype(f32) + branch
        normed, hidden, inverse = norm_forward(base, gain[...], shift[...])
        normed1[rows, :] = normed
        inverse1[rows, :] = jnp.broadcast_to(inverse, (BLOCK, 128))
        low = hidden.astype(bf16)
        hidden_low[rows, :] = low
        for column in range(width // 512):
            lanes = slice(column * 512, (column + 1) * 512)
            upper = dot_nn(low, w_up[:, lanes]) + b_up[:, lanes]
            normal = 0.5 * (1.0 + lax.erf(upper * inv_root_two))
            activated[rows, lanes] = (upper * normal).astype(bf16)
            slope[rows, lanes] = (
                normal + upper * inv_root_tau * jnp.exp(-0.5 * upper * upper)
            ).astype(bf16)
        part[rows, :] = dot_nn(activated[rows, :], w_down[...]).astype(bf16)
        return unused

    lax.fori_loop(0, meta[4], one_block, 0)
    zero_tail(meta, part)
    made = piece_copies(meta, (piece0, piece1, piece2), part, sems.at[0], True)
    start_copies(meta, made)
    zero_tail(meta, activated)
    zero_tail(meta, hidden_low)
    wait_copies(meta, made)


def second_norm(
    meta, cotangent, own0, own1, own2, got0, got1, got2, normed1, gain1, shift1, b_down, gain2, shift2,
    w_down, w_up, slope,
    layer_output, grad_y2, grad_ffn, grad_upper, sums, sums_up, piece0, piece1, piece2,
    own, got, part, sems,
):
    own_copies = piece_copies(meta, (own0, own1, own2), own, sems.at[0], False)
    got_copies = piece_copies(meta, (got0, got1, got2), got, sems.at[1], False)
    start_copies(meta, own_copies)
    start_copies(meta, got_copies)
    sums[...] = jnp.zeros(sums.shape, f32)
    sums_up[...] = jnp.zeros(sums_up.shape, f32)
    layer_output[...] = jnp.zeros(layer_output.shape, bf16)
    wait_copies(meta, own_copies)
    wait_copies(meta, got_copies)
    width = w_up.shape[1]

    def one_block(block, unused):
        second, first_row = place_of(meta, block)
        rows = rows_at(block)
        spot = pl.ds(first_row, BLOCK)
        live = live_rows(meta, second, first_row)
        ffn_out = (own[rows, :].astype(f32) + got[rows, :].astype(f32)) + b_down[...]
        hidden = normed1[rows, :] * gain1[...] + shift1[...]
        normed, result, inverse = norm_forward(hidden + ffn_out, gain2[...], shift2[...])
        layer_output[second, spot, :] = jnp.where(live, result, 0.0).astype(bf16)
        grad_result = jnp.where(live, cotangent[second, spot, :].astype(f32), 0.0)
        sums[0:1, :] += jnp.sum(grad_result * normed, axis=0, keepdims=True)
        sums[1:2, :] += jnp.sum(grad_result, axis=0, keepdims=True)
        grad = norm_back(grad_result, normed, inverse, gain2[...])
        grad_y2[rows, :] = grad
        low = grad.astype(bf16)
        grad_ffn[rows, :] = low
        sums[2:3, :] += jnp.sum(low.astype(f32), axis=0, keepdims=True)
        for column in range(width // 512):
            lanes = slice(column * 512, (column + 1) * 512)
            back = dot_nt(low, w_down[lanes, :]) * slope[rows, lanes].astype(f32)
            back = back.astype(bf16)
            grad_upper[rows, lanes] = back
            sums_up[:, lanes] += jnp.sum(back.astype(f32), axis=0, keepdims=True)
        part[rows, :] = dot_nt(grad_upper[rows, :], w_up[...]).astype(bf16)
        return unused

    lax.fori_loop(0, meta[4], one_block, 0)
    zero_tail(meta, part)
    made = piece_copies(meta, (piece0, piece1, piece2), part, sems.at[0], True)
    start_copies(meta, made)
    zero_tail(meta, grad_ffn)
    zero_tail(meta, grad_upper)
    wait_copies(meta, made)


def ffn_weights(meta, slots, activated, grad_ffn, hidden_low, grad_upper, chunks, stacked):
    width = grad_ffn.shape[1]
    units = activated.shape[1]

    def sized(count):
        def down(tile, unused):
            lanes = pl.ds(pl.multiple_of(tile * 256, 256), 256)
            stacked[lanes, :] = dot_tn(activated[:count, lanes], grad_ffn[:count, :])
            return unused

        lax.fori_loop(0, units // 256, down, 0)

        def up(tile, unused):
            lanes = pl.ds(pl.multiple_of(tile * 256, 256), 256)
            product = dot_tn(hidden_low[:count, lanes], grad_upper[:count, :])
            for half in range(units // width):
                spot = pl.ds(pl.multiple_of(units + half * width + tile * 256, 256), 256)
                stacked[spot, :] = product[:, half * width : (half + 1) * width]
            return unused

        lax.fori_loop(0, width // 256, up, 0)

    by_cap(meta, sized)
    scatter_chunks(slots, chunks, stacked)


def scatter_chunks(slots, chunks, stacked):
    rows = chunks.shape[1]

    def move(index, unused):
        chunks[slots[index]] = stacked[pl.ds(pl.multiple_of(index * rows, 8), rows), :].astype(bf16)
        return unused

    lax.fori_loop(0, chunks.shape[0], move, 0)


def attention_backward(
    meta, own0, own1, own2, got0, got1, got2, grad_y2, normed1, inverse1, gain1,
    w_out, w_query, w_key, w_value, query3, key3, value3, key_t, probs_t,
    grad_y1, grad_branch, grad_qkv, grad_scores_t, sums, sums_qv, piece0, piece1, piece2,
    own, got, part, grad_attended, grad_query_t, grad_key, grad_value, sems,
):
    own_copies = piece_copies(meta, (own0, own1, own2), own, sems.at[0], False)
    got_copies = piece_copies(meta, (got0, got1, got2), got, sems.at[1], False)
    start_copies(meta, own_copies)
    start_copies(meta, got_copies)
    sums[...] = jnp.zeros(sums.shape, f32)
    sums_qv[...] = jnp.zeros(sums_qv.shape, f32)
    wait_copies(meta, own_copies)
    wait_copies(meta, got_copies)
    heads = probs_t.shape[0]
    pairs = heads // 2
    local = heads * 64
    scale = 0.125

    def first_norm(block, unused):
        rows = rows_at(block)
        grad_hidden = (own[rows, :].astype(f32) + got[rows, :].astype(f32)) + grad_y2[rows, :]
        normed = normed1[rows, :]
        sums[0:1, :] += jnp.sum(grad_hidden * normed, axis=0, keepdims=True)
        sums[1:2, :] += jnp.sum(grad_hidden, axis=0, keepdims=True)
        grad = norm_back(grad_hidden, normed, inverse1[rows, 0:1], gain1[...])
        grad_y1[rows, :] = grad
        low = grad.astype(bf16)
        grad_branch[rows, :] = low
        sums[2:3, :] += jnp.sum(low.astype(f32), axis=0, keepdims=True)
        back = dot_nt(low, w_out[...]).astype(bf16)
        for pair in range(pairs):
            grad_attended[pair, rows, :] = back[:, pair * 128 : (pair + 1) * 128]
            grad_key[pair, rows, :] = jnp.zeros((BLOCK, 128), f32)
            grad_value[pair, rows, :] = jnp.zeros((BLOCK, 128), f32)
        return unused

    lax.fori_loop(0, meta[4], first_norm, 0)

    def one_sequence(second, unused):
        offset = second * meta[0]

        def sized(blocks):
            count = blocks * BLOCK
            wide = min(count, 256)
            every = rows_at(offset, blocks)

            def one_head(head, unused):
                pair = head // 2
                lane = lax.broadcasted_iota(jnp.int32, (wide, 128), 1)
                mine = (lane >= 64) == (head % 2 == 1)
                head_rows = pl.ds(pl.multiple_of(head * 64, 64), 64)
                values = value3[pair, every, :]
                keys = key_t[head_rows, every]
                for column in range(count // wide):
                    lanes = slice(column * wide, (column + 1) * wide)
                    places = rows_at(offset + column * (wide // BLOCK), wide // BLOCK)
                    zero = jnp.zeros((), bf16)
                    back = jnp.where(mine, grad_attended[pair, places, :], zero)
                    queries = jnp.where(mine, query3[pair, places, :], zero)
                    grad_probs = dot_nt(values, back)
                    probs_low = probs_t[head, every, lanes]
                    probs = probs_low.astype(f32)
                    mean = jnp.sum(probs * grad_probs, axis=0, keepdims=True)
                    grad_scores = (probs * (grad_probs - mean)).astype(bf16)
                    grad_scores_t[head, every, lanes] = grad_scores
                    grad_value[pair, every, :] += dot_nn(probs_low, back)
                    grad_key[pair, every, :] += dot_nn(grad_scores, queries)
                    grad_query_t[head_rows, places] = dot_nn(keys, grad_scores)
                return unused

            lax.fori_loop(0, heads, one_head, 0)

        by_length(meta, second, sized)
        return unused

    lax.fori_loop(0, 2, one_sequence, 0)

    def gather_grads(block, unused):
        rows = rows_at(block)
        query = (grad_query_t[:, rows].T * scale).astype(bf16)
        grad_qkv[rows, :local] = query
        for pair in range(pairs):
            lanes = slice(pair * 128, (pair + 1) * 128)
            grad_qkv[rows, local + pair * 128 : local + (pair + 1) * 128] = grad_key[pair, rows, :].astype(bf16)
            value = grad_value[pair, rows, :].astype(bf16)
            grad_qkv[rows, 2 * local + pair * 128 : 2 * local + (pair + 1) * 128] = value
            sums_qv[1:2, lanes] += jnp.sum(value.astype(f32), axis=0, keepdims=True)
        sums_qv[0:1, :] += jnp.sum(query.astype(f32), axis=0, keepdims=True)
        total = dot_nt(query, w_query[...])
        total = total + dot_nt(grad_qkv[rows, local : 2 * local], w_key[...])
        total = total + dot_nt(grad_qkv[rows, 2 * local :], w_value[...])
        part[rows, :] = total.astype(bf16)
        return unused

    lax.fori_loop(0, meta[4], gather_grads, 0)
    zero_tail(meta, part)
    made = piece_copies(meta, (piece0, piece1, piece2), part, sems.at[0], True)
    start_copies(meta, made)
    zero_tail(meta, grad_qkv)
    zero_tail(meta, grad_branch)
    wait_copies(meta, made)


def attention_weights(meta, slots, packed_x, grad_qkv, own0, own1, own2, grad_branch, chunks, stacked, attended, sems):
    copies = piece_copies(meta, (own0, own1, own2), attended, sems, False)
    start_copies(meta, copies)
    width = packed_x.shape[1]
    local = attended.shape[1]
    wait_copies(meta, copies)

    def sized(count):
        def project(tile, unused):
            lanes = pl.ds(pl.multiple_of(tile * 256, 256), 256)
            product = dot_tn(packed_x[:count, lanes], grad_qkv[:count, :])
            for part in range(3):
                spot = pl.ds(pl.multiple_of(part * width + tile * 256, 256), 256)
                stacked[spot, :] = product[:, part * local : (part + 1) * local]
            return unused

        lax.fori_loop(0, width // 256, project, 0)
        product = dot_tn(attended[:count, :], grad_branch[:count, :])
        for half in range(width // local):
            first = 3 * width + half * local
            stacked[first : first + local, :] = product[:, half * local : (half + 1) * local]

    by_cap(meta, sized)
    scatter_chunks(slots, chunks, stacked)


def table_histogram(meta, grad_scores_t, buckets, total, left, right):
    heads = grad_scores_t.shape[0]
    seq_len = buckets.shape[1]
    group = 16
    total[...] = jnp.zeros(total.shape, f32)

    def one_sequence(second, unused):
        offset = second * meta[0]

        def sized(blocks):
            count = blocks * BLOCK
            digit = lax.broadcasted_iota(jnp.int32, (16, count), 0)

            def one_group(index, unused):
                rows = pl.ds(pl.multiple_of(index * group, group), group)
                spots = pl.ds(pl.multiple_of(offset * BLOCK + index * group, group), group)
                bucket = buckets[rows, :count]
                upper = bucket >> 4
                lower = bucket & 15
                grads = [grad_scores_t[head, spots, :count].astype(f32) for head in range(heads)]
                for row in range(group):
                    lanes = slice(row * count, (row + 1) * count)
                    left[:, lanes] = jnp.where(digit == upper[row : row + 1, :], 1.0, 0.0).astype(bf16)
                    chosen = digit == lower[row : row + 1, :]
                    for head in range(heads):
                        spread = jnp.where(chosen, grads[head][row : row + 1, :], 0.0)
                        right[head * 16 : (head + 1) * 16, lanes] = spread.astype(bf16)
                total[...] += dot_nt(right[:, : group * count], left[:, : group * count])
                return unused

            lax.fori_loop(0, count // group, one_group, 0)

        by_length(meta, second, sized)
        return unused

    lax.fori_loop(0, 2, one_sequence, 0)


def input_gradient(meta, grad_y1, own0, own1, own2, got0, got1, got2, out, own, got, sems):
    own_copies = piece_copies(meta, (own0, own1, own2), own, sems.at[0], False)
    got_copies = piece_copies(meta, (got0, got1, got2), got, sems.at[1], False)
    start_copies(meta, own_copies)
    start_copies(meta, got_copies)
    out[...] = jnp.zeros(out.shape, f32)
    wait_copies(meta, own_copies)
    wait_copies(meta, got_copies)

    def one_block(block, unused):
        second, first_row = place_of(meta, block)
        rows = rows_at(block)
        live = live_rows(meta, second, first_row)
        total = (own[rows, :].astype(f32) + got[rows, :].astype(f32)) + grad_y1[rows, :]
        out[second, pl.ds(first_row, BLOCK), :] = jnp.where(live, total, 0.0)
        return unused

    lax.fori_loop(0, meta[4], one_block, 0)


def unpack_ffn(places, *refs):
    chunks, (grad_up, grad_down) = refs[:-2], refs[-2:]
    rows = chunks[0].shape[0]
    units, width = grad_down.shape
    for index, chunk in enumerate(chunks):
        first = places[index] * rows
        values = chunk[...].astype(f32)

        @pl.when(first < units)
        def _():
            grad_down[pl.ds(pl.multiple_of(first, 8), rows), :] = values

        for half in range(units // width):
            low = units + half * width

            @pl.when((first >= low) & (first < low + width))
            def _():
                spot = pl.ds(pl.multiple_of(first - low, 8), rows)
                grad_up[spot, half * width : (half + 1) * width] = values


def unpack_attention(places, *refs):
    chunks, (grad_query, grad_key, grad_value, grad_out) = refs[:-4], refs[-4:]
    rows = chunks[0].shape[0]
    width, local = grad_query.shape
    for index, chunk in enumerate(chunks):
        first = places[index] * rows
        values = chunk[...].astype(f32)
        for part, target in enumerate((grad_query, grad_key, grad_value)):
            low = part * width

            @pl.when((first >= low) & (first < low + width))
            def _():
                target[pl.ds(pl.multiple_of(first - low, 8), rows), :] = values

        for half in range(width // local):
            low = 3 * width + half * local

            @pl.when((first >= low) & (first < low + local))
            def _():
                spot = pl.ds(pl.multiple_of(first - low, 8), rows)
                grad_out[spot, half * local : (half + 1) * local] = values


def run(kernel, specs, outs, scratch, name):
    params = pltpu.CompilerParams(vmem_limit_bytes=60 * 1024 * 1024)

    def call(*args):
        return pl.pallas_call(
            kernel,
            in_specs=[{"s": in_smem, "v": in_vmem, "a": in_any}[kind] for kind in specs],
            out_specs=[in_any if kind == "a" else in_vmem for kind, unused in outs],
            out_shape=[shape for unused, shape in outs],
            scratch_shapes=scratch,
            compiler_params=params,
            name=name,
        )(*args)

    return call


def swap_tensor(value):
    return lax.ppermute(value, "tensor", ((0, 1), (1, 0)))


def exchange(pieces, level):
    got0 = swap_tensor(pieces[0])
    got1, got2 = lax.switch(
        level,
        (
            lambda one, two: (one, two),
            lambda one, two: (swap_tensor(one), two),
            lambda one, two: (swap_tensor(one), swap_tensor(two)),
        ),
        pieces[1],
        pieces[2],
    )
    return got0, got1, got2


def ring_pairs(dp_count):
    chips = dp_count // 2
    order = list(range(0, chips, 2)) + list(range(chips - 1, 0, -2))
    pairs = []
    for place, chip in enumerate(order):
        after = order[(place + 1) % chips]
        pairs.append((2 * chip, 2 * after))
        pairs.append((2 * after + 1, 2 * chip + 1))
    return tuple(pairs)


def ring_places(dp_count):
    chips = dp_count // 2
    index = lax.axis_index("dp")
    chip, core = index // 2, index % 2
    forward = jnp.where(chip % 2 == 0, chip // 2, chips - 1 - chip // 2)
    own = jnp.where(core == 0, forward, (chips - forward) % chips)
    other = jnp.where(core == 0, (chips - forward) % chips, forward)
    steps = jnp.arange(chips, dtype=jnp.int32)
    own_slots = (own - steps) % chips
    other_slots = chips + (other - steps) % chips
    slots = jnp.where(core == 0, jnp.concatenate([own_slots, other_slots]), jnp.concatenate([other_slots, own_slots]))
    own_chunks = core * chips + (own - steps) % chips
    other_chunks = (1 - core) * chips + (other - steps) % chips
    return slots.astype(jnp.int32), jnp.concatenate([own_chunks, other_chunks]).astype(jnp.int32)


def reduce_chunks(chunks, dp_count):
    chips = dp_count // 2
    siblings = tuple((i, i ^ 1) for i in range(dp_count))
    pairs = ring_pairs(dp_count)
    got = lax.ppermute(chunks[chips:], "dp", siblings)

    def local(step):
        return chunks[step].astype(f32) + got[step].astype(f32)

    moving = local(0).astype(bf16)
    for step in range(1, chips):
        moving = (lax.ppermute(moving, "dp", pairs).astype(f32) + local(step)).astype(bf16)
    own = [None] * chips
    own[chips - 1] = moving
    for step in range(chips - 1):
        moving = lax.ppermute(moving, "dp", pairs)
        own[step] = moving
    other = [lax.ppermute(piece, "dp", siblings) for piece in own]
    return own + other


def sum_small(value, dp_count):
    bit = 1
    while bit < dp_count:
        value = value + lax.ppermute(value, "dp", tuple((i, i ^ bit) for i in range(dp_count)))
        bit *= 2
    return value


def per_device(dp_count, *arrays):
    (
        inputs, lengths, buckets, w_query, b_query, w_key, w_value, b_value, w_out, b_out, norm1_gain, norm1_shift,
        w_up, b_up, w_down, b_down, norm2_gain, norm2_shift, position_table, cotangent,
    ) = arrays
    micro, seqs, seq_len, width = inputs.shape
    bucket_count, heads = position_table.shape
    local = w_query.shape[1]
    units = w_up.shape[1]
    chips = dp_count // 2
    rows = micro * seq_len
    x = inputs.reshape(micro, seq_len, width)
    grad_out = cotangent.reshape(micro, seq_len, width)
    sizes = lengths[:, 0]
    blocks = jnp.where(sizes <= BLOCK, 1, jnp.where(sizes <= 2 * BLOCK, 2, 4))
    used = blocks[0] + blocks[1]
    level = (used > CAPS[0]).astype(jnp.int32) + (used > CAPS[1]).astype(jnp.int32)
    cap = jnp.where(level == 0, CAPS[0], jnp.where(level == 1, CAPS[1], CAPS[2]))
    meta = jnp.stack([blocks[0], blocks[1], sizes[0], sizes[1], used, cap, cap, cap]).astype(jnp.int32)
    slots, places = ring_places(dp_count)
    buckets_t = buckets.T
    table = position_table.T
    row = lambda vector: vector.reshape(1, -1)
    piece_rows = (CAPS[0] * BLOCK, (CAPS[1] - CAPS[0]) * BLOCK, rows - CAPS[1] * BLOCK)
    pieces = lambda columns: [("a", shape_of((count, columns), bf16)) for count in piece_rows]
    vmem = pltpu.VMEM
    dma = pltpu.SemaphoreType.DMA

    w_out_got = swap_tensor(w_out)
    packed_x, query3, key3, value3, key_t, probs_t, *attended = run(
        attention_forward,
        "svvvvvvvv",
        [
            ("v", shape_of((rows, width), bf16)),
            ("v", shape_of((heads // 2, rows, 128), bf16)),
            ("v", shape_of((heads // 2, rows, 128), bf16)),
            ("v", shape_of((heads // 2, rows, 128), bf16)),
            ("v", shape_of((local, rows), bf16)),
            ("v", shape_of((heads, rows, seq_len), bf16)),
            *pieces(local),
        ],
        [
            vmem((heads, seq_len, seq_len), f32),
            vmem((local, rows), bf16),
            vmem((local, rows), f32),
            vmem((rows, local), bf16),
            dma((3,)),
        ],
        "attention_forward",
    )(meta, x, w_query, row(b_query), w_key, w_value, row(b_value), buckets_t, table)
    attended_got = exchange(attended, level)

    normed1, inverse1, hidden_low, activated, slope, *unit_part = run(
        feed_forward,
        "svaaaaaavvvvvvvv",
        [
            ("v", shape_of((rows, width), f32)),
            ("v", shape_of((rows, 128), f32)),
            ("v", shape_of((rows, width), bf16)),
            ("v", shape_of((rows, units), bf16)),
            ("v", shape_of((rows, units), bf16)),
            *pieces(width),
        ],
        [vmem((rows, local), bf16), vmem((rows, local), bf16), vmem((rows, width), bf16), dma((2, 3))],
        "feed_forward",
    )(
        meta, x, *attended, *attended_got, w_out, w_out_got, row(b_out), row(norm1_gain), row(norm1_shift),
        w_up, row(b_up), w_down,
    )
    unit_got = exchange(unit_part, level)

    layer_output, grad_y2, grad_ffn, grad_upper, sums2, sums_up, *hidden_part = run(
        second_norm,
        "svaaaaaavvvvvvvvv",
        [
            ("v", shape_of((micro, seq_len, width), bf16)),
            ("v", shape_of((rows, width), f32)),
            ("v", shape_of((rows, width), bf16)),
            ("v", shape_of((rows, units), bf16)),
            ("v", shape_of((8, width), f32)),
            ("v", shape_of((1, units), f32)),
            *pieces(width),
        ],
        [vmem((rows, width), bf16), vmem((rows, width), bf16), vmem((rows, width), bf16), dma((2, 3))],
        "second_norm",
    )(
        meta, grad_out, *unit_part, *unit_got, normed1, row(norm1_gain), row(norm1_shift), row(b_down),
        row(norm2_gain), row(norm2_shift), w_down, w_up, slope,
    )
    hidden_got = exchange(hidden_part, level)

    stacked_ffn = 2 * units
    (ffn_chunks,) = run(
        ffn_weights,
        "ssvvvv",
        [("v", shape_of((2 * chips, stacked_ffn // (2 * chips), width), bf16))],
        [vmem((stacked_ffn, width), f32)],
        "ffn_weights",
    )(meta, slots, activated, grad_ffn, hidden_low, grad_upper)

    grad_y1, grad_branch, grad_qkv, grad_scores_t, sums1, sums_qv, *input_part = run(
        attention_backward,
        "saaaaaavvvvvvvvvvvvv",
        [
            ("v", shape_of((rows, width), f32)),
            ("v", shape_of((rows, width), bf16)),
            ("v", shape_of((rows, 3 * local), bf16)),
            ("v", shape_of((heads, rows, seq_len), bf16)),
            ("v", shape_of((8, width), f32)),
            ("v", shape_of((8, local), f32)),
            *pieces(width),
        ],
        [
            vmem((rows, width), bf16),
            vmem((rows, width), bf16),
            vmem((rows, width), bf16),
            vmem((heads // 2, rows, 128), bf16),
            vmem((local, rows), f32),
            vmem((heads // 2, rows, 128), f32),
            vmem((heads // 2, rows, 128), f32),
            dma((2, 3)),
        ],
        "attention_backward",
    )(
        meta, *hidden_part, *hidden_got, grad_y2, normed1, inverse1, row(norm1_gain), w_out, w_query, w_key, w_value,
        query3, key3, value3, key_t, probs_t,
    )
    input_got = exchange(input_part, level)

    stacked_attention = 3 * width + width * local // local
    (attention_chunks,) = run(
        attention_weights,
        "ssvvaaav",
        [("v", shape_of((2 * chips, stacked_attention // (2 * chips), local), bf16))],
        [vmem((stacked_attention, local), f32), vmem((rows, local), bf16), dma((3,))],
        "attention_weights",
    )(meta, slots, packed_x, grad_qkv, *attended, grad_branch)

    (table_sums,) = run(
        table_histogram,
        "svv",
        [("v", shape_of((16 * heads, 16), f32))],
        [vmem((16, 16 * seq_len), bf16), vmem((16 * heads, 16 * seq_len), bf16)],
        "table_histogram",
    )(meta, grad_scores_t, buckets_t)

    ffn_pieces = reduce_chunks(ffn_chunks, dp_count)
    attention_pieces = reduce_chunks(attention_chunks, dp_count)
    grad_w_up, grad_w_down = run(
        unpack_ffn,
        "s" + "v" * len(ffn_pieces),
        [("v", shape_of((width, units), f32)), ("v", shape_of((units, width), f32))],
        [],
        "unpack_ffn",
    )(places, *ffn_pieces)
    grad_w_query, grad_w_key, grad_w_value, grad_w_out = run(
        unpack_attention,
        "s" + "v" * len(attention_pieces),
        [("v", shape_of((width, local), f32))] * 3 + [("v", shape_of((local, width), f32))],
        [],
        "unpack_attention",
    )(places, *attention_pieces)

    (grad_inputs,) = run(
        input_gradient,
        "svaaaaaa",
        [("v", shape_of((micro, seq_len, width), f32))],
        [vmem((rows, width), bf16), vmem((rows, width), bf16), dma((2, 3))],
        "input_gradient",
    )(meta, grad_y1, *input_part, *input_got)

    table_part = table_sums.reshape(heads, 16, 16).transpose(2, 1, 0).reshape(bucket_count, heads)
    small = jnp.concatenate(
        [
            sums2[0], sums2[1], sums2[2], sums_up[0], sums1[0], sums1[1], sums1[2], sums_qv[0], sums_qv[1],
            table_part.reshape(-1),
        ]
    ).reshape(-1, 128)
    small = sum_small(small, dp_count).reshape(-1)
    cuts = []
    start = 0
    for count in (width, width, width, units, width, width, width, local, local, bucket_count * heads):
        cuts.append(small[start : start + count])
        start += count
    grad_gain2, grad_shift2, grad_b_down, grad_b_up, grad_gain1, grad_shift1, grad_b_out, grad_b_query, grad_b_value, table_grad = cuts
    return (
        layer_output.reshape(inputs.shape),
        grad_inputs.reshape(inputs.shape),
        grad_w_query,
        grad_b_query,
        grad_w_key,
        grad_w_value,
        grad_b_value,
        grad_w_out,
        grad_b_out,
        grad_gain1,
        grad_shift1,
        grad_w_up,
        grad_b_up,
        grad_w_down,
        grad_b_down,
        grad_gain2,
        grad_shift2,
        table_grad.reshape(bucket_count, heads),
    )


def solution(mesh):
    placed = (
        P(None, "dp", None, None),
        P(None, "dp"),
        P(),
        P(None, "tensor"),
        P("tensor"),
        P(None, "tensor"),
        P(None, "tensor"),
        P("tensor"),
        P("tensor", None),
        P(),
        P(),
        P(),
        P(None, "tensor"),
        P("tensor"),
        P("tensor", None),
        P(),
        P(),
        P(),
        P(None, "tensor"),
        P(None, "dp", None, None),
    )
    dp_count = mesh.shape["dp"]
    return jax.shard_map(
        lambda *arrays: per_device(dp_count, *arrays),
        mesh=mesh,
        in_specs=placed,
        out_specs=(
            P(None, "dp", None, None),
            P(None, "dp", None, None),
            P(None, "tensor"),
            P("tensor"),
            P(None, "tensor"),
            P(None, "tensor"),
            P("tensor"),
            P("tensor", None),
            P(),
            P(),
            P(),
            P(None, "tensor"),
            P("tensor"),
            P("tensor", None),
            P(),
            P(),
            P(),
            P(None, "tensor"),
        ),
        check_vma=False,
    )
```

```python
import jax
import jax.numpy as jnp
from jax import lax
from jax.experimental import pallas as pl
from jax.experimental.pallas import tpu as pltpu
from jax.sharding import PartitionSpec as P

epsilon = 1e-05
masked_value = -1e30
inv_root_two = 0.7071067811865476
inv_root_tau = 0.3989422804014327

BLOCK = 128
CAPS = (2, 5, 8)
bf16 = jnp.bfloat16
f32 = jnp.float32
shape_of = jax.ShapeDtypeStruct

in_vmem = pl.BlockSpec(memory_space=pltpu.VMEM)
in_smem = pl.BlockSpec(memory_space=pltpu.SMEM)
in_any = pl.BlockSpec(memory_space=pl.ANY)


def rows_at(block, count=1):
    return pl.ds(pl.multiple_of(block * BLOCK, BLOCK), count * BLOCK)


def dot_nn(left, right):
    return lax.dot_general(left, right, (((1,), (0,)), ((), ())), preferred_element_type=f32)


def dot_nt(left, right):
    return lax.dot_general(left, right, (((1,), (1,)), ((), ())), preferred_element_type=f32)


def dot_tn(left, right):
    return lax.dot_general(left, right, (((0,), (0,)), ((), ())), preferred_element_type=f32)


def place_of(meta, block):
    second = (block >= meta[0]).astype(jnp.int32)
    return second, pl.multiple_of((block - second * meta[0]) * BLOCK, BLOCK)


def live_rows(meta, second, first_row):
    rows = lax.broadcasted_iota(jnp.int32, (BLOCK, 1), 0) + first_row
    return rows < meta[2 + second]


def zero_tail(meta, ref):
    def clear(block, unused):
        ref[rows_at(block), :] = jnp.zeros((BLOCK, ref.shape[1]), ref.dtype)
        return unused

    lax.fori_loop(meta[4], meta[5], clear, 0)


def piece_copies(meta, pieces, whole, sems, to_pieces):
    start = 0
    made = []
    for index, piece in enumerate(pieces):
        rows = piece.shape[0]
        part = whole.at[pl.ds(start, rows), :]
        pair = (part, piece) if to_pieces else (piece, part)
        made.append((start // BLOCK, pltpu.make_async_copy(pair[0], pair[1], sems.at[index])))
        start += rows
    return made


def start_copies(meta, made):
    for first, copy in made:
        @pl.when(meta[5] > first)
        def _():
            copy.start()


def wait_copies(meta, made):
    for first, copy in made:
        @pl.when(meta[5] > first)
        def _():
            copy.wait()


def by_length(meta, second, body):
    for blocks in (1, 2, 4):
        @pl.when(meta[second] == blocks)
        def _():
            body(blocks)


def by_cap(meta, body):
    for blocks in CAPS:
        @pl.when(meta[5] == blocks)
        def _():
            body(blocks * BLOCK)


def norm_forward(rows, gain, shift):
    centre = rows - jnp.mean(rows, axis=-1, keepdims=True)
    inverse = lax.rsqrt(jnp.mean(centre * centre, axis=-1, keepdims=True) + epsilon)
    normed = centre * inverse
    return normed, normed * gain + shift, inverse


def norm_back(grad_rows, normed, inverse, gain):
    scaled = grad_rows * gain
    first_mean = jnp.mean(scaled, axis=-1, keepdims=True)
    second_mean = jnp.mean(scaled * normed, axis=-1, keepdims=True)
    return inverse * (scaled - first_mean - normed * second_mean)


def attention_forward(
    meta, x, w_query, b_query, w_key, w_value, b_value, buckets, table,
    packed_x, query3, key3, value3, key_t, probs_t, piece0, piece1, piece2,
    bias, value_t, attended_t, attended, sems,
):
    heads = probs_t.shape[0]
    pairs = heads // 2
    scale = 0.125
    seq_len = x.shape[1]
    columns = seq_len // BLOCK

    def bias_rows(group, unused):
        rows = pl.ds(pl.multiple_of(group * 8, 8), 8)
        for column in range(columns):
            lanes = slice(column * BLOCK, (column + 1) * BLOCK)
            bucket = buckets[rows, lanes]
            low = bucket & 127
            upper = bucket >= 128
            for head in range(heads):
                first = jnp.broadcast_to(table[head : head + 1, :128], (8, 128))
                second = jnp.broadcast_to(table[head : head + 1, 128:], (8, 128))
                bias[head, rows, lanes] = jnp.where(
                    upper,
                    jnp.take_along_axis(second, low, axis=1, mode="promise_in_bounds"),
                    jnp.take_along_axis(first, low, axis=1, mode="promise_in_bounds"),
                )
        return unused

    lax.fori_loop(0, jnp.maximum(meta[0], meta[1]) * (BLOCK // 8), bias_rows, 0)

    def project(block, unused):
        second, first_row = place_of(meta, block)
        rows = rows_at(block)
        part = x[second, pl.ds(first_row, BLOCK), :]
        packed_x[rows, :] = part
        query = ((dot_nn(part, w_query[...]) + b_query[...]).astype(bf16).astype(f32) * scale).astype(bf16)
        key = dot_nn(part, w_key[...])
        value = dot_nn(part, w_value[...]) + b_value[...]
        key_t[:, rows] = key.T.astype(bf16)
        value_t[:, rows] = value.T.astype(bf16)
        key = key.astype(bf16)
        value = value.astype(bf16)
        for pair in range(pairs):
            lanes = slice(pair * 128, (pair + 1) * 128)
            query3[pair, rows, :] = query[:, lanes]
            key3[pair, rows, :] = key[:, lanes]
            value3[pair, rows, :] = value[:, lanes]
        return unused

    lax.fori_loop(0, meta[4], project, 0)

    def one_sequence(second, unused):
        offset = second * meta[0]
        length = meta[2 + second]

        def sized(blocks):
            count = blocks * BLOCK
            wide = min(count, 256)

            def one_head(head, unused):
                pair = head // 2
                lane = lax.broadcasted_iota(jnp.int32, (count, 128), 1)
                mine = (lane >= 64) == (head % 2 == 1)
                keys = jnp.where(mine, key3[pair, rows_at(offset, blocks), :], jnp.zeros((), bf16))
                values = value_t[pl.ds(pl.multiple_of(head * 64, 64), 64), rows_at(offset, blocks)]
                live = lax.broadcasted_iota(jnp.int32, (count, wide), 0) < length
                for column in range(count // wide):
                    lanes = slice(column * wide, (column + 1) * wide)
                    places = rows_at(offset + column * (wide // BLOCK), wide // BLOCK)
                    scores = dot_nt(keys, query3[pair, places, :]) + bias[head, :count, lanes]
                    scores = jnp.where(live, scores, masked_value)
                    top = jnp.max(scores, axis=0, keepdims=True)
                    powers = jnp.exp(scores - top)
                    total = jnp.sum(powers, axis=0, keepdims=True)
                    probs = (powers * (1.0 / total)).astype(bf16)
                    probs_t[head, rows_at(offset, blocks), lanes] = probs
                    attended_t[pl.ds(pl.multiple_of(head * 64, 64), 64), places] = dot_nn(values, probs)
                return unused

            lax.fori_loop(0, heads, one_head, 0)

        by_length(meta, second, sized)
        return unused

    lax.fori_loop(0, 2, one_sequence, 0)

    def turn(block, unused):
        attended[rows_at(block), :] = attended_t[:, rows_at(block)].T.astype(bf16)
        return unused

    lax.fori_loop(0, meta[4], turn, 0)
    zero_tail(meta, attended)
    zero_tail(meta, packed_x)
    made = piece_copies(meta, (piece0, piece1, piece2), attended, sems, True)
    start_copies(meta, made)
    wait_copies(meta, made)


def feed_forward(
    meta, x, own0, own1, own2, got0, got1, got2, w_out_own, w_out_got, b_out, gain, shift,
    w_up, b_up, w_down,
    normed1, inverse1, hidden_low, activated, slope, piece0, piece1, piece2,
    own, got, part, sems,
):
    own_copies = piece_copies(meta, (own0, own1, own2), own, sems.at[0], False)
    got_copies = piece_copies(meta, (got0, got1, got2), got, sems.at[1], False)
    start_copies(meta, own_copies)
    start_copies(meta, got_copies)
    wait_copies(meta, own_copies)
    wait_copies(meta, got_copies)
    width = w_up.shape[1]

    def one_block(block, unused):
        second, first_row = place_of(meta, block)
        rows = rows_at(block)
        head_own = dot_nn(own[rows, :], w_out_own[...]).astype(bf16).astype(f32)
        head_got = dot_nn(got[rows, :], w_out_got[...]).astype(bf16).astype(f32)
        branch = (head_own + head_got) + b_out[...]
        base = x[second, pl.ds(first_row, BLOCK), :].astype(f32) + branch
        normed, hidden, inverse = norm_forward(base, gain[...], shift[...])
        normed1[rows, :] = normed
        inverse1[rows, :] = jnp.broadcast_to(inverse, (BLOCK, 128))
        low = hidden.astype(bf16)
        hidden_low[rows, :] = low
        for column in range(width // 512):
            lanes = slice(column * 512, (column + 1) * 512)
            upper = dot_nn(low, w_up[:, lanes]) + b_up[:, lanes]
            normal = 0.5 * (1.0 + lax.erf(upper * inv_root_two))
            activated[rows, lanes] = (upper * normal).astype(bf16)
            slope[rows, lanes] = (
                normal + upper * inv_root_tau * jnp.exp(-0.5 * upper * upper)
            ).astype(bf16)
        part[rows, :] = dot_nn(activated[rows, :], w_down[...]).astype(bf16)
        return unused

    lax.fori_loop(0, meta[4], one_block, 0)
    zero_tail(meta, part)
    made = piece_copies(meta, (piece0, piece1, piece2), part, sems.at[0], True)
    start_copies(meta, made)
    zero_tail(meta, activated)
    zero_tail(meta, hidden_low)
    wait_copies(meta, made)


def second_norm(
    meta, cotangent, own0, own1, own2, got0, got1, got2, normed1, gain1, shift1, b_down, gain2, shift2,
    w_down, w_up, slope,
    layer_output, grad_y2, grad_ffn, grad_upper, sums, sums_up, piece0, piece1, piece2,
    own, got, part, sems,
):
    own_copies = piece_copies(meta, (own0, own1, own2), own, sems.at[0], False)
    got_copies = piece_copies(meta, (got0, got1, got2), got, sems.at[1], False)
    start_copies(meta, own_copies)
    start_copies(meta, got_copies)
    sums[...] = jnp.zeros(sums.shape, f32)
    sums_up[...] = jnp.zeros(sums_up.shape, f32)
    layer_output[...] = jnp.zeros(layer_output.shape, bf16)
    wait_copies(meta, own_copies)
    wait_copies(meta, got_copies)
    width = w_up.shape[1]

    def one_block(block, unused):
        second, first_row = place_of(meta, block)
        rows = rows_at(block)
        spot = pl.ds(first_row, BLOCK)
        live = live_rows(meta, second, first_row)
        ffn_out = (own[rows, :].astype(f32) + got[rows, :].astype(f32)) + b_down[...]
        hidden = normed1[rows, :] * gain1[...] + shift1[...]
        normed, result, inverse = norm_forward(hidden + ffn_out, gain2[...], shift2[...])
        layer_output[second, spot, :] = jnp.where(live, result, 0.0).astype(bf16)
        grad_result = jnp.where(live, cotangent[second, spot, :].astype(f32), 0.0)
        sums[0:1, :] += jnp.sum(grad_result * normed, axis=0, keepdims=True)
        sums[1:2, :] += jnp.sum(grad_result, axis=0, keepdims=True)
        grad = norm_back(grad_result, normed, inverse, gain2[...])
        grad_y2[rows, :] = grad
        low = grad.astype(bf16)
        grad_ffn[rows, :] = low
        sums[2:3, :] += jnp.sum(low.astype(f32), axis=0, keepdims=True)
        for column in range(width // 512):
            lanes = slice(column * 512, (column + 1) * 512)
            back = dot_nt(low, w_down[lanes, :]) * slope[rows, lanes].astype(f32)
            back = back.astype(bf16)
            grad_upper[rows, lanes] = back
            sums_up[:, lanes] += jnp.sum(back.astype(f32), axis=0, keepdims=True)
        part[rows, :] = dot_nt(grad_upper[rows, :], w_up[...]).astype(bf16)
        return unused

    lax.fori_loop(0, meta[4], one_block, 0)
    zero_tail(meta, part)
    made = piece_copies(meta, (piece0, piece1, piece2), part, sems.at[0], True)
    start_copies(meta, made)
    zero_tail(meta, grad_ffn)
    zero_tail(meta, grad_upper)
    wait_copies(meta, made)


def ffn_weights(meta, slots, activated, grad_ffn, hidden_low, grad_upper, chunks, stacked):
    width = grad_ffn.shape[1]
    units = activated.shape[1]

    def sized(count):
        def down(tile, unused):
            lanes = pl.ds(pl.multiple_of(tile * 256, 256), 256)
            stacked[lanes, :] = dot_tn(activated[:count, lanes], grad_ffn[:count, :])
            return unused

        lax.fori_loop(0, units // 256, down, 0)

        def up(tile, unused):
            lanes = pl.ds(pl.multiple_of(tile * 256, 256), 256)
            product = dot_tn(hidden_low[:count, lanes], grad_upper[:count, :])
            for half in range(units // width):
                spot = pl.ds(pl.multiple_of(units + half * width + tile * 256, 256), 256)
                stacked[spot, :] = product[:, half * width : (half + 1) * width]
            return unused

        lax.fori_loop(0, width // 256, up, 0)

    by_cap(meta, sized)
    scatter_chunks(slots, chunks, stacked)


def scatter_chunks(slots, chunks, stacked):
    rows = chunks.shape[1]

    def move(index, unused):
        chunks[slots[index]] = stacked[pl.ds(pl.multiple_of(index * rows, 8), rows), :].astype(bf16)
        return unused

    lax.fori_loop(0, chunks.shape[0], move, 0)


def attention_backward(
    meta, own0, own1, own2, got0, got1, got2, grad_y2, normed1, inverse1, gain1,
    w_out, w_query, w_key, w_value, query3, key3, value3, key_t, probs_t,
    grad_y1, grad_branch, grad_qkv, grad_scores_t, sums, sums_qv, piece0, piece1, piece2,
    own, got, part, grad_attended, grad_query_t, grad_key, grad_value, sems,
):
    own_copies = piece_copies(meta, (own0, own1, own2), own, sems.at[0], False)
    got_copies = piece_copies(meta, (got0, got1, got2), got, sems.at[1], False)
    start_copies(meta, own_copies)
    start_copies(meta, got_copies)
    sums[...] = jnp.zeros(sums.shape, f32)
    sums_qv[...] = jnp.zeros(sums_qv.shape, f32)
    wait_copies(meta, own_copies)
    wait_copies(meta, got_copies)
    heads = probs_t.shape[0]
    pairs = heads // 2
    local = heads * 64
    scale = 0.125

    def first_norm(block, unused):
        rows = rows_at(block)
        grad_hidden = (own[rows, :].astype(f32) + got[rows, :].astype(f32)) + grad_y2[rows, :]
        normed = normed1[rows, :]
        sums[0:1, :] += jnp.sum(grad_hidden * normed, axis=0, keepdims=True)
        sums[1:2, :] += jnp.sum(grad_hidden, axis=0, keepdims=True)
        grad = norm_back(grad_hidden, normed, inverse1[rows, 0:1], gain1[...])
        grad_y1[rows, :] = grad
        low = grad.astype(bf16)
        grad_branch[rows, :] = low
        sums[2:3, :] += jnp.sum(low.astype(f32), axis=0, keepdims=True)
        back = dot_nt(low, w_out[...]).astype(bf16)
        for pair in range(pairs):
            grad_attended[pair, rows, :] = back[:, pair * 128 : (pair + 1) * 128]
            grad_key[pair, rows, :] = jnp.zeros((BLOCK, 128), f32)
            grad_value[pair, rows, :] = jnp.zeros((BLOCK, 128), f32)
        return unused

    lax.fori_loop(0, meta[4], first_norm, 0)

    def one_sequence(second, unused):
        offset = second * meta[0]

        def sized(blocks):
            count = blocks * BLOCK
            wide = min(count, 256)
            every = rows_at(offset, blocks)

            def one_head(head, unused):
                pair = head // 2
                lane = lax.broadcasted_iota(jnp.int32, (wide, 128), 1)
                mine = (lane >= 64) == (head % 2 == 1)
                head_rows = pl.ds(pl.multiple_of(head * 64, 64), 64)
                values = value3[pair, every, :]
                keys = key_t[head_rows, every]
                for column in range(count // wide):
                    lanes = slice(column * wide, (column + 1) * wide)
                    places = rows_at(offset + column * (wide // BLOCK), wide // BLOCK)
                    zero = jnp.zeros((), bf16)
                    back = jnp.where(mine, grad_attended[pair, places, :], zero)
                    queries = jnp.where(mine, query3[pair, places, :], zero)
                    grad_probs = dot_nt(values, back)
                    probs_low = probs_t[head, every, lanes]
                    probs = probs_low.astype(f32)
                    mean = jnp.sum(probs * grad_probs, axis=0, keepdims=True)
                    grad_scores = (probs * (grad_probs - mean)).astype(bf16)
                    grad_scores_t[head, every, lanes] = grad_scores
                    grad_value[pair, every, :] += dot_nn(probs_low, back)
                    grad_key[pair, every, :] += dot_nn(grad_scores, queries)
                    grad_query_t[head_rows, places] = dot_nn(keys, grad_scores)
                return unused

            lax.fori_loop(0, heads, one_head, 0)

        by_length(meta, second, sized)
        return unused

    lax.fori_loop(0, 2, one_sequence, 0)

    def gather_grads(block, unused):
        rows = rows_at(block)
        query = (grad_query_t[:, rows].T * scale).astype(bf16)
        grad_qkv[rows, :local] = query
        for pair in range(pairs):
            lanes = slice(pair * 128, (pair + 1) * 128)
            grad_qkv[rows, local + pair * 128 : local + (pair + 1) * 128] = grad_key[pair, rows, :].astype(bf16)
            value = grad_value[pair, rows, :].astype(bf16)
            grad_qkv[rows, 2 * local + pair * 128 : 2 * local + (pair + 1) * 128] = value
            sums_qv[1:2, lanes] += jnp.sum(value.astype(f32), axis=0, keepdims=True)
        sums_qv[0:1, :] += jnp.sum(query.astype(f32), axis=0, keepdims=True)
        total = dot_nt(query, w_query[...])
        total = total + dot_nt(grad_qkv[rows, local : 2 * local], w_key[...])
        total = total + dot_nt(grad_qkv[rows, 2 * local :], w_value[...])
        part[rows, :] = total.astype(bf16)
        return unused

    lax.fori_loop(0, meta[4], gather_grads, 0)
    zero_tail(meta, part)
    made = piece_copies(meta, (piece0, piece1, piece2), part, sems.at[0], True)
    start_copies(meta, made)
    zero_tail(meta, grad_qkv)
    zero_tail(meta, grad_branch)
    wait_copies(meta, made)


def attention_weights(meta, slots, packed_x, grad_qkv, own0, own1, own2, grad_branch, chunks, stacked, attended, sems):
    copies = piece_copies(meta, (own0, own1, own2), attended, sems, False)
    start_copies(meta, copies)
    width = packed_x.shape[1]
    local = attended.shape[1]
    wait_copies(meta, copies)

    def sized(count):
        def project(tile, unused):
            lanes = pl.ds(pl.multiple_of(tile * 256, 256), 256)
            product = dot_tn(packed_x[:count, lanes], grad_qkv[:count, :])
            for part in range(3):
                spot = pl.ds(pl.multiple_of(part * width + tile * 256, 256), 256)
                stacked[spot, :] = product[:, part * local : (part + 1) * local]
            return unused

        lax.fori_loop(0, width // 256, project, 0)
        product = dot_tn(attended[:count, :], grad_branch[:count, :])
        for half in range(width // local):
            first = 3 * width + half * local
            stacked[first : first + local, :] = product[:, half * local : (half + 1) * local]

    by_cap(meta, sized)
    scatter_chunks(slots, chunks, stacked)


def table_histogram(meta, grad_scores_t, buckets, total, left, right):
    heads = grad_scores_t.shape[0]
    seq_len = buckets.shape[1]
    group = 16
    total[...] = jnp.zeros(total.shape, f32)

    def one_sequence(second, unused):
        offset = second * meta[0]

        def sized(blocks):
            count = blocks * BLOCK
            digit = lax.broadcasted_iota(jnp.int32, (16, count), 0)

            def one_group(index, unused):
                rows = pl.ds(pl.multiple_of(index * group, group), group)
                spots = pl.ds(pl.multiple_of(offset * BLOCK + index * group, group), group)
                bucket = buckets[rows, :count]
                upper = bucket >> 4
                lower = bucket & 15
                grads = [grad_scores_t[head, spots, :count].astype(f32) for head in range(heads)]
                for row in range(group):
                    lanes = slice(row * count, (row + 1) * count)
                    left[:, lanes] = jnp.where(digit == upper[row : row + 1, :], 1.0, 0.0).astype(bf16)
                    chosen = digit == lower[row : row + 1, :]
                    for head in range(heads):
                        spread = jnp.where(chosen, grads[head][row : row + 1, :], 0.0)
                        right[head * 16 : (head + 1) * 16, lanes] = spread.astype(bf16)
                total[...] += dot_nt(right[:, : group * count], left[:, : group * count])
                return unused

            lax.fori_loop(0, count // group, one_group, 0)

        by_length(meta, second, sized)
        return unused

    lax.fori_loop(0, 2, one_sequence, 0)


def input_gradient(meta, grad_y1, own0, own1, own2, got0, got1, got2, out, own, got, sems):
    own_copies = piece_copies(meta, (own0, own1, own2), own, sems.at[0], False)
    got_copies = piece_copies(meta, (got0, got1, got2), got, sems.at[1], False)
    start_copies(meta, own_copies)
    start_copies(meta, got_copies)
    out[...] = jnp.zeros(out.shape, f32)
    wait_copies(meta, own_copies)
    wait_copies(meta, got_copies)

    def one_block(block, unused):
        second, first_row = place_of(meta, block)
        rows = rows_at(block)
        live = live_rows(meta, second, first_row)
        total = (own[rows, :].astype(f32) + got[rows, :].astype(f32)) + grad_y1[rows, :]
        out[second, pl.ds(first_row, BLOCK), :] = jnp.where(live, total, 0.0)
        return unused

    lax.fori_loop(0, meta[4], one_block, 0)


def unpack_ffn(places, *refs):
    chunks, (grad_up, grad_down) = refs[:-2], refs[-2:]
    rows = chunks[0].shape[0]
    units, width = grad_down.shape
    for index, chunk in enumerate(chunks):
        first = places[index] * rows
        values = chunk[...].astype(f32)

        @pl.when(first < units)
        def _():
            grad_down[pl.ds(pl.multiple_of(first, 8), rows), :] = values

        for half in range(units // width):
            low = units + half * width

            @pl.when((first >= low) & (first < low + width))
            def _():
                spot = pl.ds(pl.multiple_of(first - low, 8), rows)
                grad_up[spot, half * width : (half + 1) * width] = values


def unpack_attention(places, *refs):
    chunks, (grad_query, grad_key, grad_value, grad_out) = refs[:-4], refs[-4:]
    rows = chunks[0].shape[0]
    width, local = grad_query.shape
    for index, chunk in enumerate(chunks):
        first = places[index] * rows
        values = chunk[...].astype(f32)
        for part, target in enumerate((grad_query, grad_key, grad_value)):
            low = part * width

            @pl.when((first >= low) & (first < low + width))
            def _():
                target[pl.ds(pl.multiple_of(first - low, 8), rows), :] = values

        for half in range(width // local):
            low = 3 * width + half * local

            @pl.when((first >= low) & (first < low + local))
            def _():
                spot = pl.ds(pl.multiple_of(first - low, 8), rows)
                grad_out[spot, half * local : (half + 1) * local] = values


def run(kernel, specs, outs, scratch, name, room):
    params = pltpu.CompilerParams(vmem_limit_bytes=room * 1024 * 1024)

    def call(*args):
        return pl.pallas_call(
            kernel,
            in_specs=[{"s": in_smem, "v": in_vmem, "a": in_any}[kind] for kind in specs],
            out_specs=[in_any if kind == "a" else in_vmem for kind, unused in outs],
            out_shape=[shape for unused, shape in outs],
            scratch_shapes=scratch,
            compiler_params=params,
            name=name,
        )(*args)

    return call


def swap_tensor(value):
    return lax.ppermute(value, "tensor", ((0, 1), (1, 0)))


def exchange(pieces, level):
    got0 = swap_tensor(pieces[0])
    got1, got2 = lax.switch(
        level,
        (
            lambda one, two: (one, two),
            lambda one, two: (swap_tensor(one), two),
            lambda one, two: (swap_tensor(one), swap_tensor(two)),
        ),
        pieces[1],
        pieces[2],
    )
    return got0, got1, got2


def ring_pairs(dp_count):
    chips = dp_count // 2
    order = list(range(0, chips, 2)) + list(range(chips - 1, 0, -2))
    pairs = []
    for place, chip in enumerate(order):
        after = order[(place + 1) % chips]
        pairs.append((2 * chip, 2 * after))
        pairs.append((2 * after + 1, 2 * chip + 1))
    return tuple(pairs)


def ring_places(dp_count):
    chips = dp_count // 2
    index = lax.axis_index("dp")
    chip, core = index // 2, index % 2
    forward = jnp.where(chip % 2 == 0, chip // 2, chips - 1 - chip // 2)
    own = jnp.where(core == 0, forward, (chips - forward) % chips)
    other = jnp.where(core == 0, (chips - forward) % chips, forward)
    steps = jnp.arange(chips, dtype=jnp.int32)
    own_slots = (own - steps) % chips
    other_slots = chips + (other - steps) % chips
    slots = jnp.where(core == 0, jnp.concatenate([own_slots, other_slots]), jnp.concatenate([other_slots, own_slots]))
    own_chunks = core * chips + (own - steps) % chips
    other_chunks = (1 - core) * chips + (other - steps) % chips
    return slots.astype(jnp.int32), jnp.concatenate([own_chunks, other_chunks]).astype(jnp.int32)


def reduce_chunks(chunks, dp_count):
    chips = dp_count // 2
    siblings = tuple((i, i ^ 1) for i in range(dp_count))
    pairs = ring_pairs(dp_count)
    got = lax.ppermute(chunks[chips:], "dp", siblings)

    def local(step):
        return chunks[step].astype(f32) + got[step].astype(f32)

    moving = local(0).astype(bf16)
    for step in range(1, chips):
        moving = (lax.ppermute(moving, "dp", pairs).astype(f32) + local(step)).astype(bf16)
    own = [None] * chips
    own[chips - 1] = moving
    for step in range(chips - 1):
        moving = lax.ppermute(moving, "dp", pairs)
        own[step] = moving
    other = [lax.ppermute(piece, "dp", siblings) for piece in own]
    return own + other


def sum_small(value, dp_count):
    bit = 1
    while bit < dp_count:
        value = value + lax.ppermute(value, "dp", tuple((i, i ^ bit) for i in range(dp_count)))
        bit *= 2
    return value


def per_device(dp_count, *arrays):
    (
        inputs, lengths, buckets, w_query, b_query, w_key, w_value, b_value, w_out, b_out, norm1_gain, norm1_shift,
        w_up, b_up, w_down, b_down, norm2_gain, norm2_shift, position_table, cotangent,
    ) = arrays
    micro, seqs, seq_len, width = inputs.shape
    bucket_count, heads = position_table.shape
    local = w_query.shape[1]
    units = w_up.shape[1]
    chips = dp_count // 2
    rows = micro * seq_len
    x = inputs.reshape(micro, seq_len, width)
    grad_out = cotangent.reshape(micro, seq_len, width)
    sizes = lengths[:, 0]
    blocks = jnp.where(sizes <= BLOCK, 1, jnp.where(sizes <= 2 * BLOCK, 2, 4))
    used = blocks[0] + blocks[1]
    level = (used > CAPS[0]).astype(jnp.int32) + (used > CAPS[1]).astype(jnp.int32)
    cap = jnp.where(level == 0, CAPS[0], jnp.where(level == 1, CAPS[1], CAPS[2]))
    meta = jnp.stack([blocks[0], blocks[1], sizes[0], sizes[1], used, cap, cap, cap]).astype(jnp.int32)
    slots, places = ring_places(dp_count)
    buckets_t = buckets.T
    table = position_table.T
    row = lambda vector: vector.reshape(1, -1)
    piece_rows = (CAPS[0] * BLOCK, (CAPS[1] - CAPS[0]) * BLOCK, rows - CAPS[1] * BLOCK)
    pieces = lambda columns: [("a", shape_of((count, columns), bf16)) for count in piece_rows]
    vmem = pltpu.VMEM
    dma = pltpu.SemaphoreType.DMA

    w_out_got = swap_tensor(w_out)
    packed_x, query3, key3, value3, key_t, probs_t, *attended = run(
        attention_forward,
        "svvvvvvvv",
        [
            ("v", shape_of((rows, width), bf16)),
            ("v", shape_of((heads // 2, rows, 128), bf16)),
            ("v", shape_of((heads // 2, rows, 128), bf16)),
            ("v", shape_of((heads // 2, rows, 128), bf16)),
            ("v", shape_of((local, rows), bf16)),
            ("v", shape_of((heads, rows, seq_len), bf16)),
            *pieces(local),
        ],
        [
            vmem((heads, seq_len, seq_len), f32),
            vmem((local, rows), bf16),
            vmem((local, rows), f32),
            vmem((rows, local), bf16),
            dma((3,)),
        ],
        "attention_forward",
        16,
    )(meta, x, w_query, row(b_query), w_key, w_value, row(b_value), buckets_t, table)
    attended_got = exchange(attended, level)

    normed1, inverse1, hidden_low, activated, slope, *unit_part = run(
        feed_forward,
        "svaaaaaavvvvvvvv",
        [
            ("v", shape_of((rows, width), f32)),
            ("v", shape_of((rows, 128), f32)),
            ("v", shape_of((rows, width), bf16)),
            ("v", shape_of((rows, units), bf16)),
            ("v", shape_of((rows, units), bf16)),
            *pieces(width),
        ],
        [vmem((rows, local), bf16), vmem((rows, local), bf16), vmem((rows, width), bf16), dma((2, 3))],
        "feed_forward",
        8,
    )(
        meta, x, *attended, *attended_got, w_out, w_out_got, row(b_out), row(norm1_gain), row(norm1_shift),
        w_up, row(b_up), w_down,
    )
    unit_got = exchange(unit_part, level)

    layer_output, grad_y2, grad_ffn, grad_upper, sums2, sums_up, *hidden_part = run(
        second_norm,
        "svaaaaaavvvvvvvvv",
        [
            ("v", shape_of((micro, seq_len, width), bf16)),
            ("v", shape_of((rows, width), f32)),
            ("v", shape_of((rows, width), bf16)),
            ("v", shape_of((rows, units), bf16)),
            ("v", shape_of((8, width), f32)),
            ("v", shape_of((1, units), f32)),
            *pieces(width),
        ],
        [vmem((rows, width), bf16), vmem((rows, width), bf16), vmem((rows, width), bf16), dma((2, 3))],
        "second_norm",
        12,
    )(
        meta, grad_out, *unit_part, *unit_got, normed1, row(norm1_gain), row(norm1_shift), row(b_down),
        row(norm2_gain), row(norm2_shift), w_down, w_up, slope,
    )
    hidden_got = exchange(hidden_part, level)

    stacked_ffn = 2 * units
    (ffn_chunks,) = run(
        ffn_weights,
        "ssvvvv",
        [("v", shape_of((2 * chips, stacked_ffn // (2 * chips), width), bf16))],
        [vmem((stacked_ffn, width), f32)],
        "ffn_weights",
        14,
    )(meta, slots, activated, grad_ffn, hidden_low, grad_upper)

    grad_y1, grad_branch, grad_qkv, grad_scores_t, sums1, sums_qv, *input_part = run(
        attention_backward,
        "saaaaaavvvvvvvvvvvvv",
        [
            ("v", shape_of((rows, width), f32)),
            ("v", shape_of((rows, width), bf16)),
            ("v", shape_of((rows, 3 * local), bf16)),
            ("v", shape_of((heads, rows, seq_len), bf16)),
            ("v", shape_of((8, width), f32)),
            ("v", shape_of((8, local), f32)),
            *pieces(width),
        ],
        [
            vmem((rows, width), bf16),
            vmem((rows, width), bf16),
            vmem((rows, width), bf16),
            vmem((heads // 2, rows, 128), bf16),
            vmem((local, rows), f32),
            vmem((heads // 2, rows, 128), f32),
            vmem((heads // 2, rows, 128), f32),
            dma((2, 3)),
        ],
        "attention_backward",
        26,
    )(
        meta, *hidden_part, *hidden_got, grad_y2, normed1, inverse1, row(norm1_gain), w_out, w_query, w_key, w_value,
        query3, key3, value3, key_t, probs_t,
    )
    input_got = exchange(input_part, level)

    stacked_attention = 3 * width + width * local // local
    (attention_chunks,) = run(
        attention_weights,
        "ssvvaaav",
        [("v", shape_of((2 * chips, stacked_attention // (2 * chips), local), bf16))],
        [vmem((stacked_attention, local), f32), vmem((rows, local), bf16), dma((3,))],
        "attention_weights",
        9,
    )(meta, slots, packed_x, grad_qkv, *attended, grad_branch)

    (table_sums,) = run(
        table_histogram,
        "svv",
        [("v", shape_of((16 * heads, 16), f32))],
        [vmem((16, 16 * seq_len), bf16), vmem((16 * heads, 16 * seq_len), bf16)],
        "table_histogram",
        10,
    )(meta, grad_scores_t, buckets_t)

    ffn_pieces = reduce_chunks(ffn_chunks, dp_count)
    attention_pieces = reduce_chunks(attention_chunks, dp_count)
    grad_w_up, grad_w_down = run(
        unpack_ffn,
        "s" + "v" * len(ffn_pieces),
        [("v", shape_of((width, units), f32)), ("v", shape_of((units, width), f32))],
        [],
        "unpack_ffn",
        18,
    )(places, *ffn_pieces)
    grad_w_query, grad_w_key, grad_w_value, grad_w_out = run(
        unpack_attention,
        "s" + "v" * len(attention_pieces),
        [("v", shape_of((width, local), f32))] * 3 + [("v", shape_of((local, width), f32))],
        [],
        "unpack_attention",
        10,
    )(places, *attention_pieces)

    (grad_inputs,) = run(
        input_gradient,
        "svaaaaaa",
        [("v", shape_of((micro, seq_len, width), f32))],
        [vmem((rows, width), bf16), vmem((rows, width), bf16), dma((2, 3))],
        "input_gradient",
        12,
    )(meta, grad_y1, *input_part, *input_got)

    table_part = table_sums.reshape(heads, 16, 16).transpose(2, 1, 0).reshape(bucket_count, heads)
    small = jnp.concatenate(
        [
            sums2[0], sums2[1], sums2[2], sums_up[0], sums1[0], sums1[1], sums1[2], sums_qv[0], sums_qv[1],
            table_part.reshape(-1),
        ]
    ).reshape(-1, 128)
    small = sum_small(small, dp_count).reshape(-1)
    cuts = []
    start = 0
    for count in (width, width, width, units, width, width, width, local, local, bucket_count * heads):
        cuts.append(small[start : start + count])
        start += count
    grad_gain2, grad_shift2, grad_b_down, grad_b_up, grad_gain1, grad_shift1, grad_b_out, grad_b_query, grad_b_value, table_grad = cuts
    return (
        layer_output.reshape(inputs.shape),
        grad_inputs.reshape(inputs.shape),
        grad_w_query,
        grad_b_query,
        grad_w_key,
        grad_w_value,
        grad_b_value,
        grad_w_out,
        grad_b_out,
        grad_gain1,
        grad_shift1,
        grad_w_up,
        grad_b_up,
        grad_w_down,
        grad_b_down,
        grad_gain2,
        grad_shift2,
        table_grad.reshape(bucket_count, heads),
    )


def solution(mesh):
    placed = (
        P(None, "dp", None, None),
        P(None, "dp"),
        P(),
        P(None, "tensor"),
        P("tensor"),
        P(None, "tensor"),
        P(None, "tensor"),
        P("tensor"),
        P("tensor", None),
        P(),
        P(),
        P(),
        P(None, "tensor"),
        P("tensor"),
        P("tensor", None),
        P(),
        P(),
        P(),
        P(None, "tensor"),
        P(None, "dp", None, None),
    )
    dp_count = mesh.shape["dp"]
    return jax.shard_map(
        lambda *arrays: per_device(dp_count, *arrays),
        mesh=mesh,
        in_specs=placed,
        out_specs=(
            P(None, "dp", None, None),
            P(None, "dp", None, None),
            P(None, "tensor"),
            P("tensor"),
            P(None, "tensor"),
            P(None, "tensor"),
            P("tensor"),
            P("tensor", None),
            P(),
            P(),
            P(),
            P(None, "tensor"),
            P("tensor"),
            P("tensor", None),
            P(),
            P(),
            P(),
            P(None, "tensor"),
        ),
        check_vma=False,
    )
```

```python
import functools

import jax
import jax.numpy as jnp
from jax import lax
from jax.experimental import pallas as pl
from jax.experimental.pallas import tpu as pltpu
from jax.sharding import PartitionSpec as P

epsilon = 1e-05
masked_value = -1e30
inv_root_two = 0.7071067811865476
inv_root_tau = 0.3989422804014327

BLOCK = 128
CAPS = (2, 5, 8)
TABLE_PARTS = 3
bf16 = jnp.bfloat16
f32 = jnp.float32
shape_of = jax.ShapeDtypeStruct

in_vmem = pl.BlockSpec(memory_space=pltpu.VMEM)
in_smem = pl.BlockSpec(memory_space=pltpu.SMEM)
in_any = pl.BlockSpec(memory_space=pl.ANY)


def rows_at(block, count=1):
    return pl.ds(pl.multiple_of(block * BLOCK, BLOCK), count * BLOCK)


def dot_nn(left, right):
    return lax.dot_general(left, right, (((1,), (0,)), ((), ())), preferred_element_type=f32)


def dot_nt(left, right):
    return lax.dot_general(left, right, (((1,), (1,)), ((), ())), preferred_element_type=f32)


def dot_tn(left, right):
    return lax.dot_general(left, right, (((0,), (0,)), ((), ())), preferred_element_type=f32)


def place_of(meta, block):
    second = (block >= meta[0]).astype(jnp.int32)
    return second, pl.multiple_of((block - second * meta[0]) * BLOCK, BLOCK)


def live_rows(meta, second, first_row):
    rows = lax.broadcasted_iota(jnp.int32, (BLOCK, 1), 0) + first_row
    return rows < meta[2 + second]


def zero_tail(meta, ref):
    def clear(block, unused):
        ref[rows_at(block), :] = jnp.zeros((BLOCK, ref.shape[1]), ref.dtype)
        return unused

    lax.fori_loop(meta[4], meta[5], clear, 0)


def piece_copies(meta, pieces, whole, sems, to_pieces):
    start = 0
    made = []
    for index, piece in enumerate(pieces):
        rows = piece.shape[0]
        part = whole.at[pl.ds(start, rows), :]
        pair = (part, piece) if to_pieces else (piece, part)
        made.append((start // BLOCK, pltpu.make_async_copy(pair[0], pair[1], sems.at[index])))
        start += rows
    return made


def start_copies(meta, made):
    for first, copy in made:
        @pl.when(meta[5] > first)
        def _():
            copy.start()


def wait_copies(meta, made):
    for first, copy in made:
        @pl.when(meta[5] > first)
        def _():
            copy.wait()


def by_length(meta, second, body):
    for blocks in (1, 2, 4):
        @pl.when(meta[second] == blocks)
        def _():
            body(blocks)


def by_cap(meta, body):
    for blocks in CAPS:
        @pl.when(meta[5] == blocks)
        def _():
            body(blocks * BLOCK)


def norm_forward(rows, gain, shift):
    centre = rows - jnp.mean(rows, axis=-1, keepdims=True)
    inverse = lax.rsqrt(jnp.mean(centre * centre, axis=-1, keepdims=True) + epsilon)
    normed = centre * inverse
    return normed, normed * gain + shift, inverse


def norm_back(grad_rows, normed, inverse, gain):
    scaled = grad_rows * gain
    first_mean = jnp.mean(scaled, axis=-1, keepdims=True)
    second_mean = jnp.mean(scaled * normed, axis=-1, keepdims=True)
    return inverse * (scaled - first_mean - normed * second_mean)


def attention_forward(
    meta, x, w_query, b_query, w_key, w_value, b_value, buckets, table,
    packed_x, query3, key3, value3, key_t, probs_t, piece0, piece1, piece2,
    bias, value_t, attended_t, attended, sems,
):
    heads = probs_t.shape[0]
    pairs = heads // 2
    scale = 0.125
    seq_len = x.shape[1]
    columns = seq_len // BLOCK

    def bias_rows(group, unused):
        rows = pl.ds(pl.multiple_of(group * 8, 8), 8)
        for column in range(columns):
            lanes = slice(column * BLOCK, (column + 1) * BLOCK)
            bucket = buckets[rows, lanes]
            low = bucket & 127
            upper = bucket >= 128
            for head in range(heads):
                first = jnp.broadcast_to(table[head : head + 1, :128], (8, 128))
                second = jnp.broadcast_to(table[head : head + 1, 128:], (8, 128))
                bias[head, rows, lanes] = jnp.where(
                    upper,
                    jnp.take_along_axis(second, low, axis=1, mode="promise_in_bounds"),
                    jnp.take_along_axis(first, low, axis=1, mode="promise_in_bounds"),
                )
        return unused

    lax.fori_loop(0, jnp.maximum(meta[0], meta[1]) * (BLOCK // 8), bias_rows, 0)

    def project(block, unused):
        second, first_row = place_of(meta, block)
        rows = rows_at(block)
        part = x[second, pl.ds(first_row, BLOCK), :]
        packed_x[rows, :] = part
        query = ((dot_nn(part, w_query[...]) + b_query[...]).astype(bf16).astype(f32) * scale).astype(bf16)
        key = dot_nn(part, w_key[...])
        value = dot_nn(part, w_value[...]) + b_value[...]
        key_t[:, rows] = key.T.astype(bf16)
        value_t[:, rows] = value.T.astype(bf16)
        key = key.astype(bf16)
        value = value.astype(bf16)
        for pair in range(pairs):
            lanes = slice(pair * 128, (pair + 1) * 128)
            query3[pair, rows, :] = query[:, lanes]
            key3[pair, rows, :] = key[:, lanes]
            value3[pair, rows, :] = value[:, lanes]
        return unused

    lax.fori_loop(0, meta[4], project, 0)

    def one_sequence(second, unused):
        offset = second * meta[0]
        length = meta[2 + second]

        def sized(blocks):
            count = blocks * BLOCK
            wide = min(count, 256)

            def one_head(head, unused):
                pair = head // 2
                lane = lax.broadcasted_iota(jnp.int32, (count, 128), 1)
                mine = (lane >= 64) == (head % 2 == 1)
                keys = jnp.where(mine, key3[pair, rows_at(offset, blocks), :], jnp.zeros((), bf16))
                values = value_t[pl.ds(pl.multiple_of(head * 64, 64), 64), rows_at(offset, blocks)]
                live = lax.broadcasted_iota(jnp.int32, (count, wide), 0) < length
                for column in range(count // wide):
                    lanes = slice(column * wide, (column + 1) * wide)
                    places = rows_at(offset + column * (wide // BLOCK), wide // BLOCK)
                    scores = dot_nt(keys, query3[pair, places, :]) + bias[head, :count, lanes]
                    scores = jnp.where(live, scores, masked_value)
                    top = jnp.max(scores, axis=0, keepdims=True)
                    powers = jnp.exp(scores - top)
                    total = jnp.sum(powers, axis=0, keepdims=True)
                    probs = (powers * (1.0 / total)).astype(bf16)
                    probs_t[head, rows_at(offset, blocks), lanes] = probs
                    attended_t[pl.ds(pl.multiple_of(head * 64, 64), 64), places] = dot_nn(values, probs)
                return unused

            lax.fori_loop(0, heads, one_head, 0)

        by_length(meta, second, sized)
        return unused

    lax.fori_loop(0, 2, one_sequence, 0)

    def turn(block, unused):
        attended[rows_at(block), :] = attended_t[:, rows_at(block)].T.astype(bf16)
        return unused

    lax.fori_loop(0, meta[4], turn, 0)
    zero_tail(meta, attended)
    zero_tail(meta, packed_x)
    made = piece_copies(meta, (piece0, piece1, piece2), attended, sems, True)
    start_copies(meta, made)
    wait_copies(meta, made)


def feed_forward(
    meta, x, own0, own1, own2, got0, got1, got2, w_out_own, w_out_got, b_out, gain, shift,
    w_up, b_up, w_down,
    normed1, inverse1, hidden_low, activated, slope, piece0, piece1, piece2,
    own, got, part, sems,
):
    own_copies = piece_copies(meta, (own0, own1, own2), own, sems.at[0], False)
    got_copies = piece_copies(meta, (got0, got1, got2), got, sems.at[1], False)
    start_copies(meta, own_copies)
    start_copies(meta, got_copies)
    wait_copies(meta, own_copies)
    wait_copies(meta, got_copies)
    width = w_up.shape[1]

    def one_block(block, unused):
        second, first_row = place_of(meta, block)
        rows = rows_at(block)
        head_own = dot_nn(own[rows, :], w_out_own[...]).astype(bf16).astype(f32)
        head_got = dot_nn(got[rows, :], w_out_got[...]).astype(bf16).astype(f32)
        branch = (head_own + head_got) + b_out[...]
        base = x[second, pl.ds(first_row, BLOCK), :].astype(f32) + branch
        normed, hidden, inverse = norm_forward(base, gain[...], shift[...])
        normed1[rows, :] = normed
        inverse1[rows, :] = jnp.broadcast_to(inverse, (BLOCK, 128))
        low = hidden.astype(bf16)
        hidden_low[rows, :] = low
        for column in range(width // 512):
            lanes = slice(column * 512, (column + 1) * 512)
            upper = dot_nn(low, w_up[:, lanes]) + b_up[:, lanes]
            normal = 0.5 * (1.0 + lax.erf(upper * inv_root_two))
            activated[rows, lanes] = (upper * normal).astype(bf16)
            slope[rows, lanes] = (
                normal + upper * inv_root_tau * jnp.exp(-0.5 * upper * upper)
            ).astype(bf16)
        part[rows, :] = dot_nn(activated[rows, :], w_down[...]).astype(bf16)
        return unused

    lax.fori_loop(0, meta[4], one_block, 0)
    zero_tail(meta, part)
    made = piece_copies(meta, (piece0, piece1, piece2), part, sems.at[0], True)
    start_copies(meta, made)
    zero_tail(meta, activated)
    zero_tail(meta, hidden_low)
    wait_copies(meta, made)


def second_norm(
    meta, cotangent, own0, own1, own2, got0, got1, got2, normed1, gain1, shift1, b_down, gain2, shift2,
    w_down, w_up, slope,
    layer_output, grad_y2, grad_ffn, grad_upper, sums, sums_up, piece0, piece1, piece2,
    own, got, part, sems,
):
    own_copies = piece_copies(meta, (own0, own1, own2), own, sems.at[0], False)
    got_copies = piece_copies(meta, (got0, got1, got2), got, sems.at[1], False)
    start_copies(meta, own_copies)
    start_copies(meta, got_copies)
    sums[...] = jnp.zeros(sums.shape, f32)
    sums_up[...] = jnp.zeros(sums_up.shape, f32)
    layer_output[...] = jnp.zeros(layer_output.shape, bf16)
    wait_copies(meta, own_copies)
    wait_copies(meta, got_copies)
    width = w_up.shape[1]

    def one_block(block, unused):
        second, first_row = place_of(meta, block)
        rows = rows_at(block)
        spot = pl.ds(first_row, BLOCK)
        live = live_rows(meta, second, first_row)
        ffn_out = (own[rows, :].astype(f32) + got[rows, :].astype(f32)) + b_down[...]
        hidden = normed1[rows, :] * gain1[...] + shift1[...]
        normed, result, inverse = norm_forward(hidden + ffn_out, gain2[...], shift2[...])
        layer_output[second, spot, :] = jnp.where(live, result, 0.0).astype(bf16)
        grad_result = jnp.where(live, cotangent[second, spot, :].astype(f32), 0.0)
        sums[0:1, :] += jnp.sum(grad_result * normed, axis=0, keepdims=True)
        sums[1:2, :] += jnp.sum(grad_result, axis=0, keepdims=True)
        grad = norm_back(grad_result, normed, inverse, gain2[...])
        grad_y2[rows, :] = grad
        low = grad.astype(bf16)
        grad_ffn[rows, :] = low
        sums[2:3, :] += jnp.sum(low.astype(f32), axis=0, keepdims=True)
        for column in range(width // 512):
            lanes = slice(column * 512, (column + 1) * 512)
            back = dot_nt(low, w_down[lanes, :]) * slope[rows, lanes].astype(f32)
            back = back.astype(bf16)
            grad_upper[rows, lanes] = back
            sums_up[:, lanes] += jnp.sum(back.astype(f32), axis=0, keepdims=True)
        part[rows, :] = dot_nt(grad_upper[rows, :], w_up[...]).astype(bf16)
        return unused

    lax.fori_loop(0, meta[4], one_block, 0)
    zero_tail(meta, part)
    made = piece_copies(meta, (piece0, piece1, piece2), part, sems.at[0], True)
    start_copies(meta, made)
    zero_tail(meta, grad_ffn)
    zero_tail(meta, grad_upper)
    wait_copies(meta, made)


def ffn_weights(meta, slots, activated, grad_ffn, hidden_low, grad_upper, keep, give, stacked):
    width = grad_ffn.shape[1]
    units = activated.shape[1]

    def sized(count):
        def down(tile, unused):
            lanes = pl.ds(pl.multiple_of(tile * 256, 256), 256)
            stacked[lanes, :] = dot_tn(activated[:count, lanes], grad_ffn[:count, :])
            return unused

        lax.fori_loop(0, units // 256, down, 0)

        def up(tile, unused):
            lanes = pl.ds(pl.multiple_of(tile * 256, 256), 256)
            product = dot_tn(hidden_low[:count, lanes], grad_upper[:count, :])
            for half in range(units // width):
                spot = pl.ds(pl.multiple_of(units + half * width + tile * 256, 256), 256)
                stacked[spot, :] = product[:, half * width : (half + 1) * width]
            return unused

        lax.fori_loop(0, width // 256, up, 0)

    by_cap(meta, sized)
    scatter_chunks(slots, keep, give, stacked)


def scatter_chunks(slots, keep, give, stacked):
    chips, rows, unused = keep.shape

    def move(index, unused):
        for first, target in ((0, keep), (chips, give)):
            spot = pl.ds(pl.multiple_of(slots[first + index] * rows, 8), rows)
            target[index] = stacked[spot, :].astype(bf16)
        return unused

    lax.fori_loop(0, chips, move, 0)


def add_halves(keep, got, *outs):
    count = outs[0].shape[0]
    for index in range(keep.shape[0]):
        total = keep[index].astype(f32) + got[index].astype(f32)
        outs[index // count][index % count] = total.astype(bf16)


def attention_backward(
    meta, own0, own1, own2, got0, got1, got2, grad_y2, normed1, inverse1, gain1,
    w_out, w_query, w_key, w_value, query3, key3, value3, key_t, probs_t,
    grad_y1, grad_branch, grad_qkv, grad_scores_t, sums, sums_qv, part,
    own, got, grad_attended, grad_query_t, grad_key, grad_value, sems,
):
    own_copies = piece_copies(meta, (own0, own1, own2), own, sems.at[0], False)
    got_copies = piece_copies(meta, (got0, got1, got2), got, sems.at[1], False)
    start_copies(meta, own_copies)
    start_copies(meta, got_copies)
    sums[...] = jnp.zeros(sums.shape, f32)
    sums_qv[...] = jnp.zeros(sums_qv.shape, f32)
    wait_copies(meta, own_copies)
    wait_copies(meta, got_copies)
    heads = probs_t.shape[0]
    pairs = heads // 2
    local = heads * 64
    scale = 0.125

    def first_norm(block, unused):
        rows = rows_at(block)
        grad_hidden = (own[rows, :].astype(f32) + got[rows, :].astype(f32)) + grad_y2[rows, :]
        normed = normed1[rows, :]
        sums[0:1, :] += jnp.sum(grad_hidden * normed, axis=0, keepdims=True)
        sums[1:2, :] += jnp.sum(grad_hidden, axis=0, keepdims=True)
        grad = norm_back(grad_hidden, normed, inverse1[rows, 0:1], gain1[...])
        grad_y1[rows, :] = grad
        low = grad.astype(bf16)
        grad_branch[rows, :] = low
        sums[2:3, :] += jnp.sum(low.astype(f32), axis=0, keepdims=True)
        back = dot_nt(low, w_out[...]).astype(bf16)
        for pair in range(pairs):
            grad_attended[pair, rows, :] = back[:, pair * 128 : (pair + 1) * 128]
            grad_key[pair, rows, :] = jnp.zeros((BLOCK, 128), f32)
            grad_value[pair, rows, :] = jnp.zeros((BLOCK, 128), f32)
        return unused

    lax.fori_loop(0, meta[4], first_norm, 0)

    def one_sequence(second, unused):
        offset = second * meta[0]

        def sized(blocks):
            count = blocks * BLOCK
            wide = min(count, 256)
            every = rows_at(offset, blocks)

            def one_head(head, unused):
                pair = head // 2
                lane = lax.broadcasted_iota(jnp.int32, (wide, 128), 1)
                mine = (lane >= 64) == (head % 2 == 1)
                head_rows = pl.ds(pl.multiple_of(head * 64, 64), 64)
                values = value3[pair, every, :]
                keys = key_t[head_rows, every]
                for column in range(count // wide):
                    lanes = slice(column * wide, (column + 1) * wide)
                    places = rows_at(offset + column * (wide // BLOCK), wide // BLOCK)
                    zero = jnp.zeros((), bf16)
                    back = jnp.where(mine, grad_attended[pair, places, :], zero)
                    queries = jnp.where(mine, query3[pair, places, :], zero)
                    grad_probs = dot_nt(values, back)
                    probs_low = probs_t[head, every, lanes]
                    probs = probs_low.astype(f32)
                    mean = jnp.sum(probs * grad_probs, axis=0, keepdims=True)
                    grad_scores = (probs * (grad_probs - mean)).astype(bf16)
                    grad_scores_t[head, every, lanes] = grad_scores
                    grad_value[pair, every, :] += dot_nn(probs_low, back)
                    grad_key[pair, every, :] += dot_nn(grad_scores, queries)
                    grad_query_t[head_rows, places] = dot_nn(keys, grad_scores)
                return unused

            lax.fori_loop(0, heads, one_head, 0)

        by_length(meta, second, sized)
        return unused

    lax.fori_loop(0, 2, one_sequence, 0)

    def gather_grads(block, unused):
        rows = rows_at(block)
        query = (grad_query_t[:, rows].T * scale).astype(bf16)
        grad_qkv[rows, :local] = query
        for pair in range(pairs):
            lanes = slice(pair * 128, (pair + 1) * 128)
            grad_qkv[rows, local + pair * 128 : local + (pair + 1) * 128] = grad_key[pair, rows, :].astype(bf16)
            value = grad_value[pair, rows, :].astype(bf16)
            grad_qkv[rows, 2 * local + pair * 128 : 2 * local + (pair + 1) * 128] = value
            sums_qv[1:2, lanes] += jnp.sum(value.astype(f32), axis=0, keepdims=True)
        sums_qv[0:1, :] += jnp.sum(query.astype(f32), axis=0, keepdims=True)
        total = dot_nt(query, w_query[...])
        total = total + dot_nt(grad_qkv[rows, local : 2 * local], w_key[...])
        total = total + dot_nt(grad_qkv[rows, 2 * local :], w_value[...])
        part[rows, :] = total.astype(bf16)
        return unused

    lax.fori_loop(0, meta[4], gather_grads, 0)
    zero_tail(meta, grad_qkv)
    zero_tail(meta, grad_branch)


def attention_weights(meta, slots, packed_x, grad_qkv, own0, own1, own2, grad_branch, keep, give, stacked, attended, sems):
    copies = piece_copies(meta, (own0, own1, own2), attended, sems, False)
    start_copies(meta, copies)
    width = packed_x.shape[1]
    local = attended.shape[1]
    wait_copies(meta, copies)

    def sized(count):
        def project(tile, unused):
            lanes = pl.ds(pl.multiple_of(tile * 256, 256), 256)
            product = dot_tn(packed_x[:count, lanes], grad_qkv[:count, :])
            for part in range(3):
                spot = pl.ds(pl.multiple_of(part * width + tile * 256, 256), 256)
                stacked[spot, :] = product[:, part * local : (part + 1) * local]
            return unused

        lax.fori_loop(0, width // 256, project, 0)
        product = dot_tn(attended[:count, :], grad_branch[:count, :])
        for half in range(width // local):
            first = 3 * width + half * local
            stacked[first : first + local, :] = product[:, half * local : (half + 1) * local]

    by_cap(meta, sized)
    scatter_chunks(slots, keep, give, stacked)


def table_histogram(part, meta, grad_scores_t, buckets, total, left, right):
    heads = grad_scores_t.shape[0]
    group = 16
    total[...] = jnp.zeros(total.shape, f32)

    def one_sequence(second, unused):
        offset = second * meta[0]

        def sized(blocks):
            count = blocks * BLOCK
            upper_digit = lax.broadcasted_iota(jnp.int32, (32, count), 0)
            lower_digit = lax.broadcasted_iota(jnp.int32, (8, count), 0)

            def one_group(index, unused):
                rows = pl.ds(pl.multiple_of(index * group, group), group)
                spots = pl.ds(pl.multiple_of(offset * BLOCK + index * group, group), group)
                bucket = buckets[rows, :count]
                upper = bucket >> 3
                lower = bucket & 7
                grads = [grad_scores_t[head, spots, :count].astype(f32) for head in range(heads)]
                for row in range(group):
                    lanes = slice(row * count, (row + 1) * count)
                    left[:, lanes] = jnp.where(upper_digit == upper[row : row + 1, :], 1.0, 0.0).astype(bf16)
                    chosen = lower_digit == lower[row : row + 1, :]
                    for head in range(0, heads, 2):
                        spread = jnp.concatenate(
                            [jnp.where(chosen, grads[head + odd][row : row + 1, :], 0.0) for odd in range(2)], axis=0
                        )
                        right[head * 8 : (head + 2) * 8, lanes] = spread.astype(bf16)
                total[...] += dot_nt(right[:, : group * count], left[:, : group * count])
                return unused

            groups = count // group
            lax.fori_loop(groups * part // TABLE_PARTS, groups * (part + 1) // TABLE_PARTS, one_group, 0)

        by_length(meta, second, sized)
        return unused

    lax.fori_loop(0, 2, one_sequence, 0)


def input_gradient(meta, grad_y1, own, got, out):
    out[...] = jnp.zeros(out.shape, f32)

    def one_block(block, unused):
        second, first_row = place_of(meta, block)
        rows = rows_at(block)
        live = live_rows(meta, second, first_row)
        total = (own[rows, :].astype(f32) + got[rows, :].astype(f32)) + grad_y1[rows, :]
        out[second, pl.ds(first_row, BLOCK), :] = jnp.where(live, total, 0.0)
        return unused

    lax.fori_loop(0, meta[4], one_block, 0)


def unpack_ffn(places, *refs):
    chunks, (grad_up, grad_down) = refs[:-2], refs[-2:]
    rows = chunks[0].shape[0]
    units, width = grad_down.shape
    for index, chunk in enumerate(chunks):
        first = places[index] * rows
        values = chunk[...].astype(f32)

        @pl.when(first < units)
        def _():
            grad_down[pl.ds(pl.multiple_of(first, 8), rows), :] = values

        for half in range(units // width):
            low = units + half * width

            @pl.when((first >= low) & (first < low + width))
            def _():
                spot = pl.ds(pl.multiple_of(first - low, 8), rows)
                grad_up[spot, half * width : (half + 1) * width] = values


def unpack_attention(places, *refs):
    chunks, (grad_query, grad_key, grad_value, grad_out) = refs[:-4], refs[-4:]
    rows = chunks[0].shape[0]
    width, local = grad_query.shape
    for index, chunk in enumerate(chunks):
        first = places[index] * rows
        values = chunk[...].astype(f32)
        for part, target in enumerate((grad_query, grad_key, grad_value)):
            low = part * width

            @pl.when((first >= low) & (first < low + width))
            def _():
                target[pl.ds(pl.multiple_of(first - low, 8), rows), :] = values

        for half in range(width // local):
            low = 3 * width + half * local

            @pl.when((first >= low) & (first < low + local))
            def _():
                spot = pl.ds(pl.multiple_of(first - low, 8), rows)
                grad_out[spot, half * local : (half + 1) * local] = values


def run(kernel, specs, outs, scratch, name, room):
    params = pltpu.CompilerParams(vmem_limit_bytes=room * 1024 * 1024)

    def call(*args):
        return pl.pallas_call(
            kernel,
            in_specs=[{"s": in_smem, "v": in_vmem, "a": in_any}[kind] for kind in specs],
            out_specs=[in_any if kind == "a" else in_vmem for kind, unused in outs],
            out_shape=[shape for unused, shape in outs],
            scratch_shapes=scratch,
            compiler_params=params,
            name=name,
        )(*args)

    return call


def swap_tensor(value):
    return lax.ppermute(value, "tensor", ((0, 1), (1, 0)))


def exchange(pieces, level):
    got0 = swap_tensor(pieces[0])
    got1, got2 = lax.switch(
        level,
        (
            lambda one, two: (one, two),
            lambda one, two: (swap_tensor(one), two),
            lambda one, two: (swap_tensor(one), swap_tensor(two)),
        ),
        pieces[1],
        pieces[2],
    )
    return got0, got1, got2


def ring_pairs(dp_count):
    chips = dp_count // 2
    order = list(range(0, chips, 2)) + list(range(chips - 1, 0, -2))
    pairs = []
    for place, chip in enumerate(order):
        after = order[(place + 1) % chips]
        pairs.append((2 * chip, 2 * after))
        pairs.append((2 * after + 1, 2 * chip + 1))
    return tuple(pairs)


def exchange_within(pieces, level):
    return lax.switch(
        level,
        (
            lambda zero, one, two: (swap_tensor(zero), one, two),
            lambda zero, one, two: (swap_tensor(zero), swap_tensor(one), two),
            lambda zero, one, two: (swap_tensor(zero), swap_tensor(one), swap_tensor(two)),
        ),
        *pieces,
    )


def fold_bits(chips):
    bits = [1]
    bit = chips // 2
    while bit > 1:
        bits.append(bit)
        bit //= 2
    return bits


def ring_places(dp_count):
    chips = dp_count // 2
    index = lax.axis_index("dp")
    chip, core = index // 2, index % 2
    position = lambda at: jnp.where(at % 2 == 0, at // 2, chips - 1 - at // 2)
    steps = jnp.arange(chips, dtype=jnp.int32)
    mine, theirs = core * chips, (1 - core) * chips
    offsets = [
        sum(bit for step, bit in enumerate(fold_bits(chips)) if slot & (chips >> (step + 1))) for slot in range(chips)
    ]
    targets = position(chip ^ jnp.array(offsets, jnp.int32))
    turn = steps * (1 - 2 * core)
    own_chunks = mine + (position(chip) - turn) % chips
    other_chunks = theirs + (position(chip) + turn) % chips
    slots = jnp.concatenate([mine + targets, theirs + targets])
    return slots.astype(jnp.int32), jnp.concatenate([own_chunks, other_chunks]).astype(jnp.int32)


def siblings(dp_count):
    return tuple((i, i ^ 1) for i in range(dp_count))


def fold(parts, stage, dp_count, room, name):
    keep, give = parts
    if stage == 0:
        pairs = siblings(dp_count)
    else:
        distance = 2 * fold_bits(dp_count // 2)[stage - 1]
        pairs = tuple((i, i ^ distance) for i in range(dp_count))
    got = lax.ppermute(give, "dp", pairs)
    count = keep.shape[0]
    halves = [count // 2, count // 2] if count > 1 else [1]
    outs = [("v", shape_of((half, *keep.shape[1:]), bf16)) for half in halves]
    return run(add_halves, "vv", outs, [], f"{name}{stage}", room)(keep, got)


def gather_chunks(moving, dp_count):
    pairs = ring_pairs(dp_count)
    own = [moving]
    for unused in range(dp_count // 2 - 1):
        moving = lax.ppermute(moving, "dp", pairs)
        own.append(moving)
    return own + [lax.ppermute(piece, "dp", siblings(dp_count)) for piece in own]


def later(parts, *earlier):
    return after(parts[0], *earlier), parts[1]


def after(value, *earlier):
    return lax.optimization_barrier((value, earlier))[0]


def sum_small(value, dp_count):
    bit = 1
    while bit < dp_count:
        value = value + lax.ppermute(value, "dp", tuple((i, i ^ bit) for i in range(dp_count)))
        bit *= 2
    return value


def per_device(dp_count, *arrays):
    (
        inputs, lengths, buckets, w_query, b_query, w_key, w_value, b_value, w_out, b_out, norm1_gain, norm1_shift,
        w_up, b_up, w_down, b_down, norm2_gain, norm2_shift, position_table, cotangent,
    ) = arrays
    micro, seqs, seq_len, width = inputs.shape
    bucket_count, heads = position_table.shape
    local = w_query.shape[1]
    units = w_up.shape[1]
    chips = dp_count // 2
    rows = micro * seq_len
    x = inputs.reshape(micro, seq_len, width)
    grad_out = cotangent.reshape(micro, seq_len, width)
    sizes = lengths[:, 0]
    blocks = jnp.where(sizes <= BLOCK, 1, jnp.where(sizes <= 2 * BLOCK, 2, 4))
    used = blocks[0] + blocks[1]
    level = (used > CAPS[0]).astype(jnp.int32) + (used > CAPS[1]).astype(jnp.int32)
    cap = jnp.where(level == 0, CAPS[0], jnp.where(level == 1, CAPS[1], CAPS[2]))
    meta = jnp.stack([blocks[0], blocks[1], sizes[0], sizes[1], used, cap, cap, cap]).astype(jnp.int32)
    slots, places = ring_places(dp_count)
    buckets_t = buckets.T
    table = position_table.T
    row = lambda vector: vector.reshape(1, -1)
    piece_rows = (CAPS[0] * BLOCK, (CAPS[1] - CAPS[0]) * BLOCK, rows - CAPS[1] * BLOCK)
    pieces = lambda columns: [("a", shape_of((count, columns), bf16)) for count in piece_rows]
    vmem = pltpu.VMEM
    dma = pltpu.SemaphoreType.DMA

    w_out_got = swap_tensor(w_out)
    packed_x, query3, key3, value3, key_t, probs_t, *attended = run(
        attention_forward,
        "svvvvvvvv",
        [
            ("v", shape_of((rows, width), bf16)),
            ("v", shape_of((heads // 2, rows, 128), bf16)),
            ("v", shape_of((heads // 2, rows, 128), bf16)),
            ("v", shape_of((heads // 2, rows, 128), bf16)),
            ("v", shape_of((local, rows), bf16)),
            ("v", shape_of((heads, rows, seq_len), bf16)),
            *pieces(local),
        ],
        [
            vmem((heads, seq_len, seq_len), f32),
            vmem((local, rows), bf16),
            vmem((local, rows), f32),
            vmem((rows, local), bf16),
            dma((3,)),
        ],
        "attention_forward",
        16,
    )(meta, x, w_query, row(b_query), w_key, w_value, row(b_value), buckets_t, table)
    attended_got = exchange(attended, level)

    normed1, inverse1, hidden_low, activated, slope, *unit_part = run(
        feed_forward,
        "svaaaaaavvvvvvvv",
        [
            ("v", shape_of((rows, width), f32)),
            ("v", shape_of((rows, 128), f32)),
            ("v", shape_of((rows, width), bf16)),
            ("v", shape_of((rows, units), bf16)),
            ("v", shape_of((rows, units), bf16)),
            *pieces(width),
        ],
        [vmem((rows, local), bf16), vmem((rows, local), bf16), vmem((rows, width), bf16), dma((2, 3))],
        "feed_forward",
        8,
    )(
        meta, x, *attended, *attended_got, w_out, w_out_got, row(b_out), row(norm1_gain), row(norm1_shift),
        w_up, row(b_up), w_down,
    )
    unit_got = exchange(unit_part, level)

    layer_output, grad_y2, grad_ffn, grad_upper, sums2, sums_up, *hidden_part = run(
        second_norm,
        "svaaaaaavvvvvvvvv",
        [
            ("v", shape_of((micro, seq_len, width), bf16)),
            ("v", shape_of((rows, width), f32)),
            ("v", shape_of((rows, width), bf16)),
            ("v", shape_of((rows, units), bf16)),
            ("v", shape_of((8, width), f32)),
            ("v", shape_of((1, units), f32)),
            *pieces(width),
        ],
        [vmem((rows, width), bf16), vmem((rows, width), bf16), vmem((rows, width), bf16), dma((2, 3))],
        "second_norm",
        12,
    )(
        meta, grad_out, *unit_part, *unit_got, normed1, row(norm1_gain), row(norm1_shift), row(b_down),
        row(norm2_gain), row(norm2_shift), w_down, w_up, slope,
    )
    stacked_ffn = 2 * units
    ffn_parts = run(
        ffn_weights,
        "ssvvvv",
        [("v", shape_of((chips, stacked_ffn // (2 * chips), width), bf16))] * 2,
        [vmem((stacked_ffn, width), f32)],
        "ffn_weights",
        14,
    )(meta, slots, activated, grad_ffn, hidden_low, grad_upper)
    ffn_parts = fold(ffn_parts, 0, dp_count, 8, "ffn_fold")
    hidden_got = exchange_within(hidden_part, after(level, ffn_parts[0]))
    ffn_parts = fold(later(ffn_parts, hidden_got[0]), 1, dp_count, 8, "ffn_fold")

    grad_y1, grad_branch, grad_qkv, grad_scores_t, sums1, sums_qv, input_part = run(
        attention_backward,
        "saaaaaavvvvvvvvvvvvv",
        [
            ("v", shape_of((rows, width), f32)),
            ("v", shape_of((rows, width), bf16)),
            ("v", shape_of((rows, 3 * local), bf16)),
            ("v", shape_of((heads, rows, seq_len), bf16)),
            ("v", shape_of((8, width), f32)),
            ("v", shape_of((8, local), f32)),
            ("v", shape_of((rows, width), bf16)),
        ],
        [
            vmem((rows, width), bf16),
            vmem((rows, width), bf16),
            vmem((heads // 2, rows, 128), bf16),
            vmem((local, rows), f32),
            vmem((heads // 2, rows, 128), f32),
            vmem((heads // 2, rows, 128), f32),
            dma((2, 3)),
        ],
        "attention_backward",
        26,
    )(
        after(meta, ffn_parts[0]), *hidden_part, *hidden_got, grad_y2, normed1, inverse1, row(norm1_gain), w_out, w_query, w_key, w_value,
        query3, key3, value3, key_t, probs_t,
    )
    input_got = swap_tensor(input_part)
    ffn_parts = fold(ffn_parts, 2, dp_count, 8, "ffn_fold")

    stacked_attention = 3 * width + width * local // local
    attention_parts = run(
        attention_weights,
        "ssvvaaav",
        [("v", shape_of((chips, stacked_attention // (2 * chips), local), bf16))] * 2,
        [vmem((stacked_attention, local), f32), vmem((rows, local), bf16), dma((3,))],
        "attention_weights",
        9,
    )(after(meta, ffn_parts[0]), slots, packed_x, grad_qkv, *attended, grad_branch)

    table_sums = []

    def add_table(earlier):
        part = len(table_sums)
        table_sums.extend(
            run(
                functools.partial(table_histogram, part),
                "svv",
                [("v", shape_of((8 * heads, 32), f32))],
                [vmem((32, 16 * seq_len), bf16), vmem((8 * heads, 16 * seq_len), bf16)],
                f"table_histogram{part}",
                10,
            )(after(meta, *earlier), grad_scores_t, buckets_t)
        )

    stages = len(fold_bits(chips)) + 1
    for stage in range(3, stages):
        ffn_parts = fold(ffn_parts, stage, dp_count, 8, "ffn_fold")
    for stage in range(stages):
        attention_parts = fold(later(attention_parts, *table_sums[-1:]), stage, dp_count, 4, "attention_fold")
        if stage < TABLE_PARTS:
            add_table(attention_parts)
    ffn_pieces = gather_chunks(ffn_parts[0][0], dp_count)
    attention_pieces = gather_chunks(attention_parts[0][0], dp_count)
    grad_w_up, grad_w_down = run(
        unpack_ffn,
        "s" + "v" * len(ffn_pieces),
        [("v", shape_of((width, units), f32)), ("v", shape_of((units, width), f32))],
        [],
        "unpack_ffn",
        18,
    )(places, *ffn_pieces)
    grad_w_query, grad_w_key, grad_w_value, grad_w_out = run(
        unpack_attention,
        "s" + "v" * len(attention_pieces),
        [("v", shape_of((width, local), f32))] * 3 + [("v", shape_of((local, width), f32))],
        [],
        "unpack_attention",
        10,
    )(places, *attention_pieces)

    (grad_inputs,) = run(
        input_gradient,
        "svvv",
        [("v", shape_of((micro, seq_len, width), f32))],
        [],
        "input_gradient",
        12,
    )(meta, grad_y1, input_part, input_got)

    table_part = sum(table_sums).reshape(heads, 8, 32).transpose(2, 1, 0).reshape(bucket_count, heads)
    small = jnp.concatenate(
        [
            sums2[0], sums2[1], sums2[2], sums_up[0], sums1[0], sums1[1], sums1[2], sums_qv[0], sums_qv[1],
            table_part.reshape(-1),
        ]
    ).reshape(-1, 128)
    small = sum_small(small, dp_count).reshape(-1)
    cuts = []
    start = 0
    for count in (width, width, width, units, width, width, width, local, local, bucket_count * heads):
        cuts.append(small[start : start + count])
        start += count
    grad_gain2, grad_shift2, grad_b_down, grad_b_up, grad_gain1, grad_shift1, grad_b_out, grad_b_query, grad_b_value, table_grad = cuts
    return (
        layer_output.reshape(inputs.shape),
        grad_inputs.reshape(inputs.shape),
        grad_w_query,
        grad_b_query,
        grad_w_key,
        grad_w_value,
        grad_b_value,
        grad_w_out,
        grad_b_out,
        grad_gain1,
        grad_shift1,
        grad_w_up,
        grad_b_up,
        grad_w_down,
        grad_b_down,
        grad_gain2,
        grad_shift2,
        table_grad.reshape(bucket_count, heads),
    )


def solution(mesh):
    placed = (
        P(None, "dp", None, None),
        P(None, "dp"),
        P(),
        P(None, "tensor"),
        P("tensor"),
        P(None, "tensor"),
        P(None, "tensor"),
        P("tensor"),
        P("tensor", None),
        P(),
        P(),
        P(),
        P(None, "tensor"),
        P("tensor"),
        P("tensor", None),
        P(),
        P(),
        P(),
        P(None, "tensor"),
        P(None, "dp", None, None),
    )
    dp_count = mesh.shape["dp"]
    return jax.shard_map(
        lambda *arrays: per_device(dp_count, *arrays),
        mesh=mesh,
        in_specs=placed,
        out_specs=(
            P(None, "dp", None, None),
            P(None, "dp", None, None),
            P(None, "tensor"),
            P("tensor"),
            P(None, "tensor"),
            P(None, "tensor"),
            P("tensor"),
            P("tensor", None),
            P(),
            P(),
            P(),
            P(None, "tensor"),
            P("tensor"),
            P("tensor", None),
            P(),
            P(),
            P(),
            P(None, "tensor"),
        ),
        check_vma=False,
    )
```

```python
import functools

import jax
import jax.numpy as jnp
from jax import lax
from jax.experimental import pallas as pl
from jax.experimental.pallas import tpu as pltpu
from jax.sharding import PartitionSpec as P

epsilon = 1e-05
masked_value = -1e30
inv_root_two = 0.7071067811865476
inv_root_tau = 0.3989422804014327

BLOCK = 128
CAPS = (2, 5, 8)
TABLE_PARTS = 6
UNPACK_PARTS = 4
bf16 = jnp.bfloat16
f32 = jnp.float32
shape_of = jax.ShapeDtypeStruct

in_vmem = pl.BlockSpec(memory_space=pltpu.VMEM)
in_smem = pl.BlockSpec(memory_space=pltpu.SMEM)
in_any = pl.BlockSpec(memory_space=pl.ANY)


def rows_at(block, count=1):
    return pl.ds(pl.multiple_of(block * BLOCK, BLOCK), count * BLOCK)


def dot_nn(left, right):
    return lax.dot_general(left, right, (((1,), (0,)), ((), ())), preferred_element_type=f32)


def dot_nt(left, right):
    return lax.dot_general(left, right, (((1,), (1,)), ((), ())), preferred_element_type=f32)


def dot_tn(left, right):
    return lax.dot_general(left, right, (((0,), (0,)), ((), ())), preferred_element_type=f32)


def place_of(meta, block):
    second = (block >= meta[0]).astype(jnp.int32)
    return second, pl.multiple_of((block - second * meta[0]) * BLOCK, BLOCK)


def live_rows(meta, second, first_row):
    rows = lax.broadcasted_iota(jnp.int32, (BLOCK, 1), 0) + first_row
    return rows < meta[2 + second]


def zero_tail(meta, ref):
    def clear(block, unused):
        ref[rows_at(block), :] = jnp.zeros((BLOCK, ref.shape[1]), ref.dtype)
        return unused

    lax.fori_loop(meta[4], meta[5], clear, 0)


def piece_copies(meta, pieces, whole, sems, to_pieces):
    start = 0
    made = []
    for index, piece in enumerate(pieces):
        rows = piece.shape[0]
        part = whole.at[pl.ds(start, rows), :]
        pair = (part, piece) if to_pieces else (piece, part)
        made.append((start // BLOCK, pltpu.make_async_copy(pair[0], pair[1], sems.at[index])))
        start += rows
    return made


def start_copies(meta, made):
    for first, copy in made:
        @pl.when(meta[5] > first)
        def _():
            copy.start()


def wait_copies(meta, made):
    for first, copy in made:
        @pl.when(meta[5] > first)
        def _():
            copy.wait()


def by_length(meta, second, body):
    for blocks in (1, 2, 4):
        @pl.when(meta[second] == blocks)
        def _():
            body(blocks)


def by_cap(meta, body):
    for blocks in CAPS:
        @pl.when(meta[5] == blocks)
        def _():
            body(blocks * BLOCK)


def norm_forward(rows, gain, shift):
    centre = rows - jnp.mean(rows, axis=-1, keepdims=True)
    inverse = lax.rsqrt(jnp.mean(centre * centre, axis=-1, keepdims=True) + epsilon)
    normed = centre * inverse
    return normed, normed * gain + shift, inverse


def norm_back(grad_rows, normed, inverse, gain):
    scaled = grad_rows * gain
    first_mean = jnp.mean(scaled, axis=-1, keepdims=True)
    second_mean = jnp.mean(scaled * normed, axis=-1, keepdims=True)
    return inverse * (scaled - first_mean - normed * second_mean)


def attention_forward(
    meta, x, w_query, b_query, w_key, w_value, b_value, buckets, table,
    packed_x, query3, key3, value3, key_t, probs_t, piece0, piece1, piece2,
    bias, value_t, attended_t, attended, sems,
):
    heads = probs_t.shape[0]
    pairs = heads // 2
    scale = 0.125
    seq_len = x.shape[1]
    columns = seq_len // BLOCK

    def bias_rows(group, unused):
        rows = pl.ds(pl.multiple_of(group * 8, 8), 8)
        for column in range(columns):
            lanes = slice(column * BLOCK, (column + 1) * BLOCK)
            bucket = buckets[rows, lanes]
            low = bucket & 127
            upper = bucket >= 128
            for head in range(heads):
                first = jnp.broadcast_to(table[head : head + 1, :128], (8, 128))
                second = jnp.broadcast_to(table[head : head + 1, 128:], (8, 128))
                bias[head, rows, lanes] = jnp.where(
                    upper,
                    jnp.take_along_axis(second, low, axis=1, mode="promise_in_bounds"),
                    jnp.take_along_axis(first, low, axis=1, mode="promise_in_bounds"),
                )
        return unused

    lax.fori_loop(0, jnp.maximum(meta[0], meta[1]) * (BLOCK // 8), bias_rows, 0)

    def project(block, unused):
        second, first_row = place_of(meta, block)
        rows = rows_at(block)
        part = x[second, pl.ds(first_row, BLOCK), :]
        packed_x[rows, :] = part
        query = ((dot_nn(part, w_query[...]) + b_query[...]).astype(bf16).astype(f32) * scale).astype(bf16)
        key = dot_nn(part, w_key[...])
        value = dot_nn(part, w_value[...]) + b_value[...]
        key_t[:, rows] = key.T.astype(bf16)
        value_t[:, rows] = value.T.astype(bf16)
        key = key.astype(bf16)
        value = value.astype(bf16)
        for pair in range(pairs):
            lanes = slice(pair * 128, (pair + 1) * 128)
            query3[pair, rows, :] = query[:, lanes]
            key3[pair, rows, :] = key[:, lanes]
            value3[pair, rows, :] = value[:, lanes]
        return unused

    lax.fori_loop(0, meta[4], project, 0)

    def one_sequence(second, unused):
        offset = second * meta[0]
        length = meta[2 + second]

        def sized(blocks):
            count = blocks * BLOCK
            wide = min(count, 256)

            def one_head(head, unused):
                pair = head // 2
                lane = lax.broadcasted_iota(jnp.int32, (count, 128), 1)
                mine = (lane >= 64) == (head % 2 == 1)
                keys = jnp.where(mine, key3[pair, rows_at(offset, blocks), :], jnp.zeros((), bf16))
                values = value_t[pl.ds(pl.multiple_of(head * 64, 64), 64), rows_at(offset, blocks)]
                live = lax.broadcasted_iota(jnp.int32, (count, wide), 0) < length
                for column in range(count // wide):
                    lanes = slice(column * wide, (column + 1) * wide)
                    places = rows_at(offset + column * (wide // BLOCK), wide // BLOCK)
                    scores = dot_nt(keys, query3[pair, places, :]) + bias[head, :count, lanes]
                    scores = jnp.where(live, scores, masked_value)
                    top = jnp.max(scores, axis=0, keepdims=True)
                    powers = jnp.exp(scores - top)
                    total = jnp.sum(powers, axis=0, keepdims=True)
                    probs = (powers * (1.0 / total)).astype(bf16)
                    probs_t[head, rows_at(offset, blocks), lanes] = probs
                    attended_t[pl.ds(pl.multiple_of(head * 64, 64), 64), places] = dot_nn(values, probs)
                return unused

            lax.fori_loop(0, heads, one_head, 0)

        by_length(meta, second, sized)
        return unused

    lax.fori_loop(0, 2, one_sequence, 0)

    def turn(block, unused):
        attended[rows_at(block), :] = attended_t[:, rows_at(block)].T.astype(bf16)
        return unused

    lax.fori_loop(0, meta[4], turn, 0)
    zero_tail(meta, attended)
    zero_tail(meta, packed_x)
    made = piece_copies(meta, (piece0, piece1, piece2), attended, sems, True)
    start_copies(meta, made)
    wait_copies(meta, made)


def feed_forward(
    meta, x, own0, own1, own2, got0, got1, got2, w_out_own, w_out_got, b_out, gain, shift,
    w_up, b_up, w_down,
    normed1, inverse1, hidden_low, activated, slope, piece0, piece1, piece2,
    own, got, part, sems,
):
    own_copies = piece_copies(meta, (own0, own1, own2), own, sems.at[0], False)
    got_copies = piece_copies(meta, (got0, got1, got2), got, sems.at[1], False)
    start_copies(meta, own_copies)
    start_copies(meta, got_copies)
    wait_copies(meta, own_copies)
    wait_copies(meta, got_copies)
    width = w_up.shape[1]

    def one_block(block, unused):
        second, first_row = place_of(meta, block)
        rows = rows_at(block)
        head_own = dot_nn(own[rows, :], w_out_own[...]).astype(bf16).astype(f32)
        head_got = dot_nn(got[rows, :], w_out_got[...]).astype(bf16).astype(f32)
        branch = (head_own + head_got) + b_out[...]
        base = x[second, pl.ds(first_row, BLOCK), :].astype(f32) + branch
        normed, hidden, inverse = norm_forward(base, gain[...], shift[...])
        normed1[rows, :] = normed
        inverse1[rows, :] = jnp.broadcast_to(inverse, (BLOCK, 128))
        low = hidden.astype(bf16)
        hidden_low[rows, :] = low
        for column in range(width // 512):
            lanes = slice(column * 512, (column + 1) * 512)
            upper = dot_nn(low, w_up[:, lanes]) + b_up[:, lanes]
            normal = 0.5 * (1.0 + lax.erf(upper * inv_root_two))
            activated[rows, lanes] = (upper * normal).astype(bf16)
            slope[rows, lanes] = (
                normal + upper * inv_root_tau * jnp.exp(-0.5 * upper * upper)
            ).astype(bf16)
        part[rows, :] = dot_nn(activated[rows, :], w_down[...]).astype(bf16)
        return unused

    lax.fori_loop(0, meta[4], one_block, 0)
    zero_tail(meta, part)
    made = piece_copies(meta, (piece0, piece1, piece2), part, sems.at[0], True)
    start_copies(meta, made)
    zero_tail(meta, activated)
    zero_tail(meta, hidden_low)
    wait_copies(meta, made)


def second_norm(
    meta, cotangent, own0, own1, own2, got0, got1, got2, normed1, gain1, shift1, b_down, gain2, shift2,
    w_down, w_up, slope,
    layer_output, grad_y2, grad_ffn, grad_upper, sums, sums_up, piece0, piece1, piece2,
    own, got, part, sems,
):
    own_copies = piece_copies(meta, (own0, own1, own2), own, sems.at[0], False)
    got_copies = piece_copies(meta, (got0, got1, got2), got, sems.at[1], False)
    start_copies(meta, own_copies)
    start_copies(meta, got_copies)
    sums[...] = jnp.zeros(sums.shape, f32)
    sums_up[...] = jnp.zeros(sums_up.shape, f32)
    layer_output[...] = jnp.zeros(layer_output.shape, bf16)
    wait_copies(meta, own_copies)
    wait_copies(meta, got_copies)
    width = w_up.shape[1]

    def one_block(block, unused):
        second, first_row = place_of(meta, block)
        rows = rows_at(block)
        spot = pl.ds(first_row, BLOCK)
        live = live_rows(meta, second, first_row)
        ffn_out = (own[rows, :].astype(f32) + got[rows, :].astype(f32)) + b_down[...]
        hidden = normed1[rows, :] * gain1[...] + shift1[...]
        normed, result, inverse = norm_forward(hidden + ffn_out, gain2[...], shift2[...])
        layer_output[second, spot, :] = jnp.where(live, result, 0.0).astype(bf16)
        grad_result = jnp.where(live, cotangent[second, spot, :].astype(f32), 0.0)
        sums[0:1, :] += jnp.sum(grad_result * normed, axis=0, keepdims=True)
        sums[1:2, :] += jnp.sum(grad_result, axis=0, keepdims=True)
        grad = norm_back(grad_result, normed, inverse, gain2[...])
        grad_y2[rows, :] = grad
        low = grad.astype(bf16)
        grad_ffn[rows, :] = low
        sums[2:3, :] += jnp.sum(low.astype(f32), axis=0, keepdims=True)
        for column in range(width // 512):
            lanes = slice(column * 512, (column + 1) * 512)
            back = dot_nt(low, w_down[lanes, :]) * slope[rows, lanes].astype(f32)
            back = back.astype(bf16)
            grad_upper[rows, lanes] = back
            sums_up[:, lanes] += jnp.sum(back.astype(f32), axis=0, keepdims=True)
        part[rows, :] = dot_nt(grad_upper[rows, :], w_up[...]).astype(bf16)
        return unused

    lax.fori_loop(0, meta[4], one_block, 0)
    zero_tail(meta, part)
    made = piece_copies(meta, (piece0, piece1, piece2), part, sems.at[0], True)
    start_copies(meta, made)
    zero_tail(meta, grad_ffn)
    zero_tail(meta, grad_upper)
    wait_copies(meta, made)


def ffn_weights(meta, slots, activated, grad_ffn, hidden_low, grad_upper, keep, give, stacked):
    width = grad_ffn.shape[1]
    units = activated.shape[1]

    def sized(count):
        def down(tile, unused):
            lanes = pl.ds(pl.multiple_of(tile * 256, 256), 256)
            stacked[lanes, :] = dot_tn(activated[:count, lanes], grad_ffn[:count, :])
            return unused

        lax.fori_loop(0, units // 256, down, 0)

        def up(tile, unused):
            lanes = pl.ds(pl.multiple_of(tile * 256, 256), 256)
            product = dot_tn(hidden_low[:count, lanes], grad_upper[:count, :])
            for half in range(units // width):
                spot = pl.ds(pl.multiple_of(units + half * width + tile * 256, 256), 256)
                stacked[spot, :] = product[:, half * width : (half + 1) * width]
            return unused

        lax.fori_loop(0, width // 256, up, 0)

    by_cap(meta, sized)
    scatter_chunks(slots, keep, give, stacked)


def scatter_chunks(slots, keep, give, stacked):
    chips, rows, unused = keep.shape

    def move(index, unused):
        for first, target in ((0, keep), (chips, give)):
            spot = pl.ds(pl.multiple_of(slots[first + index] * rows, 8), rows)
            target[index] = stacked[spot, :].astype(bf16)
        return unused

    lax.fori_loop(0, chips, move, 0)


def add_halves(keep, got, *outs):
    count = outs[0].shape[0]
    for index in range(keep.shape[0]):
        total = keep[index].astype(f32) + got[index].astype(f32)
        outs[index // count][index % count] = total.astype(bf16)


def attention_backward(
    meta, own0, own1, own2, got0, got1, got2, grad_y2, normed1, inverse1, gain1,
    w_out, w_query, w_key, w_value, query3, key3, value3, key_t, probs_t,
    grad_y1, grad_branch, grad_qkv, grad_scores_t, sums, sums_qv, part,
    own, got, grad_attended, grad_query_t, grad_key, grad_value, sems,
):
    own_copies = piece_copies(meta, (own0, own1, own2), own, sems.at[0], False)
    got_copies = piece_copies(meta, (got0, got1, got2), got, sems.at[1], False)
    start_copies(meta, own_copies)
    start_copies(meta, got_copies)
    sums[...] = jnp.zeros(sums.shape, f32)
    sums_qv[...] = jnp.zeros(sums_qv.shape, f32)
    wait_copies(meta, own_copies)
    wait_copies(meta, got_copies)
    heads = probs_t.shape[0]
    pairs = heads // 2
    local = heads * 64
    scale = 0.125

    def first_norm(block, unused):
        rows = rows_at(block)
        grad_hidden = (own[rows, :].astype(f32) + got[rows, :].astype(f32)) + grad_y2[rows, :]
        normed = normed1[rows, :]
        sums[0:1, :] += jnp.sum(grad_hidden * normed, axis=0, keepdims=True)
        sums[1:2, :] += jnp.sum(grad_hidden, axis=0, keepdims=True)
        grad = norm_back(grad_hidden, normed, inverse1[rows, 0:1], gain1[...])
        grad_y1[rows, :] = grad
        low = grad.astype(bf16)
        grad_branch[rows, :] = low
        sums[2:3, :] += jnp.sum(low.astype(f32), axis=0, keepdims=True)
        back = dot_nt(low, w_out[...]).astype(bf16)
        for pair in range(pairs):
            grad_attended[pair, rows, :] = back[:, pair * 128 : (pair + 1) * 128]
            grad_key[pair, rows, :] = jnp.zeros((BLOCK, 128), f32)
            grad_value[pair, rows, :] = jnp.zeros((BLOCK, 128), f32)
        return unused

    lax.fori_loop(0, meta[4], first_norm, 0)

    def one_sequence(second, unused):
        offset = second * meta[0]

        def sized(blocks):
            count = blocks * BLOCK
            wide = min(count, 256)
            every = rows_at(offset, blocks)

            def one_head(head, unused):
                pair = head // 2
                lane = lax.broadcasted_iota(jnp.int32, (wide, 128), 1)
                mine = (lane >= 64) == (head % 2 == 1)
                head_rows = pl.ds(pl.multiple_of(head * 64, 64), 64)
                values = value3[pair, every, :]
                keys = key_t[head_rows, every]
                for column in range(count // wide):
                    lanes = slice(column * wide, (column + 1) * wide)
                    places = rows_at(offset + column * (wide // BLOCK), wide // BLOCK)
                    zero = jnp.zeros((), bf16)
                    back = jnp.where(mine, grad_attended[pair, places, :], zero)
                    queries = jnp.where(mine, query3[pair, places, :], zero)
                    grad_probs = dot_nt(values, back)
                    probs_low = probs_t[head, every, lanes]
                    probs = probs_low.astype(f32)
                    mean = jnp.sum(probs * grad_probs, axis=0, keepdims=True)
                    grad_scores = (probs * (grad_probs - mean)).astype(bf16)
                    grad_scores_t[head, every, lanes] = grad_scores
                    grad_value[pair, every, :] += dot_nn(probs_low, back)
                    grad_key[pair, every, :] += dot_nn(grad_scores, queries)
                    grad_query_t[head_rows, places] = dot_nn(keys, grad_scores)
                return unused

            lax.fori_loop(0, heads, one_head, 0)

        by_length(meta, second, sized)
        return unused

    lax.fori_loop(0, 2, one_sequence, 0)

    def gather_grads(block, unused):
        rows = rows_at(block)
        query = (grad_query_t[:, rows].T * scale).astype(bf16)
        grad_qkv[rows, :local] = query
        for pair in range(pairs):
            lanes = slice(pair * 128, (pair + 1) * 128)
            grad_qkv[rows, local + pair * 128 : local + (pair + 1) * 128] = grad_key[pair, rows, :].astype(bf16)
            value = grad_value[pair, rows, :].astype(bf16)
            grad_qkv[rows, 2 * local + pair * 128 : 2 * local + (pair + 1) * 128] = value
            sums_qv[1:2, lanes] += jnp.sum(value.astype(f32), axis=0, keepdims=True)
        sums_qv[0:1, :] += jnp.sum(query.astype(f32), axis=0, keepdims=True)
        total = dot_nt(query, w_query[...])
        total = total + dot_nt(grad_qkv[rows, local : 2 * local], w_key[...])
        total = total + dot_nt(grad_qkv[rows, 2 * local :], w_value[...])
        part[rows, :] = total.astype(bf16)
        return unused

    lax.fori_loop(0, meta[4], gather_grads, 0)
    zero_tail(meta, grad_qkv)
    zero_tail(meta, grad_branch)


def attention_weights(meta, slots, packed_x, grad_qkv, own0, own1, own2, grad_branch, keep, give, stacked, attended, sems):
    copies = piece_copies(meta, (own0, own1, own2), attended, sems, False)
    start_copies(meta, copies)
    width = packed_x.shape[1]
    local = attended.shape[1]
    wait_copies(meta, copies)

    def sized(count):
        def project(tile, unused):
            lanes = pl.ds(pl.multiple_of(tile * 256, 256), 256)
            product = dot_tn(packed_x[:count, lanes], grad_qkv[:count, :])
            for part in range(3):
                spot = pl.ds(pl.multiple_of(part * width + tile * 256, 256), 256)
                stacked[spot, :] = product[:, part * local : (part + 1) * local]
            return unused

        lax.fori_loop(0, width // 256, project, 0)
        product = dot_tn(attended[:count, :], grad_branch[:count, :])
        for half in range(width // local):
            first = 3 * width + half * local
            stacked[first : first + local, :] = product[:, half * local : (half + 1) * local]

    by_cap(meta, sized)
    scatter_chunks(slots, keep, give, stacked)


def table_histogram(part, meta, grad_scores_t, buckets, total, left, right):
    heads = grad_scores_t.shape[0]
    group = 16
    total[...] = jnp.zeros(total.shape, f32)

    def one_sequence(second, unused):
        offset = second * meta[0]

        def sized(blocks):
            count = blocks * BLOCK
            upper_digit = lax.broadcasted_iota(jnp.int32, (32, count), 0)
            lower_digit = lax.broadcasted_iota(jnp.int32, (8, count), 0)

            def one_group(index, unused):
                rows = pl.ds(pl.multiple_of(index * group, group), group)
                spots = pl.ds(pl.multiple_of(offset * BLOCK + index * group, group), group)
                bucket = buckets[rows, :count]
                upper = bucket >> 3
                lower = bucket & 7
                grads = [grad_scores_t[head, spots, :count].astype(f32) for head in range(heads)]
                for row in range(group):
                    lanes = slice(row * count, (row + 1) * count)
                    left[:, lanes] = jnp.where(upper_digit == upper[row : row + 1, :], 1.0, 0.0).astype(bf16)
                    chosen = lower_digit == lower[row : row + 1, :]
                    for head in range(0, heads, 2):
                        spread = jnp.concatenate(
                            [jnp.where(chosen, grads[head + odd][row : row + 1, :], 0.0) for odd in range(2)], axis=0
                        )
                        right[head * 8 : (head + 2) * 8, lanes] = spread.astype(bf16)
                total[...] += dot_nt(right[:, : group * count], left[:, : group * count])
                return unused

            groups = count // group
            lax.fori_loop(groups * part // TABLE_PARTS, groups * (part + 1) // TABLE_PARTS, one_group, 0)

        by_length(meta, second, sized)
        return unused

    lax.fori_loop(0, 2, one_sequence, 0)


def input_gradient(meta, grad_y1, own, got, out):
    out[...] = jnp.zeros(out.shape, f32)

    def one_block(block, unused):
        second, first_row = place_of(meta, block)
        rows = rows_at(block)
        live = live_rows(meta, second, first_row)
        total = (own[rows, :].astype(f32) + got[rows, :].astype(f32)) + grad_y1[rows, :]
        out[second, pl.ds(first_row, BLOCK), :] = jnp.where(live, total, 0.0)
        return unused

    lax.fori_loop(0, meta[4], one_block, 0)


def pack_small(sums2, sums_up, sums1, sums_qv, *refs):
    tables, out = refs[:-1], refs[-1]
    out[...] = jnp.zeros(out.shape, f32)
    row = 0
    for source, count in ((sums2, 3), (sums_up, 1), (sums1, 3), (sums_qv, 2)):
        for line in range(count):
            for column in range(source.shape[1] // 128):
                out[row : row + 1, :] = source[line : line + 1, column * 128 : (column + 1) * 128]
                row += 1
    height, wide = tables[0].shape
    first = out.shape[0] - height
    out[first:, :wide] = sum(table[...] for table in tables)


def unpack(first_place, count, targets_of, places, *refs):
    chunks, (wide, sems) = refs[:count], refs[-2:]
    outs, token = refs[-3 - targets_of.outs : -3], refs[-3]
    token[...] = jnp.zeros(token.shape, f32)
    rows = chunks[0].shape[0]
    copies = []
    for index, chunk in enumerate(chunks):
        wide[index] = chunk[...].astype(f32)
        first = places[first_place + index] * rows
        for low, high, target in targets_of(outs, rows):
            inside = (first >= low) & (first < high)
            copy = pltpu.make_async_copy(
                wide.at[index], target(pl.ds(pl.multiple_of(first - low, 8), rows)), sems.at[index]
            )
            copies.append((inside, copy))

            @pl.when(inside)
            def _():
                copy.start()

    for inside, copy in copies:
        @pl.when(inside)
        def _():
            copy.wait()


def ffn_targets(outs, rows):
    grad_up, grad_down = outs
    units, width = grad_down.shape
    found = [(0, units, lambda spot: grad_down.at[spot, :])]
    for half in range(units // width):
        lanes = pl.ds(half * width, width)
        low = units + half * width
        found.append((low, low + width, lambda spot, lanes=lanes: grad_up.at[spot, lanes]))
    return found


def attention_targets(outs, rows):
    width, local = outs[0].shape
    found = []
    for part in range(3):
        found.append((part * width, (part + 1) * width, lambda spot, part=part: outs[part].at[spot, :]))
    for half in range(width // local):
        lanes = pl.ds(half * local, local)
        low = 3 * width + half * local
        found.append((low, low + local, lambda spot, lanes=lanes: outs[3].at[spot, lanes]))
    return found


ffn_targets.outs = 2
attention_targets.outs = 4


def run(kernel, specs, outs, scratch, name, room, aliases={}):
    params = pltpu.CompilerParams(vmem_limit_bytes=room * 1024 * 1024)

    def call(*args):
        return pl.pallas_call(
            kernel,
            in_specs=[{"s": in_smem, "v": in_vmem, "a": in_any}[kind] for kind in specs],
            out_specs=[in_any if kind == "a" else in_vmem for kind, unused in outs],
            out_shape=[shape for unused, shape in outs],
            scratch_shapes=scratch,
            compiler_params=params,
            input_output_aliases=aliases,
            name=name,
        )(*args)

    return call


def unpack_all(pieces, places, targets_of, shapes, name, earlier=()):
    chips = len(pieces) // 2
    ordered = [piece for pair in zip(pieces[:chips], pieces[chips:]) for piece in pair]
    ordered_places = jnp.stack([places[:chips], places[chips:]], axis=1).reshape(-1)
    made, tokens = [], []
    parts = min(UNPACK_PARTS, chips)
    for part in range(parts):
        first, last = 2 * (chips * part // parts), 2 * (chips * (part + 1) // parts)
        count = last - first
        rows, columns = ordered[0].shape
        *made, token = run(
            functools.partial(unpack, first, count, targets_of),
            "s" + "v" * count + "a" * (len(made) + len(earlier)),
            [("a", shape) for shape in shapes] + [("v", shape_of((8, 128), f32))],
            [pltpu.VMEM((count, rows, columns), f32), pltpu.SemaphoreType.DMA((count,))],
            f"{name}{part}",
            6,
            {1 + count + index: index for index in range(len(made))},
        )(ordered_places, *ordered[first:last], *made, *earlier)
        tokens.append(token)
    return made, tokens


def swap_tensor(value):
    return lax.ppermute(value, "tensor", ((0, 1), (1, 0)))


def exchange(pieces, level):
    got0 = swap_tensor(pieces[0])
    got1, got2 = lax.switch(
        level,
        (
            lambda one, two: (one, two),
            lambda one, two: (swap_tensor(one), two),
            lambda one, two: (swap_tensor(one), swap_tensor(two)),
        ),
        pieces[1],
        pieces[2],
    )
    return got0, got1, got2


def ring_pairs(dp_count):
    chips = dp_count // 2
    order = list(range(0, chips, 2)) + list(range(chips - 1, 0, -2))
    pairs = []
    for place, chip in enumerate(order):
        after = order[(place + 1) % chips]
        pairs.append((2 * chip, 2 * after))
        pairs.append((2 * after + 1, 2 * chip + 1))
    return tuple(pairs)


def exchange_within(pieces, level):
    return lax.switch(
        level,
        (
            lambda zero, one, two: (swap_tensor(zero), one, two),
            lambda zero, one, two: (swap_tensor(zero), swap_tensor(one), two),
            lambda zero, one, two: (swap_tensor(zero), swap_tensor(one), swap_tensor(two)),
        ),
        *pieces,
    )


def fold_bits(chips):
    bits = [1]
    bit = chips // 2
    while bit > 1:
        bits.append(bit)
        bit //= 2
    return bits


def ring_places(dp_count):
    chips = dp_count // 2
    index = lax.axis_index("dp")
    chip, core = index // 2, index % 2
    position = lambda at: jnp.where(at % 2 == 0, at // 2, chips - 1 - at // 2)
    steps = jnp.arange(chips, dtype=jnp.int32)
    mine, theirs = core * chips, (1 - core) * chips
    offsets = [
        sum(bit for step, bit in enumerate(fold_bits(chips)) if slot & (chips >> (step + 1))) for slot in range(chips)
    ]
    targets = position(chip ^ jnp.array(offsets, jnp.int32))
    turn = steps * (1 - 2 * core)
    own_chunks = mine + (position(chip) - turn) % chips
    other_chunks = theirs + (position(chip) + turn) % chips
    slots = jnp.concatenate([mine + targets, theirs + targets])
    return slots.astype(jnp.int32), jnp.concatenate([own_chunks, other_chunks]).astype(jnp.int32)


def siblings(dp_count):
    return tuple((i, i ^ 1) for i in range(dp_count))


def fold(parts, stage, dp_count, room, name):
    keep, give = parts
    if stage == 0:
        pairs = siblings(dp_count)
    else:
        distance = 2 * fold_bits(dp_count // 2)[stage - 1]
        pairs = tuple((i, i ^ distance) for i in range(dp_count))
    got = lax.ppermute(give, "dp", pairs)
    count = keep.shape[0]
    halves = [count // 2, count // 2] if count > 1 else [1]
    outs = [("v", shape_of((half, *keep.shape[1:]), bf16)) for half in halves]
    return run(add_halves, "vv", outs, [], f"{name}{stage}", room)(keep, got)


def gather_chunks(moving, dp_count, fillers={}):
    pairs = ring_pairs(dp_count)
    own = [moving]
    for step in range(dp_count // 2 - 1):
        if step in fillers:
            moving = after(moving, fillers[step])
        moving = lax.ppermute(moving, "dp", pairs)
        own.append(moving)
    return own + [lax.ppermute(piece, "dp", siblings(dp_count)) for piece in own]


def later(parts, *earlier):
    return after(parts[0], *earlier), parts[1]


def after(value, *earlier):
    return lax.optimization_barrier((value, earlier))[0]


def sum_small(value, dp_count):
    bit = 1
    while bit < dp_count:
        value = value + lax.ppermute(value, "dp", tuple((i, i ^ bit) for i in range(dp_count)))
        bit *= 2
    return value


def per_device(dp_count, *arrays):
    (
        inputs, lengths, buckets, w_query, b_query, w_key, w_value, b_value, w_out, b_out, norm1_gain, norm1_shift,
        w_up, b_up, w_down, b_down, norm2_gain, norm2_shift, position_table, cotangent,
    ) = arrays
    micro, seqs, seq_len, width = inputs.shape
    bucket_count, heads = position_table.shape
    local = w_query.shape[1]
    units = w_up.shape[1]
    chips = dp_count // 2
    rows = micro * seq_len
    x = inputs.reshape(micro, seq_len, width)
    grad_out = cotangent.reshape(micro, seq_len, width)
    sizes = lengths[:, 0]
    blocks = jnp.where(sizes <= BLOCK, 1, jnp.where(sizes <= 2 * BLOCK, 2, 4))
    used = blocks[0] + blocks[1]
    level = (used > CAPS[0]).astype(jnp.int32) + (used > CAPS[1]).astype(jnp.int32)
    cap = jnp.where(level == 0, CAPS[0], jnp.where(level == 1, CAPS[1], CAPS[2]))
    meta = jnp.stack([blocks[0], blocks[1], sizes[0], sizes[1], used, cap, cap, cap]).astype(jnp.int32)
    slots, places = ring_places(dp_count)
    buckets_t = buckets.T
    table = position_table.T
    row = lambda vector: vector.reshape(1, -1)
    piece_rows = (CAPS[0] * BLOCK, (CAPS[1] - CAPS[0]) * BLOCK, rows - CAPS[1] * BLOCK)
    pieces = lambda columns: [("a", shape_of((count, columns), bf16)) for count in piece_rows]
    vmem = pltpu.VMEM
    dma = pltpu.SemaphoreType.DMA

    w_out_got = swap_tensor(w_out)
    packed_x, query3, key3, value3, key_t, probs_t, *attended = run(
        attention_forward,
        "svvvvvvvv",
        [
            ("v", shape_of((rows, width), bf16)),
            ("v", shape_of((heads // 2, rows, 128), bf16)),
            ("v", shape_of((heads // 2, rows, 128), bf16)),
            ("v", shape_of((heads // 2, rows, 128), bf16)),
            ("v", shape_of((local, rows), bf16)),
            ("v", shape_of((heads, rows, seq_len), bf16)),
            *pieces(local),
        ],
        [
            vmem((heads, seq_len, seq_len), f32),
            vmem((local, rows), bf16),
            vmem((local, rows), f32),
            vmem((rows, local), bf16),
            dma((3,)),
        ],
        "attention_forward",
        16,
    )(meta, x, w_query, row(b_query), w_key, w_value, row(b_value), buckets_t, table)
    attended_got = exchange(attended, level)

    normed1, inverse1, hidden_low, activated, slope, *unit_part = run(
        feed_forward,
        "svaaaaaavvvvvvvv",
        [
            ("v", shape_of((rows, width), f32)),
            ("v", shape_of((rows, 128), f32)),
            ("v", shape_of((rows, width), bf16)),
            ("v", shape_of((rows, units), bf16)),
            ("v", shape_of((rows, units), bf16)),
            *pieces(width),
        ],
        [vmem((rows, local), bf16), vmem((rows, local), bf16), vmem((rows, width), bf16), dma((2, 3))],
        "feed_forward",
        8,
    )(
        meta, x, *attended, *attended_got, w_out, w_out_got, row(b_out), row(norm1_gain), row(norm1_shift),
        w_up, row(b_up), w_down,
    )
    unit_got = exchange(unit_part, level)

    layer_output, grad_y2, grad_ffn, grad_upper, sums2, sums_up, *hidden_part = run(
        second_norm,
        "svaaaaaavvvvvvvvv",
        [
            ("v", shape_of((micro, seq_len, width), bf16)),
            ("v", shape_of((rows, width), f32)),
            ("v", shape_of((rows, width), bf16)),
            ("v", shape_of((rows, units), bf16)),
            ("v", shape_of((8, width), f32)),
            ("v", shape_of((1, units), f32)),
            *pieces(width),
        ],
        [vmem((rows, width), bf16), vmem((rows, width), bf16), vmem((rows, width), bf16), dma((2, 3))],
        "second_norm",
        12,
    )(
        meta, grad_out, *unit_part, *unit_got, normed1, row(norm1_gain), row(norm1_shift), row(b_down),
        row(norm2_gain), row(norm2_shift), w_down, w_up, slope,
    )
    stacked_ffn = 2 * units
    ffn_parts = run(
        ffn_weights,
        "ssvvvv",
        [("v", shape_of((chips, stacked_ffn // (2 * chips), width), bf16))] * 2,
        [vmem((stacked_ffn, width), f32)],
        "ffn_weights",
        14,
    )(meta, slots, activated, grad_ffn, hidden_low, grad_upper)
    ffn_parts = fold(ffn_parts, 0, dp_count, 8, "ffn_fold")
    hidden_got = exchange_within(hidden_part, after(level, ffn_parts[0]))
    ffn_parts = fold(later(ffn_parts, hidden_got[0]), 1, dp_count, 8, "ffn_fold")

    grad_y1, grad_branch, grad_qkv, grad_scores_t, sums1, sums_qv, input_part = run(
        attention_backward,
        "saaaaaavvvvvvvvvvvvv",
        [
            ("v", shape_of((rows, width), f32)),
            ("v", shape_of((rows, width), bf16)),
            ("v", shape_of((rows, 3 * local), bf16)),
            ("v", shape_of((heads, rows, seq_len), bf16)),
            ("v", shape_of((8, width), f32)),
            ("v", shape_of((8, local), f32)),
            ("v", shape_of((rows, width), bf16)),
        ],
        [
            vmem((rows, width), bf16),
            vmem((rows, width), bf16),
            vmem((heads // 2, rows, 128), bf16),
            vmem((local, rows), f32),
            vmem((heads // 2, rows, 128), f32),
            vmem((heads // 2, rows, 128), f32),
            dma((2, 3)),
        ],
        "attention_backward",
        26,
    )(
        after(meta, ffn_parts[0]), *hidden_part, *hidden_got, grad_y2, normed1, inverse1, row(norm1_gain), w_out, w_query, w_key, w_value,
        query3, key3, value3, key_t, probs_t,
    )
    input_got = swap_tensor(input_part)
    ffn_parts = fold(ffn_parts, 2, dp_count, 8, "ffn_fold")

    stacked_attention = 3 * width + width * local // local
    attention_parts = run(
        attention_weights,
        "ssvvaaav",
        [("v", shape_of((chips, stacked_attention // (2 * chips), local), bf16))] * 2,
        [vmem((stacked_attention, local), f32), vmem((rows, local), bf16), dma((3,))],
        "attention_weights",
        9,
    )(after(meta, ffn_parts[0]), slots, packed_x, grad_qkv, *attended, grad_branch)

    table_sums = []

    def add_table(earlier):
        part = len(table_sums)
        table_sums.extend(
            run(
                functools.partial(table_histogram, part),
                "svv",
                [("v", shape_of((8 * heads, 32), f32))],
                [vmem((32, 16 * seq_len), bf16), vmem((8 * heads, 16 * seq_len), bf16)],
                f"table_histogram{part}",
                10,
            )(after(meta, *earlier), grad_scores_t, buckets_t)
        )

    stages = len(fold_bits(chips)) + 1
    for stage in range(3, stages):
        ffn_parts = fold(ffn_parts, stage, dp_count, 8, "ffn_fold")
    ffn_own = ffn_parts[0]
    for stage in range(stages):
        attention_parts = fold(later(attention_parts, *table_sums[-1:]), stage, dp_count, 4, "attention_fold")
        if stage == 0:
            add_table(attention_parts)
        if stage == 1:
            ffn_own = after(ffn_own, attention_parts[0])
        if len(table_sums) < TABLE_PARTS - 2:
            add_table([*attention_parts, table_sums[-1]])
    attention_own = attention_parts[0][0]
    for unused in range(TABLE_PARTS - len(table_sums)):
        add_table([attention_own, table_sums[-1]])
    ffn_pieces = gather_chunks(ffn_own[0], dp_count)
    (grad_w_up, grad_w_down), tokens = unpack_all(
        ffn_pieces, places, ffn_targets, [shape_of((width, units), f32), shape_of((units, width), f32)], "unpack_ffn"
    )
    fillers = {1: table_sums[-2], 2: table_sums[-1]}
    for token, eighths in zip(tokens, (3, 4, 6)):
        fillers[eighths * chips // 8] = token
    attention_pieces = gather_chunks(attention_own, dp_count, fillers)
    (grad_w_query, grad_w_key, grad_w_value, grad_w_out), unused = unpack_all(
        attention_pieces,
        places,
        attention_targets,
        [shape_of((width, local), f32)] * 3 + [shape_of((local, width), f32)],
        "unpack_attention",
        tokens,
    )

    (grad_inputs,) = run(
        input_gradient,
        "svvv",
        [("v", shape_of((micro, seq_len, width), f32))],
        [],
        "input_gradient",
        12,
    )(meta, grad_y1, input_part, input_got)

    table_rows = 8 * heads
    vector_rows = (6 * width + units + 2 * local) // 128
    small_rows = -(-vector_rows // 8) * 8 + table_rows
    (small,) = run(
        pack_small,
        "v" * (4 + TABLE_PARTS),
        [("v", shape_of((small_rows, 128), f32))],
        [],
        "pack_small",
        4,
    )(sums2, sums_up, sums1, sums_qv, *table_sums)
    small = sum_small(small, dp_count)
    table_grad = small[small_rows - table_rows :, :32].reshape(heads, 8, 32).transpose(2, 1, 0)
    small = small[:vector_rows].reshape(-1)
    cuts = []
    start = 0
    for count in (width, width, width, units, width, width, width, local, local):
        cuts.append(small[start : start + count])
        start += count
    grad_gain2, grad_shift2, grad_b_down, grad_b_up, grad_gain1, grad_shift1, grad_b_out, grad_b_query, grad_b_value = cuts
    return (
        layer_output.reshape(inputs.shape),
        grad_inputs.reshape(inputs.shape),
        grad_w_query,
        grad_b_query,
        grad_w_key,
        grad_w_value,
        grad_b_value,
        grad_w_out,
        grad_b_out,
        grad_gain1,
        grad_shift1,
        grad_w_up,
        grad_b_up,
        grad_w_down,
        grad_b_down,
        grad_gain2,
        grad_shift2,
        table_grad.reshape(bucket_count, heads),
    )


def solution(mesh):
    placed = (
        P(None, "dp", None, None),
        P(None, "dp"),
        P(),
        P(None, "tensor"),
        P("tensor"),
        P(None, "tensor"),
        P(None, "tensor"),
        P("tensor"),
        P("tensor", None),
        P(),
        P(),
        P(),
        P(None, "tensor"),
        P("tensor"),
        P("tensor", None),
        P(),
        P(),
        P(),
        P(None, "tensor"),
        P(None, "dp", None, None),
    )
    dp_count = mesh.shape["dp"]
    return jax.shard_map(
        lambda *arrays: per_device(dp_count, *arrays),
        mesh=mesh,
        in_specs=placed,
        out_specs=(
            P(None, "dp", None, None),
            P(None, "dp", None, None),
            P(None, "tensor"),
            P("tensor"),
            P(None, "tensor"),
            P(None, "tensor"),
            P("tensor"),
            P("tensor", None),
            P(),
            P(),
            P(),
            P(None, "tensor"),
            P("tensor"),
            P("tensor", None),
            P(),
            P(),
            P(),
            P(None, "tensor"),
        ),
        check_vma=False,
    )
```

```python
import functools

import jax
import jax.numpy as jnp
from jax import lax
from jax.experimental import pallas as pl
from jax.experimental.pallas import tpu as pltpu
from jax.sharding import PartitionSpec as P

epsilon = 1e-05
masked_value = -1e30
inv_root_two = 0.7071067811865476
inv_root_tau = 0.3989422804014327

BLOCK = 128
CAPS = (2, 5, 8)
TABLE_PARTS = 6
UNPACK_PARTS = 4
bf16 = jnp.bfloat16
f32 = jnp.float32
shape_of = jax.ShapeDtypeStruct

in_vmem = pl.BlockSpec(memory_space=pltpu.VMEM)
in_smem = pl.BlockSpec(memory_space=pltpu.SMEM)
in_any = pl.BlockSpec(memory_space=pl.ANY)
in_hbm = pl.BlockSpec(memory_space=pltpu.HBM)


def rows_at(block, count=1):
    return pl.ds(pl.multiple_of(block * BLOCK, BLOCK), count * BLOCK)


def dot_nn(left, right):
    return lax.dot_general(left, right, (((1,), (0,)), ((), ())), preferred_element_type=f32)


def dot_nt(left, right):
    return lax.dot_general(left, right, (((1,), (1,)), ((), ())), preferred_element_type=f32)


def dot_tn(left, right):
    return lax.dot_general(left, right, (((0,), (0,)), ((), ())), preferred_element_type=f32)


def place_of(meta, block):
    second = (block >= meta[0]).astype(jnp.int32)
    return second, pl.multiple_of((block - second * meta[0]) * BLOCK, BLOCK)


def live_rows(meta, second, first_row):
    rows = lax.broadcasted_iota(jnp.int32, (BLOCK, 1), 0) + first_row
    return rows < meta[2 + second]


def zero_tail(meta, ref):
    def clear(block, unused):
        ref[rows_at(block), :] = jnp.zeros((BLOCK, ref.shape[1]), ref.dtype)
        return unused

    lax.fori_loop(meta[4], meta[5], clear, 0)


def piece_copies(meta, pieces, whole, sems, to_pieces):
    start = 0
    made = []
    for index, piece in enumerate(pieces):
        rows = piece.shape[0]
        part = whole.at[pl.ds(start, rows), :]
        pair = (part, piece) if to_pieces else (piece, part)
        made.append((start // BLOCK, pltpu.make_async_copy(pair[0], pair[1], sems.at[index])))
        start += rows
    return made


def start_copies(meta, made):
    for first, copy in made:
        @pl.when(meta[5] > first)
        def _():
            copy.start()


def wait_copies(meta, made):
    for first, copy in made:
        @pl.when(meta[5] > first)
        def _():
            copy.wait()


def over_blocks(first, last, makers, act):
    def one(block, unused):
        for maker in makers:
            act(maker(block))
        return unused

    lax.fori_loop(first, last, one, 0)


def start(copy):
    copy.start()


def wait(copy):
    copy.wait()


def rows_copy(source, target, sems):
    return lambda block: pltpu.make_async_copy(source.at[rows_at(block), :], target.at[rows_at(block), :], sems.at[block])


def pairs_copy(source, target, sems):
    return lambda block: pltpu.make_async_copy(
        source.at[:, rows_at(block), :], target.at[:, rows_at(block), :], sems.at[block]
    )


def lanes_copy(source, target, sems):
    return lambda block: pltpu.make_async_copy(source.at[:, rows_at(block)], target.at[:, rows_at(block)], sems.at[block])


def packing_copy(meta, source, target, sems):
    def maker(block):
        second, first_row = place_of(meta, block)
        return pltpu.make_async_copy(
            source.at[second, pl.ds(first_row, BLOCK), :], target.at[rows_at(block), :], sems.at[block]
        )

    return maker


def probs_copy(source, target, sems, second, head, offset, blocks):
    spot = rows_at(offset, blocks)
    lanes = pl.ds(0, blocks * BLOCK)
    return pltpu.make_async_copy(
        source.at[head, spot, lanes], target.at[head, spot, lanes], sems.at[second, head]
    )


def over_probs(meta, source, target, sems, act):
    def one_sequence(second, unused):
        def sized(blocks):
            def one_head(head, unused):
                act(probs_copy(source, target, sems, second, head, second * meta[0], blocks))
                return unused

            lax.fori_loop(0, source.shape[0], one_head, 0)

        by_length(meta, second, sized)
        return unused

    lax.fori_loop(0, 2, one_sequence, 0)


def by_length(meta, second, body):
    for blocks in (1, 2, 4):
        @pl.when(meta[second] == blocks)
        def _():
            body(blocks)


def by_cap(meta, body):
    for blocks in CAPS:
        @pl.when(meta[5] == blocks)
        def _():
            body(blocks * BLOCK)


def norm_forward(rows, gain, shift):
    centre = rows - jnp.mean(rows, axis=-1, keepdims=True)
    inverse = lax.rsqrt(jnp.mean(centre * centre, axis=-1, keepdims=True) + epsilon)
    normed = centre * inverse
    return normed, normed * gain + shift, inverse


def norm_back(grad_rows, normed, inverse, gain):
    scaled = grad_rows * gain
    first_mean = jnp.mean(scaled, axis=-1, keepdims=True)
    second_mean = jnp.mean(scaled * normed, axis=-1, keepdims=True)
    return inverse * (scaled - first_mean - normed * second_mean)


def attention_forward(
    meta, x, w_query_in, b_query, w_key_in, w_value_in, b_value, buckets, table,
    query_out, value_out, key_t_out, probs_out, piece0, piece1, piece2,
    packed_x, w_query, w_key, w_value, query3, key3, value3, key_t, probs_t,
    bias, value_t, attended_t, attended, sems, in_sems, weight_sems, out_sems, probs_sems,
):
    weights = [
        pltpu.make_async_copy(source, target, weight_sems.at[index])
        for index, (source, target) in enumerate(((w_query_in, w_query), (w_key_in, w_key), (w_value_in, w_value)))
    ]
    for copy in weights:
        copy.start()
    x_copy = packing_copy(meta, x, packed_x, in_sems)
    over_blocks(0, meta[4], [x_copy], start)
    outward = [
        pairs_copy(query3, query_out, out_sems.at[0]),
        pairs_copy(value3, value_out, out_sems.at[1]),
        lanes_copy(key_t, key_t_out, out_sems.at[2]),
    ]
    heads = probs_t.shape[0]
    pairs = heads // 2
    scale = 0.125
    seq_len = buckets.shape[1]
    columns = seq_len // BLOCK

    def bias_rows(group, unused):
        rows = pl.ds(pl.multiple_of(group * 8, 8), 8)
        for column in range(columns):
            lanes = slice(column * BLOCK, (column + 1) * BLOCK)
            bucket = buckets[rows, lanes]
            low = bucket & 127
            upper = bucket >= 128
            for head in range(heads):
                first = jnp.broadcast_to(table[head : head + 1, :128], (8, 128))
                second = jnp.broadcast_to(table[head : head + 1, 128:], (8, 128))
                bias[head, rows, lanes] = jnp.where(
                    upper,
                    jnp.take_along_axis(second, low, axis=1, mode="promise_in_bounds"),
                    jnp.take_along_axis(first, low, axis=1, mode="promise_in_bounds"),
                )
        return unused

    lax.fori_loop(0, jnp.maximum(meta[0], meta[1]) * (BLOCK // 8), bias_rows, 0)

    for copy in weights:
        copy.wait()

    def project(block, unused):
        rows = rows_at(block)
        x_copy(block).wait()
        part = packed_x[rows, :]
        query = ((dot_nn(part, w_query[...]) + b_query[...]).astype(bf16).astype(f32) * scale).astype(bf16)
        key = dot_nn(part, w_key[...])
        value = dot_nn(part, w_value[...]) + b_value[...]
        key_t[:, rows] = key.T.astype(bf16)
        value_t[:, rows] = value.T.astype(bf16)
        key = key.astype(bf16)
        value = value.astype(bf16)
        for pair in range(pairs):
            lanes = slice(pair * 128, (pair + 1) * 128)
            query3[pair, rows, :] = query[:, lanes]
            key3[pair, rows, :] = key[:, lanes]
            value3[pair, rows, :] = value[:, lanes]
        for maker in outward:
            maker(block).start()
        return unused

    lax.fori_loop(0, meta[4], project, 0)

    def one_sequence(second, unused):
        offset = second * meta[0]
        length = meta[2 + second]

        def sized(blocks):
            count = blocks * BLOCK
            wide = min(count, 256)

            def one_head(head, unused):
                pair = head // 2
                lane = lax.broadcasted_iota(jnp.int32, (count, 128), 1)
                mine = (lane >= 64) == (head % 2 == 1)
                keys = jnp.where(mine, key3[pair, rows_at(offset, blocks), :], jnp.zeros((), bf16))
                values = value_t[pl.ds(pl.multiple_of(head * 64, 64), 64), rows_at(offset, blocks)]
                live = lax.broadcasted_iota(jnp.int32, (count, wide), 0) < length
                for column in range(count // wide):
                    lanes = slice(column * wide, (column + 1) * wide)
                    places = rows_at(offset + column * (wide // BLOCK), wide // BLOCK)
                    scores = dot_nt(keys, query3[pair, places, :]) + bias[head, :count, lanes]
                    scores = jnp.where(live, scores, masked_value)
                    top = jnp.max(scores, axis=0, keepdims=True)
                    powers = jnp.exp(scores - top)
                    total = jnp.sum(powers, axis=0, keepdims=True)
                    probs = (powers * (1.0 / total)).astype(bf16)
                    probs_t[head, rows_at(offset, blocks), lanes] = probs
                    attended_t[pl.ds(pl.multiple_of(head * 64, 64), 64), places] = dot_nn(values, probs)
                probs_copy(probs_t, probs_out, probs_sems, second, head, offset, blocks).start()
                return unused

            lax.fori_loop(0, heads, one_head, 0)

        by_length(meta, second, sized)
        return unused

    lax.fori_loop(0, 2, one_sequence, 0)

    def turn(block, unused):
        attended[rows_at(block), :] = attended_t[:, rows_at(block)].T.astype(bf16)
        return unused

    lax.fori_loop(0, meta[4], turn, 0)
    zero_tail(meta, attended)
    made = piece_copies(meta, (piece0, piece1, piece2), attended, sems, True)
    start_copies(meta, made)
    over_blocks(0, meta[4], outward, wait)
    over_probs(meta, probs_t, probs_out, probs_sems, wait)
    wait_copies(meta, made)


def feed_forward(
    meta, x, own0, own1, own2, got0, got1, got2, w_out_own_in, w_out_got_in, b_out, gain, shift,
    w_up_in, b_up, w_down_in,
    normed1, inverse_out, hidden_out, activated_out, slope_out, piece0, piece1, piece2,
    own, got, part, packed_x, w_out_own, w_out_got, w_up, w_down, inverse1, hidden_low, activated, slope,
    sems, in_sems, weight_sems, out_sems,
):
    own_copies = piece_copies(meta, (own0, own1, own2), own, sems.at[0], False)
    got_copies = piece_copies(meta, (got0, got1, got2), got, sems.at[1], False)
    start_copies(meta, own_copies)
    start_copies(meta, got_copies)
    sources = (w_out_own_in, w_out_got_in, w_up_in, w_down_in)
    weights = [
        pltpu.make_async_copy(source, target, weight_sems.at[index])
        for index, (source, target) in enumerate(zip(sources, (w_out_own, w_out_got, w_up, w_down)))
    ]
    x_copy = packing_copy(meta, x, packed_x, in_sems)
    weights[0].start()
    weights[1].start()
    over_blocks(0, meta[4], [x_copy], start)
    weights[2].start()
    weights[3].start()
    inverse_copy = rows_copy(inverse1, inverse_out, out_sems.at[0])
    hidden_copy = rows_copy(hidden_low, hidden_out, out_sems.at[1])
    activated_copy = rows_copy(activated, activated_out, out_sems.at[2])
    slope_copy = rows_copy(slope, slope_out, out_sems.at[3])
    wait_copies(meta, own_copies)
    wait_copies(meta, got_copies)
    weights[0].wait()
    weights[1].wait()
    width = w_up.shape[1]

    def first_norm(block, unused):
        rows = rows_at(block)
        head_own = dot_nn(own[rows, :], w_out_own[...]).astype(bf16).astype(f32)
        head_got = dot_nn(got[rows, :], w_out_got[...]).astype(bf16).astype(f32)
        branch = (head_own + head_got) + b_out[...]
        x_copy(block).wait()
        base = packed_x[rows, :].astype(f32) + branch
        normed, hidden, inverse = norm_forward(base, gain[...], shift[...])
        normed1[rows, :] = normed
        inverse1[rows, :] = jnp.broadcast_to(inverse, (BLOCK, 128))
        hidden_low[rows, :] = hidden.astype(bf16)
        inverse_copy(block).start()
        hidden_copy(block).start()
        return unused

    lax.fori_loop(0, meta[4], first_norm, 0)
    weights[2].wait()
    weights[3].wait()

    def one_block(block, unused):
        rows = rows_at(block)
        low = hidden_low[rows, :]
        for column in range(width // 512):
            lanes = slice(column * 512, (column + 1) * 512)
            upper = dot_nn(low, w_up[:, lanes]) + b_up[:, lanes]
            normal = 0.5 * (1.0 + lax.erf(upper * inv_root_two))
            activated[rows, lanes] = (upper * normal).astype(bf16)
            slope[rows, lanes] = (
                normal + upper * inv_root_tau * jnp.exp(-0.5 * upper * upper)
            ).astype(bf16)
        activated_copy(block).start()
        slope_copy(block).start()
        part[rows, :] = dot_nn(activated[rows, :], w_down[...]).astype(bf16)
        return unused

    lax.fori_loop(0, meta[4], one_block, 0)
    zero_tail(meta, part)
    made = piece_copies(meta, (piece0, piece1, piece2), part, sems.at[0], True)
    start_copies(meta, made)
    zero_tail(meta, activated)
    zero_tail(meta, hidden_low)
    over_blocks(meta[4], meta[5], [activated_copy, hidden_copy], start)
    over_blocks(0, meta[5], [activated_copy, hidden_copy], wait)
    over_blocks(0, meta[4], [inverse_copy, slope_copy], wait)
    wait_copies(meta, made)


def second_norm(
    meta, cotangent, own0, own1, own2, got0, got1, got2, normed1, gain1, shift1, b_down, gain2, shift2,
    w_down_in, w_up_in, slope_in,
    layer_out, grad_y2_out, grad_ffn, grad_upper, sums, sums_up, piece0, piece1, piece2,
    own, got, part, packed_grad, w_down, w_up, slope, layer_output, grad_y2,
    sems, in_sems, weight_sems, out_sems, layer_sem,
):
    own_copies = piece_copies(meta, (own0, own1, own2), own, sems.at[0], False)
    got_copies = piece_copies(meta, (got0, got1, got2), got, sems.at[1], False)
    start_copies(meta, own_copies)
    start_copies(meta, got_copies)
    weights = [
        pltpu.make_async_copy(source, target, weight_sems.at[index])
        for index, (source, target) in enumerate(((w_down_in, w_down), (w_up_in, w_up)))
    ]
    grad_copy = packing_copy(meta, cotangent, packed_grad, in_sems.at[0])
    slope_copy = rows_copy(slope_in, slope, in_sems.at[1])
    y2_copy = rows_copy(grad_y2, grad_y2_out, out_sems)
    over_blocks(0, meta[4], [grad_copy], start)
    weights[0].start()
    over_blocks(0, meta[4], [slope_copy], start)
    weights[1].start()
    sums[...] = jnp.zeros(sums.shape, f32)
    sums_up[...] = jnp.zeros(sums_up.shape, f32)
    layer_output[...] = jnp.zeros(layer_output.shape, bf16)
    wait_copies(meta, own_copies)
    wait_copies(meta, got_copies)
    width = w_up.shape[1]

    def norm_block(block, unused):
        second, first_row = place_of(meta, block)
        rows = rows_at(block)
        spot = pl.ds(first_row, BLOCK)
        live = live_rows(meta, second, first_row)
        ffn_out = (own[rows, :].astype(f32) + got[rows, :].astype(f32)) + b_down[...]
        hidden = normed1[rows, :] * gain1[...] + shift1[...]
        normed, result, inverse = norm_forward(hidden + ffn_out, gain2[...], shift2[...])
        layer_output[second, spot, :] = jnp.where(live, result, 0.0).astype(bf16)
        grad_copy(block).wait()
        grad_result = jnp.where(live, packed_grad[rows, :].astype(f32), 0.0)
        sums[0:1, :] += jnp.sum(grad_result * normed, axis=0, keepdims=True)
        sums[1:2, :] += jnp.sum(grad_result, axis=0, keepdims=True)
        grad = norm_back(grad_result, normed, inverse, gain2[...])
        grad_y2[rows, :] = grad
        y2_copy(block).start()
        low = grad.astype(bf16)
        grad_ffn[rows, :] = low
        sums[2:3, :] += jnp.sum(low.astype(f32), axis=0, keepdims=True)
        return unused

    lax.fori_loop(0, meta[4], norm_block, 0)
    layer_copy = pltpu.make_async_copy(layer_output, layer_out, layer_sem.at[0])
    layer_copy.start()
    for copy in weights:
        copy.wait()

    def one_block(block, unused):
        rows = rows_at(block)
        low = grad_ffn[rows, :]
        slope_copy(block).wait()
        for column in range(width // 512):
            lanes = slice(column * 512, (column + 1) * 512)
            back = dot_nt(low, w_down[lanes, :]) * slope[rows, lanes].astype(f32)
            back = back.astype(bf16)
            grad_upper[rows, lanes] = back
            sums_up[:, lanes] += jnp.sum(back.astype(f32), axis=0, keepdims=True)
        part[rows, :] = dot_nt(grad_upper[rows, :], w_up[...]).astype(bf16)
        return unused

    lax.fori_loop(0, meta[4], one_block, 0)
    zero_tail(meta, part)
    made = piece_copies(meta, (piece0, piece1, piece2), part, sems.at[0], True)
    start_copies(meta, made)
    zero_tail(meta, grad_ffn)
    zero_tail(meta, grad_upper)
    over_blocks(0, meta[4], [y2_copy], wait)
    layer_copy.wait()
    wait_copies(meta, made)


def ffn_weights(meta, slots, activated, grad_ffn, hidden_low, grad_upper, keep, give, stacked):
    width = grad_ffn.shape[1]
    units = activated.shape[1]

    def sized(count):
        def down(tile, unused):
            lanes = pl.ds(pl.multiple_of(tile * 256, 256), 256)
            stacked[lanes, :] = dot_tn(activated[:count, lanes], grad_ffn[:count, :])
            return unused

        lax.fori_loop(0, units // 256, down, 0)

        def up(tile, unused):
            lanes = pl.ds(pl.multiple_of(tile * 256, 256), 256)
            product = dot_tn(hidden_low[:count, lanes], grad_upper[:count, :])
            for half in range(units // width):
                spot = pl.ds(pl.multiple_of(units + half * width + tile * 256, 256), 256)
                stacked[spot, :] = product[:, half * width : (half + 1) * width]
            return unused

        lax.fori_loop(0, width // 256, up, 0)

    by_cap(meta, sized)
    scatter_chunks(slots, keep, give, stacked)


def scatter_chunks(slots, keep, give, stacked):
    chips, rows, unused = keep.shape

    def move(index, unused):
        for first, target in ((0, keep), (chips, give)):
            spot = pl.ds(pl.multiple_of(slots[first + index] * rows, 8), rows)
            target[index] = stacked[spot, :].astype(bf16)
        return unused

    lax.fori_loop(0, chips, move, 0)


def add_halves(keep, got, *outs):
    count = outs[0].shape[0]
    for index in range(keep.shape[0]):
        total = keep[index].astype(f32) + got[index].astype(f32)
        outs[index // count][index % count] = total.astype(bf16)


def attention_backward(
    meta, own0, own1, own2, got0, got1, got2, grad_y2_in, normed1, inverse_in, gain1,
    w_out_in, w_query_in, w_key_in, w_value_in, query_in, value_in, key_t_in, probs_in,
    grad_y1, grad_branch, grad_qkv, grad_scores_out, sums, sums_qv, part,
    own, got, grad_attended, grad_query_t, grad_key, grad_value,
    grad_y2, inverse1, w_out, w_query, w_key, w_value, query3, value3, key_t, probs_t,
    sems, in_sems, weight_sems, probs_sems, scores_sems,
):
    own_copies = piece_copies(meta, (own0, own1, own2), own, sems.at[0], False)
    got_copies = piece_copies(meta, (got0, got1, got2), got, sems.at[1], False)
    start_copies(meta, own_copies)
    start_copies(meta, got_copies)
    sources = (w_out_in, w_query_in, w_key_in, w_value_in)
    weights = [
        pltpu.make_async_copy(source, target, weight_sems.at[index])
        for index, (source, target) in enumerate(zip(sources, (w_out, w_query, w_key, w_value)))
    ]
    weights[0].start()
    row_copies = [rows_copy(grad_y2_in, grad_y2, in_sems.at[0]), rows_copy(inverse_in, inverse1, in_sems.at[1])]
    over_blocks(0, meta[4], row_copies, start)
    inward = [
        pairs_copy(value_in, value3, in_sems.at[2]),
        lanes_copy(key_t_in, key_t, in_sems.at[3]),
        pairs_copy(query_in, query3, in_sems.at[4]),
    ]
    over_blocks(0, meta[4], inward, start)
    over_probs(meta, probs_in, probs_t, probs_sems, start)
    for copy in weights[1:]:
        copy.start()
    sums[...] = jnp.zeros(sums.shape, f32)
    sums_qv[...] = jnp.zeros(sums_qv.shape, f32)
    wait_copies(meta, own_copies)
    wait_copies(meta, got_copies)
    weights[0].wait()
    heads = probs_t.shape[0]
    pairs = heads // 2
    local = heads * 64
    scale = 0.125

    def first_norm(block, unused):
        rows = rows_at(block)
        for maker in row_copies:
            maker(block).wait()
        grad_hidden = (own[rows, :].astype(f32) + got[rows, :].astype(f32)) + grad_y2[rows, :]
        normed = normed1[rows, :]
        sums[0:1, :] += jnp.sum(grad_hidden * normed, axis=0, keepdims=True)
        sums[1:2, :] += jnp.sum(grad_hidden, axis=0, keepdims=True)
        grad = norm_back(grad_hidden, normed, inverse1[rows, 0:1], gain1[...])
        grad_y1[rows, :] = grad
        low = grad.astype(bf16)
        grad_branch[rows, :] = low
        sums[2:3, :] += jnp.sum(low.astype(f32), axis=0, keepdims=True)
        back = dot_nt(low, w_out[...]).astype(bf16)
        for pair in range(pairs):
            grad_attended[pair, rows, :] = back[:, pair * 128 : (pair + 1) * 128]
            grad_key[pair, rows, :] = jnp.zeros((BLOCK, 128), f32)
            grad_value[pair, rows, :] = jnp.zeros((BLOCK, 128), f32)
        return unused

    lax.fori_loop(0, meta[4], first_norm, 0)
    over_blocks(0, meta[4], inward, wait)

    def one_sequence(second, unused):
        offset = second * meta[0]

        def sized(blocks):
            count = blocks * BLOCK
            wide = min(count, 256)
            every = rows_at(offset, blocks)

            def one_head(head, unused):
                pair = head // 2
                lane = lax.broadcasted_iota(jnp.int32, (wide, 128), 1)
                mine = (lane >= 64) == (head % 2 == 1)
                head_rows = pl.ds(pl.multiple_of(head * 64, 64), 64)
                values = value3[pair, every, :]
                keys = key_t[head_rows, every]
                probs_copy(probs_in, probs_t, probs_sems, second, head, offset, blocks).wait()
                for column in range(count // wide):
                    lanes = slice(column * wide, (column + 1) * wide)
                    places = rows_at(offset + column * (wide // BLOCK), wide // BLOCK)
                    zero = jnp.zeros((), bf16)
                    back = jnp.where(mine, grad_attended[pair, places, :], zero)
                    queries = jnp.where(mine, query3[pair, places, :], zero)
                    grad_probs = dot_nt(values, back)
                    probs_low = probs_t[head, every, lanes]
                    probs = probs_low.astype(f32)
                    mean = jnp.sum(probs * grad_probs, axis=0, keepdims=True)
                    grad_scores = (probs * (grad_probs - mean)).astype(bf16)
                    probs_t[head, every, lanes] = grad_scores
                    grad_value[pair, every, :] += dot_nn(probs_low, back)
                    grad_key[pair, every, :] += dot_nn(grad_scores, queries)
                    grad_query_t[head_rows, places] = dot_nn(keys, grad_scores)
                probs_copy(probs_t, grad_scores_out, scores_sems, second, head, offset, blocks).start()
                return unused

            lax.fori_loop(0, heads, one_head, 0)

        by_length(meta, second, sized)
        return unused

    lax.fori_loop(0, 2, one_sequence, 0)
    for copy in weights[1:]:
        copy.wait()

    def gather_grads(block, unused):
        rows = rows_at(block)
        query = (grad_query_t[:, rows].T * scale).astype(bf16)
        grad_qkv[rows, :local] = query
        for pair in range(pairs):
            lanes = slice(pair * 128, (pair + 1) * 128)
            grad_qkv[rows, local + pair * 128 : local + (pair + 1) * 128] = grad_key[pair, rows, :].astype(bf16)
            value = grad_value[pair, rows, :].astype(bf16)
            grad_qkv[rows, 2 * local + pair * 128 : 2 * local + (pair + 1) * 128] = value
            sums_qv[1:2, lanes] += jnp.sum(value.astype(f32), axis=0, keepdims=True)
        sums_qv[0:1, :] += jnp.sum(query.astype(f32), axis=0, keepdims=True)
        total = dot_nt(query, w_query[...])
        total = total + dot_nt(grad_qkv[rows, local : 2 * local], w_key[...])
        total = total + dot_nt(grad_qkv[rows, 2 * local :], w_value[...])
        part[rows, :] = total.astype(bf16)
        return unused

    lax.fori_loop(0, meta[4], gather_grads, 0)
    zero_tail(meta, grad_qkv)
    zero_tail(meta, grad_branch)
    over_probs(meta, probs_t, grad_scores_out, scores_sems, wait)


def attention_weights(
    meta, slots, x, grad_qkv, own0, own1, own2, grad_branch, keep, give, stacked, attended, packed_x, sems, in_sems
):
    x_copy = packing_copy(meta, x, packed_x, in_sems)
    over_blocks(0, meta[4], [x_copy], start)
    zero_tail(meta, packed_x)
    copies = piece_copies(meta, (own0, own1, own2), attended, sems, False)
    start_copies(meta, copies)
    width = packed_x.shape[1]
    local = attended.shape[1]
    wait_copies(meta, copies)
    over_blocks(0, meta[4], [x_copy], wait)

    def sized(count):
        def project(tile, unused):
            lanes = pl.ds(pl.multiple_of(tile * 256, 256), 256)
            product = dot_tn(packed_x[:count, lanes], grad_qkv[:count, :])
            for part in range(3):
                spot = pl.ds(pl.multiple_of(part * width + tile * 256, 256), 256)
                stacked[spot, :] = product[:, part * local : (part + 1) * local]
            return unused

        lax.fori_loop(0, width // 256, project, 0)
        product = dot_tn(attended[:count, :], grad_branch[:count, :])
        for half in range(width // local):
            first = 3 * width + half * local
            stacked[first : first + local, :] = product[:, half * local : (half + 1) * local]

    by_cap(meta, sized)
    scatter_chunks(slots, keep, give, stacked)


def table_histogram(part, meta, grad_scores_t, buckets, total, left, right):
    heads = grad_scores_t.shape[0]
    group = 16
    total[...] = jnp.zeros(total.shape, f32)

    def one_sequence(second, unused):
        offset = second * meta[0]

        def sized(blocks):
            count = blocks * BLOCK
            upper_digit = lax.broadcasted_iota(jnp.int32, (32, count), 0)
            lower_digit = lax.broadcasted_iota(jnp.int32, (8, count), 0)

            def one_group(index, unused):
                rows = pl.ds(pl.multiple_of(index * group, group), group)
                spots = pl.ds(pl.multiple_of(offset * BLOCK + index * group, group), group)
                bucket = buckets[rows, :count]
                upper = bucket >> 3
                lower = bucket & 7
                grads = [grad_scores_t[head, spots, :count].astype(f32) for head in range(heads)]
                for row in range(group):
                    lanes = slice(row * count, (row + 1) * count)
                    left[:, lanes] = jnp.where(upper_digit == upper[row : row + 1, :], 1.0, 0.0).astype(bf16)
                    chosen = lower_digit == lower[row : row + 1, :]
                    for head in range(0, heads, 2):
                        spread = jnp.concatenate(
                            [jnp.where(chosen, grads[head + odd][row : row + 1, :], 0.0) for odd in range(2)], axis=0
                        )
                        right[head * 8 : (head + 2) * 8, lanes] = spread.astype(bf16)
                total[...] += dot_nt(right[:, : group * count], left[:, : group * count])
                return unused

            groups = count // group
            lax.fori_loop(groups * part // TABLE_PARTS, groups * (part + 1) // TABLE_PARTS, one_group, 0)

        by_length(meta, second, sized)
        return unused

    lax.fori_loop(0, 2, one_sequence, 0)


def input_gradient(meta, grad_y1, own, got, out):
    out[...] = jnp.zeros(out.shape, f32)

    def one_block(block, unused):
        second, first_row = place_of(meta, block)
        rows = rows_at(block)
        live = live_rows(meta, second, first_row)
        total = (own[rows, :].astype(f32) + got[rows, :].astype(f32)) + grad_y1[rows, :]
        out[second, pl.ds(first_row, BLOCK), :] = jnp.where(live, total, 0.0)
        return unused

    lax.fori_loop(0, meta[4], one_block, 0)


def pack_small(sums2, sums_up, sums1, sums_qv, *refs):
    tables, out = refs[:-1], refs[-1]
    out[...] = jnp.zeros(out.shape, f32)
    row = 0
    for source, count in ((sums2, 3), (sums_up, 1), (sums1, 3), (sums_qv, 2)):
        for line in range(count):
            for column in range(source.shape[1] // 128):
                out[row : row + 1, :] = source[line : line + 1, column * 128 : (column + 1) * 128]
                row += 1
    height, wide = tables[0].shape
    first = out.shape[0] - height
    out[first:, :wide] = sum(table[...] for table in tables)


def unpack(first_place, count, targets_of, places, *refs):
    chunks, (wide, sems) = refs[:count], refs[-2:]
    outs, token = refs[-3 - targets_of.outs : -3], refs[-3]
    token[...] = jnp.zeros(token.shape, f32)
    rows = chunks[0].shape[0]
    copies = []
    for index, chunk in enumerate(chunks):
        wide[index] = chunk[...].astype(f32)
        first = places[first_place + index] * rows
        for low, high, target in targets_of(outs, rows):
            inside = (first >= low) & (first < high)
            copy = pltpu.make_async_copy(
                wide.at[index], target(pl.ds(pl.multiple_of(first - low, 8), rows)), sems.at[index]
            )
            copies.append((inside, copy))

            @pl.when(inside)
            def _():
                copy.start()

    for inside, copy in copies:
        @pl.when(inside)
        def _():
            copy.wait()


def ffn_targets(outs, rows):
    grad_up, grad_down = outs
    units, width = grad_down.shape
    found = [(0, units, lambda spot: grad_down.at[spot, :])]
    for half in range(units // width):
        lanes = pl.ds(half * width, width)
        low = units + half * width
        found.append((low, low + width, lambda spot, lanes=lanes: grad_up.at[spot, lanes]))
    return found


def attention_targets(outs, rows):
    width, local = outs[0].shape
    found = []
    for part in range(3):
        found.append((part * width, (part + 1) * width, lambda spot, part=part: outs[part].at[spot, :]))
    for half in range(width // local):
        lanes = pl.ds(half * local, local)
        low = 3 * width + half * local
        found.append((low, low + local, lambda spot, lanes=lanes: outs[3].at[spot, lanes]))
    return found


ffn_targets.outs = 2
attention_targets.outs = 4


spaces = {"s": in_smem, "v": in_vmem, "a": in_any, "h": in_hbm}


def run(kernel, specs, outs, scratch, name, room, aliases={}):
    params = pltpu.CompilerParams(vmem_limit_bytes=room * 1024 * 1024)

    def call(*args):
        return pl.pallas_call(
            kernel,
            in_specs=[spaces[kind] for kind in specs],
            out_specs=[spaces[kind] for kind, unused in outs],
            out_shape=[pltpu.HBM(shape.shape, shape.dtype) if kind == "h" else shape for kind, shape in outs],
            scratch_shapes=scratch,
            compiler_params=params,
            input_output_aliases=aliases,
            name=name,
        )(
            *[
                pltpu.with_memory_space_constraint(arg, pltpu.HBM) if kind == "h" else arg
                for kind, arg in zip(specs, args)
            ]
        )

    return call


def unpack_all(pieces, places, targets_of, shapes, name, earlier=()):
    chips = len(pieces) // 2
    ordered = [piece for pair in zip(pieces[:chips], pieces[chips:]) for piece in pair]
    ordered_places = jnp.stack([places[:chips], places[chips:]], axis=1).reshape(-1)
    made, tokens = [], []
    parts = min(UNPACK_PARTS, chips)
    for part in range(parts):
        first, last = 2 * (chips * part // parts), 2 * (chips * (part + 1) // parts)
        count = last - first
        rows, columns = ordered[0].shape
        *made, token = run(
            functools.partial(unpack, first, count, targets_of),
            "s" + "v" * count + "a" * (len(made) + len(earlier)),
            [("a", shape) for shape in shapes] + [("v", shape_of((8, 128), f32))],
            [pltpu.VMEM((count, rows, columns), f32), pltpu.SemaphoreType.DMA((count,))],
            f"{name}{part}",
            6,
            {1 + count + index: index for index in range(len(made))},
        )(ordered_places, *ordered[first:last], *made, *earlier)
        tokens.append(token)
    return made, tokens


def swap_tensor(value):
    return lax.ppermute(value, "tensor", ((0, 1), (1, 0)))


def exchange(pieces, level):
    got0 = swap_tensor(pieces[0])
    got1, got2 = lax.switch(
        level,
        (
            lambda one, two: (one, two),
            lambda one, two: (swap_tensor(one), two),
            lambda one, two: (swap_tensor(one), swap_tensor(two)),
        ),
        pieces[1],
        pieces[2],
    )
    return got0, got1, got2


def ring_pairs(dp_count):
    chips = dp_count // 2
    order = list(range(0, chips, 2)) + list(range(chips - 1, 0, -2))
    pairs = []
    for place, chip in enumerate(order):
        after = order[(place + 1) % chips]
        pairs.append((2 * chip, 2 * after))
        pairs.append((2 * after + 1, 2 * chip + 1))
    return tuple(pairs)


def exchange_within(pieces, level):
    return lax.switch(
        level,
        (
            lambda zero, one, two: (swap_tensor(zero), one, two),
            lambda zero, one, two: (swap_tensor(zero), swap_tensor(one), two),
            lambda zero, one, two: (swap_tensor(zero), swap_tensor(one), swap_tensor(two)),
        ),
        *pieces,
    )


def fold_bits(chips):
    bits = [1]
    bit = chips // 2
    while bit > 1:
        bits.append(bit)
        bit //= 2
    return bits


def ring_places(dp_count):
    chips = dp_count // 2
    index = lax.axis_index("dp")
    chip, core = index // 2, index % 2
    position = lambda at: jnp.where(at % 2 == 0, at // 2, chips - 1 - at // 2)
    steps = jnp.arange(chips, dtype=jnp.int32)
    mine, theirs = core * chips, (1 - core) * chips
    offsets = [
        sum(bit for step, bit in enumerate(fold_bits(chips)) if slot & (chips >> (step + 1))) for slot in range(chips)
    ]
    targets = position(chip ^ jnp.array(offsets, jnp.int32))
    turn = steps * (1 - 2 * core)
    own_chunks = mine + (position(chip) - turn) % chips
    other_chunks = theirs + (position(chip) + turn) % chips
    slots = jnp.concatenate([mine + targets, theirs + targets])
    return slots.astype(jnp.int32), jnp.concatenate([own_chunks, other_chunks]).astype(jnp.int32)


def siblings(dp_count):
    return tuple((i, i ^ 1) for i in range(dp_count))


def fold(parts, stage, dp_count, room, name):
    keep, give = parts
    if stage == 0:
        pairs = siblings(dp_count)
    else:
        distance = 2 * fold_bits(dp_count // 2)[stage - 1]
        pairs = tuple((i, i ^ distance) for i in range(dp_count))
    got = lax.ppermute(give, "dp", pairs)
    count = keep.shape[0]
    halves = [count // 2, count // 2] if count > 1 else [1]
    outs = [("v", shape_of((half, *keep.shape[1:]), bf16)) for half in halves]
    return run(add_halves, "vv", outs, [], f"{name}{stage}", room)(keep, got)


def gather_chunks(moving, dp_count, fillers={}):
    pairs = ring_pairs(dp_count)
    own = [moving]
    for step in range(dp_count // 2 - 1):
        if step in fillers:
            moving = after(moving, fillers[step])
        moving = lax.ppermute(moving, "dp", pairs)
        own.append(moving)
    return own + [lax.ppermute(piece, "dp", siblings(dp_count)) for piece in own]


def later(parts, *earlier):
    return after(parts[0], *earlier), parts[1]


def after(value, *earlier):
    return lax.optimization_barrier((value, earlier))[0]


def sum_small(value, dp_count):
    bit = 1
    while bit < dp_count:
        value = value + lax.ppermute(value, "dp", tuple((i, i ^ bit) for i in range(dp_count)))
        bit *= 2
    return value


def per_device(dp_count, *arrays):
    (
        inputs, lengths, buckets, w_query, b_query, w_key, w_value, b_value, w_out, b_out, norm1_gain, norm1_shift,
        w_up, b_up, w_down, b_down, norm2_gain, norm2_shift, position_table, cotangent,
    ) = arrays
    micro, seqs, seq_len, width = inputs.shape
    bucket_count, heads = position_table.shape
    local = w_query.shape[1]
    units = w_up.shape[1]
    chips = dp_count // 2
    rows = micro * seq_len
    x = inputs.reshape(micro, seq_len, width)
    grad_out = cotangent.reshape(micro, seq_len, width)
    sizes = lengths[:, 0]
    blocks = jnp.where(sizes <= BLOCK, 1, jnp.where(sizes <= 2 * BLOCK, 2, 4))
    used = blocks[0] + blocks[1]
    level = (used > CAPS[0]).astype(jnp.int32) + (used > CAPS[1]).astype(jnp.int32)
    cap = jnp.where(level == 0, CAPS[0], jnp.where(level == 1, CAPS[1], CAPS[2]))
    meta = jnp.stack([blocks[0], blocks[1], sizes[0], sizes[1], used, cap, cap, cap]).astype(jnp.int32)
    slots, places = ring_places(dp_count)
    buckets_t = buckets.T
    table = position_table.T
    row = lambda vector: vector.reshape(1, -1)
    piece_rows = (CAPS[0] * BLOCK, (CAPS[1] - CAPS[0]) * BLOCK, rows - CAPS[1] * BLOCK)
    pieces = lambda columns: [("a", shape_of((count, columns), bf16)) for count in piece_rows]
    vmem = pltpu.VMEM
    dma = pltpu.SemaphoreType.DMA

    w_out_got = swap_tensor(w_out)
    blocks_most = rows // BLOCK
    query3, value3, key_t, probs_t, *attended = run(
        attention_forward,
        "shhvhhvvv",
        [
            ("h", shape_of((heads // 2, rows, 128), bf16)),
            ("h", shape_of((heads // 2, rows, 128), bf16)),
            ("h", shape_of((local, rows), bf16)),
            ("h", shape_of((heads, rows, seq_len), bf16)),
            *pieces(local),
        ],
        [
            vmem((rows, width), bf16),
            *[vmem((width, local), bf16)] * 3,
            *[vmem((heads // 2, rows, 128), bf16)] * 3,
            vmem((local, rows), bf16),
            vmem((heads, rows, seq_len), bf16),
            vmem((heads, seq_len, seq_len), f32),
            vmem((local, rows), bf16),
            vmem((local, rows), f32),
            vmem((rows, local), bf16),
            dma((3,)),
            dma((blocks_most,)),
            dma((3,)),
            dma((3, blocks_most)),
            dma((2, heads)),
        ],
        "attention_forward",
        27,
    )(meta, x, w_query, row(b_query), w_key, w_value, row(b_value), buckets_t, table)
    attended_got = exchange(attended, level)

    normed1, inverse1, hidden_low, activated, slope, *unit_part = run(
        feed_forward,
        "shaaaaaahhvvvhvh",
        [
            ("v", shape_of((rows, width), f32)),
            ("h", shape_of((rows, 128), f32)),
            ("h", shape_of((rows, width), bf16)),
            ("h", shape_of((rows, units), bf16)),
            ("h", shape_of((rows, units), bf16)),
            *pieces(width),
        ],
        [
            vmem((rows, local), bf16),
            vmem((rows, local), bf16),
            vmem((rows, width), bf16),
            vmem((rows, width), bf16),
            vmem((local, width), bf16),
            vmem((local, width), bf16),
            vmem((width, units), bf16),
            vmem((units, width), bf16),
            vmem((rows, 128), f32),
            vmem((rows, width), bf16),
            vmem((rows, units), bf16),
            vmem((rows, units), bf16),
            dma((2, 3)),
            dma((blocks_most,)),
            dma((4,)),
            dma((4, blocks_most)),
        ],
        "feed_forward",
        26,
    )(
        meta, x, *attended, *attended_got, w_out, w_out_got, row(b_out), row(norm1_gain), row(norm1_shift),
        w_up, row(b_up), w_down,
    )
    unit_got = exchange(unit_part, level)

    layer_output, grad_y2, grad_ffn, grad_upper, sums2, sums_up, *hidden_part = run(
        second_norm,
        "shaaaaaavvvvvvhhh",
        [
            ("h", shape_of((micro, seq_len, width), bf16)),
            ("h", shape_of((rows, width), f32)),
            ("v", shape_of((rows, width), bf16)),
            ("v", shape_of((rows, units), bf16)),
            ("v", shape_of((8, width), f32)),
            ("v", shape_of((1, units), f32)),
            *pieces(width),
        ],
        [
            vmem((rows, width), bf16),
            vmem((rows, width), bf16),
            vmem((rows, width), bf16),
            vmem((rows, width), bf16),
            vmem((units, width), bf16),
            vmem((width, units), bf16),
            vmem((rows, units), bf16),
            vmem((micro, seq_len, width), bf16),
            vmem((rows, width), f32),
            dma((2, 3)),
            dma((2, blocks_most)),
            dma((2,)),
            dma((blocks_most,)),
            dma((1,)),
        ],
        "second_norm",
        26,
    )(
        meta, grad_out, *unit_part, *unit_got, normed1, row(norm1_gain), row(norm1_shift), row(b_down),
        row(norm2_gain), row(norm2_shift), w_down, w_up, slope,
    )
    stacked_ffn = 2 * units
    ffn_parts = run(
        ffn_weights,
        "ssvvvv",
        [("v", shape_of((chips, stacked_ffn // (2 * chips), width), bf16))] * 2,
        [vmem((stacked_ffn, width), f32)],
        "ffn_weights",
        14,
    )(meta, slots, activated, grad_ffn, hidden_low, grad_upper)
    hidden_got = exchange_within(hidden_part, after(level, ffn_parts[0]))
    ffn_parts = fold(later(ffn_parts, hidden_got[0]), 0, dp_count, 8, "ffn_fold")

    grad_y1, grad_branch, grad_qkv, grad_scores_t, sums1, sums_qv, input_part = run(
        attention_backward,
        "saaaaaahvhvhhhhhhhh",
        [
            ("v", shape_of((rows, width), f32)),
            ("v", shape_of((rows, width), bf16)),
            ("v", shape_of((rows, 3 * local), bf16)),
            ("h", shape_of((heads, rows, seq_len), bf16)),
            ("v", shape_of((8, width), f32)),
            ("v", shape_of((8, local), f32)),
            ("v", shape_of((rows, width), bf16)),
        ],
        [
            vmem((rows, width), bf16),
            vmem((rows, width), bf16),
            vmem((heads // 2, rows, 128), bf16),
            vmem((local, rows), f32),
            vmem((heads // 2, rows, 128), f32),
            vmem((heads // 2, rows, 128), f32),
            vmem((rows, width), f32),
            vmem((rows, 128), f32),
            vmem((local, width), bf16),
            *[vmem((width, local), bf16)] * 3,
            *[vmem((heads // 2, rows, 128), bf16)] * 2,
            vmem((local, rows), bf16),
            vmem((heads, rows, seq_len), bf16),
            dma((2, 3)),
            dma((5, blocks_most)),
            dma((4,)),
            dma((2, heads)),
            dma((2, heads)),
        ],
        "attention_backward",
        32,
    )(
        after(meta, ffn_parts[0]), *hidden_part, *hidden_got, grad_y2, normed1, inverse1, row(norm1_gain), w_out, w_query, w_key, w_value,
        query3, value3, key_t, probs_t,
    )
    input_got = swap_tensor(input_part)

    stacked_attention = 3 * width + width * local // local
    attention_parts = run(
        attention_weights,
        "sshvaaav",
        [("v", shape_of((chips, stacked_attention // (2 * chips), local), bf16))] * 2,
        [
            vmem((stacked_attention, local), f32),
            vmem((rows, local), bf16),
            vmem((rows, width), bf16),
            dma((3,)),
            dma((blocks_most,)),
        ],
        "attention_weights",
        11,
    )(meta, slots, x, grad_qkv, *attended, grad_branch)

    table_sums = []

    def add_table(earlier):
        part = len(table_sums)
        table_sums.extend(
            run(
                functools.partial(table_histogram, part),
                "svv",
                [("v", shape_of((8 * heads, 32), f32))],
                [vmem((32, 16 * seq_len), bf16), vmem((8 * heads, 16 * seq_len), bf16)],
                f"table_histogram{part}",
                10,
            )(after(meta, *earlier), grad_scores_t, buckets_t)
        )

    stages = len(fold_bits(chips)) + 1
    ffn_parts = fold(later(ffn_parts, attention_parts[0]), 1, dp_count, 8, "ffn_fold")
    attention_parts = later(attention_parts, ffn_parts[0])
    for stage in range(stages):
        attention_parts = fold(later(attention_parts, *table_sums[-1:]), stage, dp_count, 4, "attention_fold")
        if stage == 0:
            add_table(attention_parts)
        elif stage + 1 < stages:
            ffn_parts = fold(later(ffn_parts, attention_parts[0]), stage + 1, dp_count, 8, "ffn_fold")
        if len(table_sums) < TABLE_PARTS - 2:
            add_table([*attention_parts, table_sums[-1]])
    attention_own = attention_parts[0][0]
    for unused in range(TABLE_PARTS - len(table_sums)):
        add_table([attention_own, table_sums[-1]])
    ffn_pieces = gather_chunks(ffn_parts[0][0], dp_count, {1: attention_own})
    (grad_w_up, grad_w_down), tokens = unpack_all(
        ffn_pieces, places, ffn_targets, [shape_of((width, units), f32), shape_of((units, width), f32)], "unpack_ffn"
    )
    fillers = {1: table_sums[-2], 2: table_sums[-1]}
    for token, eighths in zip(tokens, (3, 4, 6)):
        fillers[eighths * chips // 8] = token
    attention_pieces = gather_chunks(attention_own, dp_count, fillers)
    (grad_w_query, grad_w_key, grad_w_value, grad_w_out), unused = unpack_all(
        attention_pieces,
        places,
        attention_targets,
        [shape_of((width, local), f32)] * 3 + [shape_of((local, width), f32)],
        "unpack_attention",
        tokens,
    )

    (grad_inputs,) = run(
        input_gradient,
        "svvv",
        [("v", shape_of((micro, seq_len, width), f32))],
        [],
        "input_gradient",
        12,
    )(meta, grad_y1, input_part, input_got)

    table_rows = 8 * heads
    vector_rows = (6 * width + units + 2 * local) // 128
    small_rows = -(-vector_rows // 8) * 8 + table_rows
    (small,) = run(
        pack_small,
        "v" * (4 + TABLE_PARTS),
        [("v", shape_of((small_rows, 128), f32))],
        [],
        "pack_small",
        4,
    )(sums2, sums_up, sums1, sums_qv, *table_sums)
    small = sum_small(small, dp_count)
    table_grad = small[small_rows - table_rows :, :32].reshape(heads, 8, 32).transpose(2, 1, 0)
    small = small[:vector_rows].reshape(-1)
    cuts = []
    start = 0
    for count in (width, width, width, units, width, width, width, local, local):
        cuts.append(small[start : start + count])
        start += count
    grad_gain2, grad_shift2, grad_b_down, grad_b_up, grad_gain1, grad_shift1, grad_b_out, grad_b_query, grad_b_value = cuts
    return (
        layer_output.reshape(inputs.shape),
        grad_inputs.reshape(inputs.shape),
        grad_w_query,
        grad_b_query,
        grad_w_key,
        grad_w_value,
        grad_b_value,
        grad_w_out,
        grad_b_out,
        grad_gain1,
        grad_shift1,
        grad_w_up,
        grad_b_up,
        grad_w_down,
        grad_b_down,
        grad_gain2,
        grad_shift2,
        table_grad.reshape(bucket_count, heads),
    )


def solution(mesh):
    placed = (
        P(None, "dp", None, None),
        P(None, "dp"),
        P(),
        P(None, "tensor"),
        P("tensor"),
        P(None, "tensor"),
        P(None, "tensor"),
        P("tensor"),
        P("tensor", None),
        P(),
        P(),
        P(),
        P(None, "tensor"),
        P("tensor"),
        P("tensor", None),
        P(),
        P(),
        P(),
        P(None, "tensor"),
        P(None, "dp", None, None),
    )
    dp_count = mesh.shape["dp"]
    return jax.shard_map(
        lambda *arrays: per_device(dp_count, *arrays),
        mesh=mesh,
        in_specs=placed,
        out_specs=(
            P(None, "dp", None, None),
            P(None, "dp", None, None),
            P(None, "tensor"),
            P("tensor"),
            P(None, "tensor"),
            P(None, "tensor"),
            P("tensor"),
            P("tensor", None),
            P(),
            P(),
            P(),
            P(None, "tensor"),
            P("tensor"),
            P("tensor", None),
            P(),
            P(),
            P(),
            P(None, "tensor"),
        ),
        check_vma=False,
    )
```

```python
import functools

import jax
import jax.numpy as jnp
from jax import lax
from jax.experimental import pallas as pl
from jax.experimental.pallas import tpu as pltpu
from jax.sharding import PartitionSpec as P

epsilon = 1e-05
masked_value = -1e30
inv_root_two = 0.7071067811865476
inv_root_tau = 0.3989422804014327

BLOCK = 128
CAPS = (2, 5, 8)
TABLE_PARTS = 6
UNPACK_PARTS = 4
bf16 = jnp.bfloat16
f32 = jnp.float32
shape_of = jax.ShapeDtypeStruct

in_vmem = pl.BlockSpec(memory_space=pltpu.VMEM)
in_smem = pl.BlockSpec(memory_space=pltpu.SMEM)
in_any = pl.BlockSpec(memory_space=pl.ANY)
in_hbm = pl.BlockSpec(memory_space=pltpu.HBM)


def rows_at(block, count=1):
    return pl.ds(pl.multiple_of(block * BLOCK, BLOCK), count * BLOCK)


def dot_nn(left, right):
    return lax.dot_general(left, right, (((1,), (0,)), ((), ())), preferred_element_type=f32)


def dot_nt(left, right):
    return lax.dot_general(left, right, (((1,), (1,)), ((), ())), preferred_element_type=f32)


def dot_tn(left, right):
    return lax.dot_general(left, right, (((0,), (0,)), ((), ())), preferred_element_type=f32)


def place_of(meta, block):
    second = (block >= meta[0]).astype(jnp.int32)
    return second, pl.multiple_of((block - second * meta[0]) * BLOCK, BLOCK)


def live_rows(meta, second, first_row):
    rows = lax.broadcasted_iota(jnp.int32, (BLOCK, 1), 0) + first_row
    return rows < meta[2 + second]


def zero_tail(meta, ref):
    def clear(block, unused):
        ref[rows_at(block), :] = jnp.zeros((BLOCK, ref.shape[1]), ref.dtype)
        return unused

    lax.fori_loop(meta[4], meta[5], clear, 0)


def piece_copies(meta, pieces, whole, sems, to_pieces):
    start = 0
    made = []
    for index, piece in enumerate(pieces):
        rows = piece.shape[0]
        part = whole.at[pl.ds(start, rows), :]
        pair = (part, piece) if to_pieces else (piece, part)
        made.append((start // BLOCK, pltpu.make_async_copy(pair[0], pair[1], sems.at[index])))
        start += rows
    return made


def start_copies(meta, made):
    for first, copy in made:
        @pl.when(meta[5] > first)
        def _():
            copy.start()


def wait_copies(meta, made):
    for first, copy in made:
        @pl.when(meta[5] > first)
        def _():
            copy.wait()


def over_blocks(first, last, makers, act):
    def one(block, unused):
        for maker in makers:
            act(maker(block))
        return unused

    lax.fori_loop(first, last, one, 0)


def start(copy):
    copy.start()


def wait(copy):
    copy.wait()


def rows_copy(source, target, sems):
    return lambda block: pltpu.make_async_copy(source.at[rows_at(block), :], target.at[rows_at(block), :], sems.at[block])


def pairs_copy(source, target, sems):
    return lambda block: pltpu.make_async_copy(
        source.at[:, rows_at(block), :], target.at[:, rows_at(block), :], sems.at[block]
    )


def lanes_copy(source, target, sems):
    return lambda block: pltpu.make_async_copy(source.at[:, rows_at(block)], target.at[:, rows_at(block)], sems.at[block])


def packing_copy(meta, source, target, sems):
    def maker(block):
        second, first_row = place_of(meta, block)
        return pltpu.make_async_copy(
            source.at[second, pl.ds(first_row, BLOCK), :], target.at[rows_at(block), :], sems.at[block]
        )

    return maker


def probs_copy(source, target, sems, second, head, offset, blocks):
    spot = rows_at(offset, blocks)
    lanes = pl.ds(0, blocks * BLOCK)
    return pltpu.make_async_copy(
        source.at[head, spot, lanes], target.at[head, spot, lanes], sems.at[second, head]
    )


def over_probs(meta, source, target, sems, act):
    def one_sequence(second, unused):
        def sized(blocks):
            def one_head(head, unused):
                act(probs_copy(source, target, sems, second, head, second * meta[0], blocks))
                return unused

            lax.fori_loop(0, source.shape[0], one_head, 0)

        by_length(meta, second, sized)
        return unused

    lax.fori_loop(0, 2, one_sequence, 0)


def by_length(meta, second, body):
    for blocks in (1, 2, 4):
        @pl.when(meta[second] == blocks)
        def _():
            body(blocks)


def by_cap(meta, body):
    for blocks in CAPS:
        @pl.when(meta[5] == blocks)
        def _():
            body(blocks * BLOCK)


def norm_forward(rows, gain, shift):
    centre = rows - jnp.mean(rows, axis=-1, keepdims=True)
    inverse = lax.rsqrt(jnp.mean(centre * centre, axis=-1, keepdims=True) + epsilon)
    normed = centre * inverse
    return normed, normed * gain + shift, inverse


def norm_back(grad_rows, normed, inverse, gain):
    scaled = grad_rows * gain
    first_mean = jnp.mean(scaled, axis=-1, keepdims=True)
    second_mean = jnp.mean(scaled * normed, axis=-1, keepdims=True)
    return inverse * (scaled - first_mean - normed * second_mean)


def attention_forward(
    meta, x, w_query_in, b_query, w_key_in, w_value_in, b_value, buckets, table,
    query_out, value_out, key_t_out, probs_out, piece0, piece1, piece2,
    packed_x, w_query, w_key, w_value, query3, key3, value3, key_t, probs_t,
    bias, value_t, attended_t, attended, sems, in_sems, weight_sems, out_sems, probs_sems,
):
    weights = [
        pltpu.make_async_copy(source, target, weight_sems.at[index])
        for index, (source, target) in enumerate(((w_query_in, w_query), (w_key_in, w_key), (w_value_in, w_value)))
    ]
    for copy in weights:
        copy.start()
    x_copy = packing_copy(meta, x, packed_x, in_sems)
    over_blocks(0, meta[4], [x_copy], start)
    outward = [
        pairs_copy(query3, query_out, out_sems.at[0]),
        pairs_copy(value3, value_out, out_sems.at[1]),
        lanes_copy(key_t, key_t_out, out_sems.at[2]),
    ]
    heads = probs_t.shape[0]
    pairs = heads // 2
    scale = 0.125
    seq_len = buckets.shape[1]
    columns = seq_len // BLOCK

    def bias_rows(group, unused):
        rows = pl.ds(pl.multiple_of(group * 8, 8), 8)
        for column in range(columns):
            lanes = slice(column * BLOCK, (column + 1) * BLOCK)
            bucket = buckets[rows, lanes]
            low = bucket & 127
            upper = bucket >= 128
            for head in range(heads):
                first = jnp.broadcast_to(table[head : head + 1, :128], (8, 128))
                second = jnp.broadcast_to(table[head : head + 1, 128:], (8, 128))
                bias[head, rows, lanes] = jnp.where(
                    upper,
                    jnp.take_along_axis(second, low, axis=1, mode="promise_in_bounds"),
                    jnp.take_along_axis(first, low, axis=1, mode="promise_in_bounds"),
                )
        return unused

    lax.fori_loop(0, jnp.maximum(meta[0], meta[1]) * (BLOCK // 8), bias_rows, 0)

    for copy in weights:
        copy.wait()

    def project(block, unused):
        rows = rows_at(block)
        x_copy(block).wait()
        part = packed_x[rows, :]
        query = ((dot_nn(part, w_query[...]) + b_query[...]).astype(bf16).astype(f32) * scale).astype(bf16)
        key = dot_nn(part, w_key[...])
        value = dot_nn(part, w_value[...]) + b_value[...]
        key_t[:, rows] = key.T.astype(bf16)
        value_t[:, rows] = value.T.astype(bf16)
        key = key.astype(bf16)
        value = value.astype(bf16)
        for pair in range(pairs):
            lanes = slice(pair * 128, (pair + 1) * 128)
            query3[pair, rows, :] = query[:, lanes]
            key3[pair, rows, :] = key[:, lanes]
            value3[pair, rows, :] = value[:, lanes]
        for maker in outward:
            maker(block).start()
        return unused

    lax.fori_loop(0, meta[4], project, 0)

    def one_sequence(second, unused):
        offset = second * meta[0]
        length = meta[2 + second]

        def sized(blocks):
            count = blocks * BLOCK
            wide = min(count, 256)

            def one_head(head, unused):
                pair = head // 2
                lane = lax.broadcasted_iota(jnp.int32, (count, 128), 1)
                mine = (lane >= 64) == (head % 2 == 1)
                keys = jnp.where(mine, key3[pair, rows_at(offset, blocks), :], jnp.zeros((), bf16))
                values = value_t[pl.ds(pl.multiple_of(head * 64, 64), 64), rows_at(offset, blocks)]
                live = lax.broadcasted_iota(jnp.int32, (count, wide), 0) < length
                for column in range(count // wide):
                    lanes = slice(column * wide, (column + 1) * wide)
                    places = rows_at(offset + column * (wide // BLOCK), wide // BLOCK)
                    scores = dot_nt(keys, query3[pair, places, :]) + bias[head, :count, lanes]
                    scores = jnp.where(live, scores, masked_value)
                    top = jnp.max(scores, axis=0, keepdims=True)
                    powers = jnp.exp(scores - top)
                    total = jnp.sum(powers, axis=0, keepdims=True)
                    probs = (powers * (1.0 / total)).astype(bf16)
                    probs_t[head, rows_at(offset, blocks), lanes] = probs
                    attended_t[pl.ds(pl.multiple_of(head * 64, 64), 64), places] = dot_nn(values, probs)
                probs_copy(probs_t, probs_out, probs_sems, second, head, offset, blocks).start()
                return unused

            lax.fori_loop(0, heads, one_head, 0)

        by_length(meta, second, sized)
        return unused

    lax.fori_loop(0, 2, one_sequence, 0)

    def turn(block, unused):
        attended[rows_at(block), :] = attended_t[:, rows_at(block)].T.astype(bf16)
        return unused

    lax.fori_loop(0, meta[4], turn, 0)
    zero_tail(meta, attended)
    made = piece_copies(meta, (piece0, piece1, piece2), attended, sems, True)
    start_copies(meta, made)
    over_blocks(0, meta[4], outward, wait)
    over_probs(meta, probs_t, probs_out, probs_sems, wait)
    wait_copies(meta, made)


def feed_forward(
    meta, x, own0, own1, own2, got0, got1, got2, w_out_own_in, w_out_got_in, b_out, gain, shift,
    w_up_in, b_up, w_down_in,
    normed1, inverse_out, hidden_out, activated_out, slope_out, piece0, piece1, piece2,
    own, got, part, packed_x, w_out_own, w_out_got, w_up, w_down, inverse1, hidden_low, activated, slope,
    sems, in_sems, weight_sems, out_sems,
):
    own_copies = piece_copies(meta, (own0, own1, own2), own, sems.at[0], False)
    got_copies = piece_copies(meta, (got0, got1, got2), got, sems.at[1], False)
    start_copies(meta, own_copies)
    start_copies(meta, got_copies)
    sources = (w_out_own_in, w_out_got_in, w_up_in, w_down_in)
    weights = [
        pltpu.make_async_copy(source, target, weight_sems.at[index])
        for index, (source, target) in enumerate(zip(sources, (w_out_own, w_out_got, w_up, w_down)))
    ]
    x_copy = packing_copy(meta, x, packed_x, in_sems)
    weights[0].start()
    weights[1].start()
    over_blocks(0, meta[4], [x_copy], start)
    weights[2].start()
    weights[3].start()
    inverse_copy = rows_copy(inverse1, inverse_out, out_sems.at[0])
    hidden_copy = rows_copy(hidden_low, hidden_out, out_sems.at[1])
    activated_copy = rows_copy(activated, activated_out, out_sems.at[2])
    slope_copy = rows_copy(slope, slope_out, out_sems.at[3])
    wait_copies(meta, own_copies)
    wait_copies(meta, got_copies)
    weights[0].wait()
    weights[1].wait()
    width = w_up.shape[1]

    def first_norm(block, unused):
        rows = rows_at(block)
        head_own = dot_nn(own[rows, :], w_out_own[...]).astype(bf16).astype(f32)
        head_got = dot_nn(got[rows, :], w_out_got[...]).astype(bf16).astype(f32)
        branch = (head_own + head_got) + b_out[...]
        x_copy(block).wait()
        base = packed_x[rows, :].astype(f32) + branch
        normed, hidden, inverse = norm_forward(base, gain[...], shift[...])
        normed1[rows, :] = normed
        inverse1[rows, :] = jnp.broadcast_to(inverse, (BLOCK, 128))
        hidden_low[rows, :] = hidden.astype(bf16)
        inverse_copy(block).start()
        hidden_copy(block).start()
        return unused

    lax.fori_loop(0, meta[4], first_norm, 0)
    weights[2].wait()
    weights[3].wait()

    def one_block(block, unused):
        rows = rows_at(block)
        low = hidden_low[rows, :]
        for column in range(width // 512):
            lanes = slice(column * 512, (column + 1) * 512)
            upper = dot_nn(low, w_up[:, lanes]) + b_up[:, lanes]
            normal = 0.5 * (1.0 + lax.erf(upper * inv_root_two))
            activated[rows, lanes] = (upper * normal).astype(bf16)
            slope[rows, lanes] = (
                normal + upper * inv_root_tau * jnp.exp(-0.5 * upper * upper)
            ).astype(bf16)
        activated_copy(block).start()
        slope_copy(block).start()
        part[rows, :] = dot_nn(activated[rows, :], w_down[...]).astype(bf16)
        return unused

    lax.fori_loop(0, meta[4], one_block, 0)
    zero_tail(meta, part)
    made = piece_copies(meta, (piece0, piece1, piece2), part, sems.at[0], True)
    start_copies(meta, made)
    zero_tail(meta, activated)
    zero_tail(meta, hidden_low)
    over_blocks(meta[4], meta[5], [activated_copy, hidden_copy], start)
    over_blocks(0, meta[5], [activated_copy, hidden_copy], wait)
    over_blocks(0, meta[4], [inverse_copy, slope_copy], wait)
    wait_copies(meta, made)


def second_norm(
    meta, cotangent, own0, own1, own2, got0, got1, got2, normed1, gain1, shift1, b_down, gain2, shift2,
    w_down_in, w_up_in, slope_in,
    layer_out, grad_y2_out, grad_ffn, grad_upper, sums, sums_up, piece0, piece1, piece2,
    own, got, part, packed_grad, w_down, w_up, slope, layer_output, grad_y2,
    sems, in_sems, weight_sems, out_sems, layer_sem,
):
    own_copies = piece_copies(meta, (own0, own1, own2), own, sems.at[0], False)
    got_copies = piece_copies(meta, (got0, got1, got2), got, sems.at[1], False)
    start_copies(meta, own_copies)
    start_copies(meta, got_copies)
    weights = [
        pltpu.make_async_copy(source, target, weight_sems.at[index])
        for index, (source, target) in enumerate(((w_down_in, w_down), (w_up_in, w_up)))
    ]
    grad_copy = packing_copy(meta, cotangent, packed_grad, in_sems.at[0])
    slope_copy = rows_copy(slope_in, slope, in_sems.at[1])
    y2_copy = rows_copy(grad_y2, grad_y2_out, out_sems)
    over_blocks(0, meta[4], [grad_copy], start)
    weights[0].start()
    over_blocks(0, meta[4], [slope_copy], start)
    weights[1].start()
    sums[...] = jnp.zeros(sums.shape, f32)
    sums_up[...] = jnp.zeros(sums_up.shape, f32)
    layer_output[...] = jnp.zeros(layer_output.shape, bf16)
    wait_copies(meta, own_copies)
    wait_copies(meta, got_copies)
    width = w_up.shape[1]

    def norm_block(block, unused):
        second, first_row = place_of(meta, block)
        rows = rows_at(block)
        spot = pl.ds(first_row, BLOCK)
        live = live_rows(meta, second, first_row)
        ffn_out = (own[rows, :].astype(f32) + got[rows, :].astype(f32)) + b_down[...]
        hidden = normed1[rows, :] * gain1[...] + shift1[...]
        normed, result, inverse = norm_forward(hidden + ffn_out, gain2[...], shift2[...])
        layer_output[second, spot, :] = jnp.where(live, result, 0.0).astype(bf16)
        grad_copy(block).wait()
        grad_result = jnp.where(live, packed_grad[rows, :].astype(f32), 0.0)
        sums[0:1, :] += jnp.sum(grad_result * normed, axis=0, keepdims=True)
        sums[1:2, :] += jnp.sum(grad_result, axis=0, keepdims=True)
        grad = norm_back(grad_result, normed, inverse, gain2[...])
        grad_y2[rows, :] = grad
        y2_copy(block).start()
        low = grad.astype(bf16)
        grad_ffn[rows, :] = low
        sums[2:3, :] += jnp.sum(low.astype(f32), axis=0, keepdims=True)
        return unused

    lax.fori_loop(0, meta[4], norm_block, 0)
    layer_copy = pltpu.make_async_copy(layer_output, layer_out, layer_sem.at[0])
    layer_copy.start()
    for copy in weights:
        copy.wait()

    def one_block(block, unused):
        rows = rows_at(block)
        low = grad_ffn[rows, :]
        slope_copy(block).wait()
        for column in range(width // 512):
            lanes = slice(column * 512, (column + 1) * 512)
            back = dot_nt(low, w_down[lanes, :]) * slope[rows, lanes].astype(f32)
            back = back.astype(bf16)
            grad_upper[rows, lanes] = back
            sums_up[:, lanes] += jnp.sum(back.astype(f32), axis=0, keepdims=True)
        part[rows, :] = dot_nt(grad_upper[rows, :], w_up[...]).astype(bf16)
        return unused

    lax.fori_loop(0, meta[4], one_block, 0)
    zero_tail(meta, part)
    made = piece_copies(meta, (piece0, piece1, piece2), part, sems.at[0], True)
    start_copies(meta, made)
    zero_tail(meta, grad_ffn)
    zero_tail(meta, grad_upper)
    over_blocks(0, meta[4], [y2_copy], wait)
    layer_copy.wait()
    wait_copies(meta, made)


def ffn_weights(meta, slots, activated, grad_ffn, hidden_low, grad_upper, keep, give, stacked):
    width = grad_ffn.shape[1]
    units = activated.shape[1]

    def sized(count):
        def down(tile, unused):
            lanes = pl.ds(pl.multiple_of(tile * 256, 256), 256)
            stacked[lanes, :] = dot_tn(activated[:count, lanes], grad_ffn[:count, :])
            return unused

        lax.fori_loop(0, units // 256, down, 0)

        def up(tile, unused):
            lanes = pl.ds(pl.multiple_of(tile * 256, 256), 256)
            product = dot_tn(hidden_low[:count, lanes], grad_upper[:count, :])
            for half in range(units // width):
                spot = pl.ds(pl.multiple_of(units + half * width + tile * 256, 256), 256)
                stacked[spot, :] = product[:, half * width : (half + 1) * width]
            return unused

        lax.fori_loop(0, width // 256, up, 0)

    by_cap(meta, sized)
    scatter_chunks(slots, keep, give, stacked)


def scatter_chunks(slots, keep, give, stacked):
    chips, rows, unused = keep.shape

    def move(index, unused):
        for first, target in ((0, keep), (chips, give)):
            spot = pl.ds(pl.multiple_of(slots[first + index] * rows, 8), rows)
            target[index] = stacked[spot, :].astype(bf16)
        return unused

    lax.fori_loop(0, chips, move, 0)


def add_halves(keep, got, *outs):
    count = outs[0].shape[0]
    for index in range(keep.shape[0]):
        total = keep[index].astype(f32) + got[index].astype(f32)
        outs[index // count][index % count] = total.astype(bf16)


def attention_backward(
    meta, own0, own1, own2, got0, got1, got2, grad_y2_in, normed1, inverse_in, gain1,
    w_out_in, w_query_in, w_key_in, w_value_in, query_in, value_in, key_t_in, probs_in,
    grad_y1, grad_branch, grad_qkv, grad_scores_out, sums, sums_qv, part,
    own, got, grad_attended, grad_query_t, grad_key, grad_value,
    grad_y2, inverse1, w_out, w_query, w_key, w_value, query3, value3, key_t, probs_t,
    sems, in_sems, weight_sems, probs_sems, scores_sems,
):
    own_copies = piece_copies(meta, (own0, own1, own2), own, sems.at[0], False)
    got_copies = piece_copies(meta, (got0, got1, got2), got, sems.at[1], False)
    start_copies(meta, own_copies)
    start_copies(meta, got_copies)
    sources = (w_out_in, w_query_in, w_key_in, w_value_in)
    weights = [
        pltpu.make_async_copy(source, target, weight_sems.at[index])
        for index, (source, target) in enumerate(zip(sources, (w_out, w_query, w_key, w_value)))
    ]
    weights[0].start()
    row_copies = [rows_copy(grad_y2_in, grad_y2, in_sems.at[0]), rows_copy(inverse_in, inverse1, in_sems.at[1])]
    over_blocks(0, meta[4], row_copies, start)
    inward = [
        pairs_copy(value_in, value3, in_sems.at[2]),
        lanes_copy(key_t_in, key_t, in_sems.at[3]),
        pairs_copy(query_in, query3, in_sems.at[4]),
    ]
    over_blocks(0, meta[4], inward, start)
    over_probs(meta, probs_in, probs_t, probs_sems, start)
    for copy in weights[1:]:
        copy.start()
    sums[...] = jnp.zeros(sums.shape, f32)
    sums_qv[...] = jnp.zeros(sums_qv.shape, f32)
    wait_copies(meta, own_copies)
    wait_copies(meta, got_copies)
    weights[0].wait()
    heads = probs_t.shape[0]
    pairs = heads // 2
    local = heads * 64
    scale = 0.125

    def first_norm(block, unused):
        rows = rows_at(block)
        for maker in row_copies:
            maker(block).wait()
        grad_hidden = (own[rows, :].astype(f32) + got[rows, :].astype(f32)) + grad_y2[rows, :]
        normed = normed1[rows, :]
        sums[0:1, :] += jnp.sum(grad_hidden * normed, axis=0, keepdims=True)
        sums[1:2, :] += jnp.sum(grad_hidden, axis=0, keepdims=True)
        grad = norm_back(grad_hidden, normed, inverse1[rows, 0:1], gain1[...])
        grad_y1[rows, :] = grad
        low = grad.astype(bf16)
        grad_branch[rows, :] = low
        sums[2:3, :] += jnp.sum(low.astype(f32), axis=0, keepdims=True)
        back = dot_nt(low, w_out[...]).astype(bf16)
        for pair in range(pairs):
            grad_attended[pair, rows, :] = back[:, pair * 128 : (pair + 1) * 128]
            grad_key[pair, rows, :] = jnp.zeros((BLOCK, 128), f32)
            grad_value[pair, rows, :] = jnp.zeros((BLOCK, 128), f32)
        return unused

    lax.fori_loop(0, meta[4], first_norm, 0)
    over_blocks(0, meta[4], inward, wait)

    def one_sequence(second, unused):
        offset = second * meta[0]

        def sized(blocks):
            count = blocks * BLOCK
            wide = min(count, 256)
            every = rows_at(offset, blocks)

            def one_head(head, unused):
                pair = head // 2
                lane = lax.broadcasted_iota(jnp.int32, (wide, 128), 1)
                mine = (lane >= 64) == (head % 2 == 1)
                head_rows = pl.ds(pl.multiple_of(head * 64, 64), 64)
                values = value3[pair, every, :]
                keys = key_t[head_rows, every]
                probs_copy(probs_in, probs_t, probs_sems, second, head, offset, blocks).wait()
                for column in range(count // wide):
                    lanes = slice(column * wide, (column + 1) * wide)
                    places = rows_at(offset + column * (wide // BLOCK), wide // BLOCK)
                    zero = jnp.zeros((), bf16)
                    back = jnp.where(mine, grad_attended[pair, places, :], zero)
                    queries = jnp.where(mine, query3[pair, places, :], zero)
                    grad_probs = dot_nt(values, back)
                    probs_low = probs_t[head, every, lanes]
                    probs = probs_low.astype(f32)
                    mean = jnp.sum(probs * grad_probs, axis=0, keepdims=True)
                    grad_scores = (probs * (grad_probs - mean)).astype(bf16)
                    probs_t[head, every, lanes] = grad_scores
                    grad_value[pair, every, :] += dot_nn(probs_low, back)
                    grad_key[pair, every, :] += dot_nn(grad_scores, queries)
                    grad_query_t[head_rows, places] = dot_nn(keys, grad_scores)
                probs_copy(probs_t, grad_scores_out, scores_sems, second, head, offset, blocks).start()
                return unused

            lax.fori_loop(0, heads, one_head, 0)

        by_length(meta, second, sized)
        return unused

    lax.fori_loop(0, 2, one_sequence, 0)
    for copy in weights[1:]:
        copy.wait()

    def gather_grads(block, unused):
        rows = rows_at(block)
        query = (grad_query_t[:, rows].T * scale).astype(bf16)
        grad_qkv[rows, :local] = query
        for pair in range(pairs):
            lanes = slice(pair * 128, (pair + 1) * 128)
            grad_qkv[rows, local + pair * 128 : local + (pair + 1) * 128] = grad_key[pair, rows, :].astype(bf16)
            value = grad_value[pair, rows, :].astype(bf16)
            grad_qkv[rows, 2 * local + pair * 128 : 2 * local + (pair + 1) * 128] = value
            sums_qv[1:2, lanes] += jnp.sum(value.astype(f32), axis=0, keepdims=True)
        sums_qv[0:1, :] += jnp.sum(query.astype(f32), axis=0, keepdims=True)
        total = dot_nt(query, w_query[...])
        total = total + dot_nt(grad_qkv[rows, local : 2 * local], w_key[...])
        total = total + dot_nt(grad_qkv[rows, 2 * local :], w_value[...])
        part[rows, :] = total.astype(bf16)
        return unused

    lax.fori_loop(0, meta[4], gather_grads, 0)
    zero_tail(meta, grad_qkv)
    zero_tail(meta, grad_branch)
    over_probs(meta, probs_t, grad_scores_out, scores_sems, wait)


def attention_weights(
    meta, slots, x, grad_qkv, own0, own1, own2, grad_branch, keep, give, stacked, attended, packed_x, sems, in_sems
):
    x_copy = packing_copy(meta, x, packed_x, in_sems)
    over_blocks(0, meta[4], [x_copy], start)
    zero_tail(meta, packed_x)
    copies = piece_copies(meta, (own0, own1, own2), attended, sems, False)
    start_copies(meta, copies)
    width = packed_x.shape[1]
    local = attended.shape[1]
    wait_copies(meta, copies)
    over_blocks(0, meta[4], [x_copy], wait)

    def sized(count):
        def project(tile, unused):
            lanes = pl.ds(pl.multiple_of(tile * 256, 256), 256)
            product = dot_tn(packed_x[:count, lanes], grad_qkv[:count, :])
            for part in range(3):
                spot = pl.ds(pl.multiple_of(part * width + tile * 256, 256), 256)
                stacked[spot, :] = product[:, part * local : (part + 1) * local]
            return unused

        lax.fori_loop(0, width // 256, project, 0)
        product = dot_tn(attended[:count, :], grad_branch[:count, :])
        for half in range(width // local):
            first = 3 * width + half * local
            stacked[first : first + local, :] = product[:, half * local : (half + 1) * local]

    by_cap(meta, sized)
    scatter_chunks(slots, keep, give, stacked)


def table_histogram(part, meta, grad_scores_t, buckets, total, left, right):
    heads = grad_scores_t.shape[0]
    group = 16
    total[...] = jnp.zeros(total.shape, f32)

    def one_sequence(second, unused):
        offset = second * meta[0]

        def sized(blocks):
            count = blocks * BLOCK
            upper_digit = lax.broadcasted_iota(jnp.int32, (32, count), 0)
            lower_digit = lax.broadcasted_iota(jnp.int32, (8, count), 0)

            def one_group(index, unused):
                rows = pl.ds(pl.multiple_of(index * group, group), group)
                spots = pl.ds(pl.multiple_of(offset * BLOCK + index * group, group), group)
                bucket = buckets[rows, :count]
                upper = bucket >> 3
                lower = bucket & 7
                grads = [grad_scores_t[head, spots, :count].astype(f32) for head in range(heads)]
                for row in range(group):
                    lanes = slice(row * count, (row + 1) * count)
                    left[:, lanes] = jnp.where(upper_digit == upper[row : row + 1, :], 1.0, 0.0).astype(bf16)
                    chosen = lower_digit == lower[row : row + 1, :]
                    for head in range(0, heads, 2):
                        spread = jnp.concatenate(
                            [jnp.where(chosen, grads[head + odd][row : row + 1, :], 0.0) for odd in range(2)], axis=0
                        )
                        right[head * 8 : (head + 2) * 8, lanes] = spread.astype(bf16)
                total[...] += dot_nt(right[:, : group * count], left[:, : group * count])
                return unused

            groups = count // group
            lax.fori_loop(groups * part // TABLE_PARTS, groups * (part + 1) // TABLE_PARTS, one_group, 0)

        by_length(meta, second, sized)
        return unused

    lax.fori_loop(0, 2, one_sequence, 0)


def input_gradient(meta, grad_y1, own, got, out):
    out[...] = jnp.zeros(out.shape, f32)

    def one_block(block, unused):
        second, first_row = place_of(meta, block)
        rows = rows_at(block)
        live = live_rows(meta, second, first_row)
        total = (own[rows, :].astype(f32) + got[rows, :].astype(f32)) + grad_y1[rows, :]
        out[second, pl.ds(first_row, BLOCK), :] = jnp.where(live, total, 0.0)
        return unused

    lax.fori_loop(0, meta[4], one_block, 0)


def pack_small(sums2, sums_up, sums1, sums_qv, *refs):
    tables, out = refs[:-1], refs[-1]
    out[...] = jnp.zeros(out.shape, f32)
    row = 0
    for source, count in ((sums2, 3), (sums_up, 1), (sums1, 3), (sums_qv, 2)):
        for line in range(count):
            for column in range(source.shape[1] // 128):
                out[row : row + 1, :] = source[line : line + 1, column * 128 : (column + 1) * 128]
                row += 1
    height, wide = tables[0].shape
    first = out.shape[0] - height
    out[first:, :wide] = sum(table[...] for table in tables)


def unpack(first_place, count, targets_of, places, *refs):
    chunks, (wide, sems) = refs[:count], refs[-2:]
    outs, token = refs[-3 - targets_of.outs : -3], refs[-3]
    token[...] = jnp.zeros(token.shape, f32)
    rows = chunks[0].shape[0]
    copies = []
    for index, chunk in enumerate(chunks):
        wide[index] = chunk[...].astype(f32)
        first = places[first_place + index] * rows
        for low, high, target in targets_of(outs, rows):
            inside = (first >= low) & (first < high)
            copy = pltpu.make_async_copy(
                wide.at[index], target(pl.ds(pl.multiple_of(first - low, 8), rows)), sems.at[index]
            )
            copies.append((inside, copy))

            @pl.when(inside)
            def _():
                copy.start()

    for inside, copy in copies:
        @pl.when(inside)
        def _():
            copy.wait()


def ffn_targets(outs, rows):
    grad_up, grad_down = outs
    units, width = grad_down.shape
    found = [(0, units, lambda spot: grad_down.at[spot, :])]
    for half in range(units // width):
        lanes = pl.ds(half * width, width)
        low = units + half * width
        found.append((low, low + width, lambda spot, lanes=lanes: grad_up.at[spot, lanes]))
    return found


def attention_targets(outs, rows):
    width, local = outs[0].shape
    found = []
    for part in range(3):
        found.append((part * width, (part + 1) * width, lambda spot, part=part: outs[part].at[spot, :]))
    for half in range(width // local):
        lanes = pl.ds(half * local, local)
        low = 3 * width + half * local
        found.append((low, low + local, lambda spot, lanes=lanes: outs[3].at[spot, lanes]))
    return found


ffn_targets.outs = 2
attention_targets.outs = 4


spaces = {"s": in_smem, "v": in_vmem, "a": in_any, "h": in_hbm}


def run(kernel, specs, outs, scratch, name, room, aliases={}):
    params = pltpu.CompilerParams(vmem_limit_bytes=room * 1024 * 1024)

    def call(*args):
        return pl.pallas_call(
            kernel,
            in_specs=[spaces[kind] for kind in specs],
            out_specs=[spaces[kind] for kind, unused in outs],
            out_shape=[pltpu.HBM(shape.shape, shape.dtype) if kind == "h" else shape for kind, shape in outs],
            scratch_shapes=scratch,
            compiler_params=params,
            input_output_aliases=aliases,
            name=name,
        )(
            *[
                pltpu.with_memory_space_constraint(arg, pltpu.HBM) if kind == "h" else arg
                for kind, arg in zip(specs, args)
            ]
        )

    return call


class Unpacker:
    def __init__(self, places, targets_of, shapes, name, parts, dp_count):
        chips = dp_count // 2
        self.places = jnp.stack([places[:chips], places[chips:]], axis=1).reshape(-1)
        self.targets_of, self.shapes, self.name = targets_of, shapes, name
        self.ends = [chips * (part + 1) // parts for part in range(parts)]
        self.done, self.made, self.tokens = 0, [], []
        self.pairs = siblings(dp_count)

    def next(self, own, earlier=()):
        first, last = self.done, self.ends[len(self.tokens)]
        pieces = []
        for piece in own[first:last]:
            pieces += [piece, lax.ppermute(piece, "dp", self.pairs)]
        rows, columns = own[0].shape
        count = len(pieces)
        *self.made, token = run(
            functools.partial(unpack, 2 * first, count, self.targets_of),
            "s" + "v" * count + "a" * (len(self.made) + len(earlier)),
            [("a", shape) for shape in self.shapes] + [("v", shape_of((8, 128), f32))],
            [pltpu.VMEM((count, rows, columns), f32), pltpu.SemaphoreType.DMA((count,))],
            f"{self.name}{len(self.tokens)}",
            8,
            {1 + count + index: index for index in range(len(self.made))},
        )(self.places, *pieces, *self.made, *earlier)
        self.tokens.append(token)
        self.done = last
        return token


def swap_tensor(value):
    return lax.ppermute(value, "tensor", ((0, 1), (1, 0)))


def exchange(pieces, level):
    got0 = swap_tensor(pieces[0])
    got1, got2 = lax.switch(
        level,
        (
            lambda one, two: (one, two),
            lambda one, two: (swap_tensor(one), two),
            lambda one, two: (swap_tensor(one), swap_tensor(two)),
        ),
        pieces[1],
        pieces[2],
    )
    return got0, got1, got2


def ring_pairs(dp_count):
    chips = dp_count // 2
    order = list(range(0, chips, 2)) + list(range(chips - 1, 0, -2))
    pairs = []
    for place, chip in enumerate(order):
        after = order[(place + 1) % chips]
        pairs.append((2 * chip, 2 * after))
        pairs.append((2 * after + 1, 2 * chip + 1))
    return tuple(pairs)


def exchange_within(pieces, level):
    return lax.switch(
        level,
        (
            lambda zero, one, two: (swap_tensor(zero), one, two),
            lambda zero, one, two: (swap_tensor(zero), swap_tensor(one), two),
            lambda zero, one, two: (swap_tensor(zero), swap_tensor(one), swap_tensor(two)),
        ),
        *pieces,
    )


def fold_bits(chips):
    bits = [1]
    bit = chips // 2
    while bit > 1:
        bits.append(bit)
        bit //= 2
    return bits


def ring_places(dp_count):
    chips = dp_count // 2
    index = lax.axis_index("dp")
    chip, core = index // 2, index % 2
    position = lambda at: jnp.where(at % 2 == 0, at // 2, chips - 1 - at // 2)
    steps = jnp.arange(chips, dtype=jnp.int32)
    mine, theirs = core * chips, (1 - core) * chips
    offsets = [
        sum(bit for step, bit in enumerate(fold_bits(chips)) if slot & (chips >> (step + 1))) for slot in range(chips)
    ]
    targets = position(chip ^ jnp.array(offsets, jnp.int32))
    turn = steps * (1 - 2 * core)
    own_chunks = mine + (position(chip) - turn) % chips
    other_chunks = theirs + (position(chip) + turn) % chips
    slots = jnp.concatenate([mine + targets, theirs + targets])
    return slots.astype(jnp.int32), jnp.concatenate([own_chunks, other_chunks]).astype(jnp.int32)


def siblings(dp_count):
    return tuple((i, i ^ 1) for i in range(dp_count))


def fold(parts, stage, dp_count, room, name):
    keep, give = parts
    if stage == 0:
        pairs = siblings(dp_count)
    else:
        distance = 2 * fold_bits(dp_count // 2)[stage - 1]
        pairs = tuple((i, i ^ distance) for i in range(dp_count))
    got = lax.ppermute(give, "dp", pairs)
    count = keep.shape[0]
    halves = [count // 2, count // 2] if count > 1 else [1]
    outs = [("v", shape_of((half, *keep.shape[1:]), bf16)) for half in halves]
    return run(add_halves, "vv", outs, [], f"{name}{stage}", room)(keep, got)


def gather_both(first, second, dp_count, fill):
    pairs = ring_pairs(dp_count)
    one, two = [first], [second]
    for step in range(dp_count // 2 - 1):
        moving = after(one[step], *two[: step][-1:], *fill(step, one, two))
        one.append(lax.ppermute(moving, "dp", pairs))
        moving = after(two[step], one[step])
        two.append(lax.ppermute(moving, "dp", pairs))
    return one, two


def later(parts, *earlier):
    return after(parts[0], *earlier), parts[1]


def after(value, *earlier):
    return lax.optimization_barrier((value, earlier))[0]


def add_small(value, bit, mark, dp_count):
    got = lax.ppermute(value, "dp", tuple((i, i ^ bit) for i in range(dp_count)))
    return value + after(got, mark)


def per_device(dp_count, *arrays):
    (
        inputs, lengths, buckets, w_query, b_query, w_key, w_value, b_value, w_out, b_out, norm1_gain, norm1_shift,
        w_up, b_up, w_down, b_down, norm2_gain, norm2_shift, position_table, cotangent,
    ) = arrays
    micro, seqs, seq_len, width = inputs.shape
    bucket_count, heads = position_table.shape
    local = w_query.shape[1]
    units = w_up.shape[1]
    chips = dp_count // 2
    rows = micro * seq_len
    x = inputs.reshape(micro, seq_len, width)
    grad_out = cotangent.reshape(micro, seq_len, width)
    sizes = lengths[:, 0]
    blocks = jnp.where(sizes <= BLOCK, 1, jnp.where(sizes <= 2 * BLOCK, 2, 4))
    used = blocks[0] + blocks[1]
    level = (used > CAPS[0]).astype(jnp.int32) + (used > CAPS[1]).astype(jnp.int32)
    cap = jnp.where(level == 0, CAPS[0], jnp.where(level == 1, CAPS[1], CAPS[2]))
    meta = jnp.stack([blocks[0], blocks[1], sizes[0], sizes[1], used, cap, cap, cap]).astype(jnp.int32)
    slots, places = ring_places(dp_count)
    buckets_t = buckets.T
    table = position_table.T
    row = lambda vector: vector.reshape(1, -1)
    piece_rows = (CAPS[0] * BLOCK, (CAPS[1] - CAPS[0]) * BLOCK, rows - CAPS[1] * BLOCK)
    pieces = lambda columns: [("a", shape_of((count, columns), bf16)) for count in piece_rows]
    vmem = pltpu.VMEM
    dma = pltpu.SemaphoreType.DMA

    w_out_got = swap_tensor(w_out)
    blocks_most = rows // BLOCK
    query3, value3, key_t, probs_t, *attended = run(
        attention_forward,
        "shhvhhvvv",
        [
            ("h", shape_of((heads // 2, rows, 128), bf16)),
            ("h", shape_of((heads // 2, rows, 128), bf16)),
            ("h", shape_of((local, rows), bf16)),
            ("h", shape_of((heads, rows, seq_len), bf16)),
            *pieces(local),
        ],
        [
            vmem((rows, width), bf16),
            *[vmem((width, local), bf16)] * 3,
            *[vmem((heads // 2, rows, 128), bf16)] * 3,
            vmem((local, rows), bf16),
            vmem((heads, rows, seq_len), bf16),
            vmem((heads, seq_len, seq_len), f32),
            vmem((local, rows), bf16),
            vmem((local, rows), f32),
            vmem((rows, local), bf16),
            dma((3,)),
            dma((blocks_most,)),
            dma((3,)),
            dma((3, blocks_most)),
            dma((2, heads)),
        ],
        "attention_forward",
        27,
    )(meta, x, w_query, row(b_query), w_key, w_value, row(b_value), buckets_t, table)
    attended_got = exchange(attended, level)

    normed1, inverse1, hidden_low, activated, slope, *unit_part = run(
        feed_forward,
        "shaaaaaahhvvvhvh",
        [
            ("v", shape_of((rows, width), f32)),
            ("h", shape_of((rows, 128), f32)),
            ("h", shape_of((rows, width), bf16)),
            ("h", shape_of((rows, units), bf16)),
            ("h", shape_of((rows, units), bf16)),
            *pieces(width),
        ],
        [
            vmem((rows, local), bf16),
            vmem((rows, local), bf16),
            vmem((rows, width), bf16),
            vmem((rows, width), bf16),
            vmem((local, width), bf16),
            vmem((local, width), bf16),
            vmem((width, units), bf16),
            vmem((units, width), bf16),
            vmem((rows, 128), f32),
            vmem((rows, width), bf16),
            vmem((rows, units), bf16),
            vmem((rows, units), bf16),
            dma((2, 3)),
            dma((blocks_most,)),
            dma((4,)),
            dma((4, blocks_most)),
        ],
        "feed_forward",
        26,
    )(
        meta, x, *attended, *attended_got, w_out, w_out_got, row(b_out), row(norm1_gain), row(norm1_shift),
        w_up, row(b_up), w_down,
    )
    unit_got = exchange(unit_part, level)

    layer_output, grad_y2, grad_ffn, grad_upper, sums2, sums_up, *hidden_part = run(
        second_norm,
        "shaaaaaavvvvvvhhh",
        [
            ("h", shape_of((micro, seq_len, width), bf16)),
            ("h", shape_of((rows, width), f32)),
            ("v", shape_of((rows, width), bf16)),
            ("v", shape_of((rows, units), bf16)),
            ("v", shape_of((8, width), f32)),
            ("v", shape_of((1, units), f32)),
            *pieces(width),
        ],
        [
            vmem((rows, width), bf16),
            vmem((rows, width), bf16),
            vmem((rows, width), bf16),
            vmem((rows, width), bf16),
            vmem((units, width), bf16),
            vmem((width, units), bf16),
            vmem((rows, units), bf16),
            vmem((micro, seq_len, width), bf16),
            vmem((rows, width), f32),
            dma((2, 3)),
            dma((2, blocks_most)),
            dma((2,)),
            dma((blocks_most,)),
            dma((1,)),
        ],
        "second_norm",
        26,
    )(
        meta, grad_out, *unit_part, *unit_got, normed1, row(norm1_gain), row(norm1_shift), row(b_down),
        row(norm2_gain), row(norm2_shift), w_down, w_up, slope,
    )
    stacked_ffn = 2 * units
    ffn_parts = run(
        ffn_weights,
        "ssvvvv",
        [("v", shape_of((chips, stacked_ffn // (2 * chips), width), bf16))] * 2,
        [vmem((stacked_ffn, width), f32)],
        "ffn_weights",
        14,
    )(meta, slots, activated, grad_ffn, hidden_low, grad_upper)
    hidden_got = exchange_within(hidden_part, after(level, ffn_parts[0]))
    ffn_parts = fold(later(ffn_parts, hidden_got[0]), 0, dp_count, 8, "ffn_fold")

    grad_y1, grad_branch, grad_qkv, grad_scores_t, sums1, sums_qv, input_part = run(
        attention_backward,
        "saaaaaahvhvhhhhhhhh",
        [
            ("v", shape_of((rows, width), f32)),
            ("v", shape_of((rows, width), bf16)),
            ("v", shape_of((rows, 3 * local), bf16)),
            ("h", shape_of((heads, rows, seq_len), bf16)),
            ("v", shape_of((8, width), f32)),
            ("v", shape_of((8, local), f32)),
            ("v", shape_of((rows, width), bf16)),
        ],
        [
            vmem((rows, width), bf16),
            vmem((rows, width), bf16),
            vmem((heads // 2, rows, 128), bf16),
            vmem((local, rows), f32),
            vmem((heads // 2, rows, 128), f32),
            vmem((heads // 2, rows, 128), f32),
            vmem((rows, width), f32),
            vmem((rows, 128), f32),
            vmem((local, width), bf16),
            *[vmem((width, local), bf16)] * 3,
            *[vmem((heads // 2, rows, 128), bf16)] * 2,
            vmem((local, rows), bf16),
            vmem((heads, rows, seq_len), bf16),
            dma((2, 3)),
            dma((5, blocks_most)),
            dma((4,)),
            dma((2, heads)),
            dma((2, heads)),
        ],
        "attention_backward",
        32,
    )(
        after(meta, ffn_parts[0]), *hidden_part, *hidden_got, grad_y2, normed1, inverse1, row(norm1_gain), w_out, w_query, w_key, w_value,
        query3, value3, key_t, probs_t,
    )
    input_got = swap_tensor(input_part)

    stacked_attention = 3 * width + width * local // local
    attention_parts = run(
        attention_weights,
        "sshvaaav",
        [("v", shape_of((chips, stacked_attention // (2 * chips), local), bf16))] * 2,
        [
            vmem((stacked_attention, local), f32),
            vmem((rows, local), bf16),
            vmem((rows, width), bf16),
            dma((3,)),
            dma((blocks_most,)),
        ],
        "attention_weights",
        11,
    )(meta, slots, x, grad_qkv, *attended, grad_branch)

    table_sums = []

    def add_table(earlier):
        part = len(table_sums)
        table_sums.extend(
            run(
                functools.partial(table_histogram, part),
                "svv",
                [("v", shape_of((8 * heads, 32), f32))],
                [vmem((32, 16 * seq_len), bf16), vmem((8 * heads, 16 * seq_len), bf16)],
                f"table_histogram{part}",
                10,
            )(after(meta, *earlier), grad_scores_t, buckets_t)
        )

    stages = len(fold_bits(chips)) + 1
    ffn_parts = fold(later(ffn_parts, attention_parts[0]), 1, dp_count, 8, "ffn_fold")
    attention_parts = later(attention_parts, ffn_parts[0])
    for stage in range(stages):
        attention_parts = fold(later(attention_parts, *table_sums[-1:]), stage, dp_count, 4, "attention_fold")
        if stage == 0:
            add_table(attention_parts)
        elif stage + 1 < stages:
            ffn_parts = fold(later(ffn_parts, attention_parts[0]), stage + 1, dp_count, 8, "ffn_fold")
        for unused in range((3, 2)[stage] if stage < 2 else 0):
            add_table([*attention_parts, table_sums[-1]])
    attention_own = attention_parts[0][0]
    unpack_up = Unpacker(
        places,
        ffn_targets,
        [shape_of((width, units), f32), shape_of((units, width), f32)],
        "unpack_ffn",
        UNPACK_PARTS,
        dp_count,
    )
    unpack_heads = Unpacker(
        places,
        attention_targets,
        [shape_of((width, local), f32)] * 3 + [shape_of((local, width), f32)],
        "unpack_attention",
        2,
        dp_count,
    )

    table_rows = 8 * heads
    vector_rows = (6 * width + units + 2 * local) // 128
    small_rows = -(-vector_rows // 8) * 8 + table_rows
    (small,) = run(
        pack_small,
        "v" * (4 + TABLE_PARTS),
        [("v", shape_of((small_rows, 128), f32))],
        [],
        "pack_small",
        4,
    )(sums2, sums_up, sums1, sums_qv, *table_sums)
    sums = [small]
    small_steps = dp_count.bit_length() - 1

    def fill(step, pieces, gathered):
        waits = []
        if 0 < step <= small_steps:
            sums.append(add_small(sums[-1], 1 << (step - 1), gathered[step - 1], dp_count))
        if step <= small_steps:
            waits.append(sums[-1])
        if step in (3 * chips // 8, 5 * chips // 8, 6 * chips // 8):
            waits.append(unpack_up.next(pieces))
        return waits

    ffn_pieces, attention_pieces = gather_both(ffn_parts[0][0], attention_own, dp_count, fill)
    unpack_up.next(ffn_pieces)
    unpack_heads.next(attention_pieces, unpack_up.tokens)
    unpack_heads.next(attention_pieces)
    grad_w_up, grad_w_down = unpack_up.made
    grad_w_query, grad_w_key, grad_w_value, grad_w_out = unpack_heads.made

    (grad_inputs,) = run(
        input_gradient,
        "svvv",
        [("v", shape_of((micro, seq_len, width), f32))],
        [],
        "input_gradient",
        12,
    )(meta, grad_y1, input_part, input_got)

    small = sums[-1]
    table_grad = small[small_rows - table_rows :, :32].reshape(heads, 8, 32).transpose(2, 1, 0)
    small = small[:vector_rows].reshape(-1)
    cuts = []
    start = 0
    for count in (width, width, width, units, width, width, width, local, local):
        cuts.append(small[start : start + count])
        start += count
    grad_gain2, grad_shift2, grad_b_down, grad_b_up, grad_gain1, grad_shift1, grad_b_out, grad_b_query, grad_b_value = cuts
    return (
        layer_output.reshape(inputs.shape),
        grad_inputs.reshape(inputs.shape),
        grad_w_query,
        grad_b_query,
        grad_w_key,
        grad_w_value,
        grad_b_value,
        grad_w_out,
        grad_b_out,
        grad_gain1,
        grad_shift1,
        grad_w_up,
        grad_b_up,
        grad_w_down,
        grad_b_down,
        grad_gain2,
        grad_shift2,
        table_grad.reshape(bucket_count, heads),
    )


def solution(mesh):
    placed = (
        P(None, "dp", None, None),
        P(None, "dp"),
        P(),
        P(None, "tensor"),
        P("tensor"),
        P(None, "tensor"),
        P(None, "tensor"),
        P("tensor"),
        P("tensor", None),
        P(),
        P(),
        P(),
        P(None, "tensor"),
        P("tensor"),
        P("tensor", None),
        P(),
        P(),
        P(),
        P(None, "tensor"),
        P(None, "dp", None, None),
    )
    dp_count = mesh.shape["dp"]
    return jax.shard_map(
        lambda *arrays: per_device(dp_count, *arrays),
        mesh=mesh,
        in_specs=placed,
        out_specs=(
            P(None, "dp", None, None),
            P(None, "dp", None, None),
            P(None, "tensor"),
            P("tensor"),
            P(None, "tensor"),
            P(None, "tensor"),
            P("tensor"),
            P("tensor", None),
            P(),
            P(),
            P(),
            P(None, "tensor"),
            P("tensor"),
            P("tensor", None),
            P(),
            P(),
            P(),
            P(None, "tensor"),
        ),
        check_vma=False,
    )
```

```python
import functools

import jax
import jax.numpy as jnp
from jax import lax
from jax.experimental import pallas as pl
from jax.experimental.pallas import tpu as pltpu
from jax.sharding import PartitionSpec as P

epsilon = 1e-05
masked_value = -1e30
inv_root_two = 0.7071067811865476
inv_root_tau = 0.3989422804014327

BLOCK = 128
CAPS = (2, 5, 6, 8)
TABLE_PARTS = 6
UNPACK_PARTS = 4
bf16 = jnp.bfloat16
f32 = jnp.float32
shape_of = jax.ShapeDtypeStruct

in_vmem = pl.BlockSpec(memory_space=pltpu.VMEM)
in_smem = pl.BlockSpec(memory_space=pltpu.SMEM)
in_any = pl.BlockSpec(memory_space=pl.ANY)
in_hbm = pl.BlockSpec(memory_space=pltpu.HBM)


def rows_at(block, count=1):
    return pl.ds(pl.multiple_of(block * BLOCK, BLOCK), count * BLOCK)


def dot_nn(left, right):
    return lax.dot_general(left, right, (((1,), (0,)), ((), ())), preferred_element_type=f32)


def dot_nt(left, right):
    return lax.dot_general(left, right, (((1,), (1,)), ((), ())), preferred_element_type=f32)


def dot_tn(left, right):
    return lax.dot_general(left, right, (((0,), (0,)), ((), ())), preferred_element_type=f32)


def place_of(meta, block):
    second = (block >= meta[0]).astype(jnp.int32)
    return second, pl.multiple_of((block - second * meta[0]) * BLOCK, BLOCK)


def live_rows(meta, second, first_row):
    rows = lax.broadcasted_iota(jnp.int32, (BLOCK, 1), 0) + first_row
    return rows < meta[2 + second]


def zero_tail(meta, ref):
    def clear(block, unused):
        ref[rows_at(block), :] = jnp.zeros((BLOCK, ref.shape[1]), ref.dtype)
        return unused

    lax.fori_loop(meta[4], meta[5], clear, 0)


def piece_copies(meta, pieces, whole, sems, to_pieces):
    start = 0
    made = []
    for index, piece in enumerate(pieces):
        rows = piece.shape[0]
        part = whole.at[pl.ds(start, rows), :]
        pair = (part, piece) if to_pieces else (piece, part)
        made.append((start // BLOCK, pltpu.make_async_copy(pair[0], pair[1], sems.at[index])))
        start += rows
    return made


def start_copies(meta, made):
    for first, copy in made:
        @pl.when(meta[5] > first)
        def _():
            copy.start()


def wait_copies(meta, made):
    for first, copy in made:
        @pl.when(meta[5] > first)
        def _():
            copy.wait()


def over_blocks(first, last, makers, act):
    def one(block, unused):
        for maker in makers:
            act(maker(block))
        return unused

    lax.fori_loop(first, last, one, 0)


def start(copy):
    copy.start()


def wait(copy):
    copy.wait()


def rows_copy(source, target, sems):
    return lambda block: pltpu.make_async_copy(source.at[rows_at(block), :], target.at[rows_at(block), :], sems.at[block])


def pairs_copy(source, target, sems):
    return lambda block: pltpu.make_async_copy(
        source.at[:, rows_at(block), :], target.at[:, rows_at(block), :], sems.at[block]
    )


def lanes_copy(source, target, sems):
    return lambda block: pltpu.make_async_copy(source.at[:, rows_at(block)], target.at[:, rows_at(block)], sems.at[block])


def packing_copy(meta, source, target, sems):
    def maker(block):
        second, first_row = place_of(meta, block)
        return pltpu.make_async_copy(
            source.at[second, pl.ds(first_row, BLOCK), :], target.at[rows_at(block), :], sems.at[block]
        )

    return maker


def probs_copy(source, target, sems, second, head, offset, blocks):
    spot = rows_at(offset, blocks)
    lanes = pl.ds(0, blocks * BLOCK)
    return pltpu.make_async_copy(
        source.at[head, spot, lanes], target.at[head, spot, lanes], sems.at[second, head]
    )


def over_probs(meta, source, target, sems, act):
    def one_sequence(second, unused):
        def sized(blocks):
            def one_head(head, unused):
                act(probs_copy(source, target, sems, second, head, second * meta[0], blocks))
                return unused

            lax.fori_loop(0, source.shape[0], one_head, 0)

        by_length(meta, second, sized)
        return unused

    lax.fori_loop(0, 2, one_sequence, 0)


def by_length(meta, second, body):
    for blocks in (1, 2, 4):
        @pl.when(meta[second] == blocks)
        def _():
            body(blocks)


def by_cap(meta, body):
    for blocks in CAPS:
        @pl.when(meta[5] == blocks)
        def _():
            body(blocks * BLOCK)


def norm_forward(rows, gain, shift):
    centre = rows - jnp.mean(rows, axis=-1, keepdims=True)
    inverse = lax.rsqrt(jnp.mean(centre * centre, axis=-1, keepdims=True) + epsilon)
    normed = centre * inverse
    return normed, normed * gain + shift, inverse


def norm_back(grad_rows, normed, inverse, gain):
    scaled = grad_rows * gain
    first_mean = jnp.mean(scaled, axis=-1, keepdims=True)
    second_mean = jnp.mean(scaled * normed, axis=-1, keepdims=True)
    return inverse * (scaled - first_mean - normed * second_mean)


def attention_forward(
    meta, x, w_query_in, b_query, w_key_in, w_value_in, b_value, buckets, table,
    query_out, value_out, key_t_out, probs_out, piece0, piece1, piece2, piece3,
    packed_x, w_query, w_key, w_value, query3, key3, value3, key_t, probs_t,
    bias, value_t, attended_t, attended, sems, in_sems, weight_sems, out_sems, probs_sems,
):
    weights = [
        pltpu.make_async_copy(source, target, weight_sems.at[index])
        for index, (source, target) in enumerate(((w_query_in, w_query), (w_key_in, w_key), (w_value_in, w_value)))
    ]
    for copy in weights:
        copy.start()
    x_copy = packing_copy(meta, x, packed_x, in_sems)
    over_blocks(0, meta[4], [x_copy], start)
    outward = [
        pairs_copy(query3, query_out, out_sems.at[0]),
        pairs_copy(value3, value_out, out_sems.at[1]),
        lanes_copy(key_t, key_t_out, out_sems.at[2]),
    ]
    heads = probs_t.shape[0]
    pairs = heads // 2
    scale = 0.125
    seq_len = buckets.shape[1]
    columns = seq_len // BLOCK

    def bias_rows(group, unused):
        rows = pl.ds(pl.multiple_of(group * 8, 8), 8)
        for column in range(columns):
            lanes = slice(column * BLOCK, (column + 1) * BLOCK)
            bucket = buckets[rows, lanes]
            low = bucket & 127
            upper = bucket >= 128
            for head in range(heads):
                first = jnp.broadcast_to(table[head : head + 1, :128], (8, 128))
                second = jnp.broadcast_to(table[head : head + 1, 128:], (8, 128))
                bias[head, rows, lanes] = jnp.where(
                    upper,
                    jnp.take_along_axis(second, low, axis=1, mode="promise_in_bounds"),
                    jnp.take_along_axis(first, low, axis=1, mode="promise_in_bounds"),
                )
        return unused

    lax.fori_loop(0, jnp.maximum(meta[0], meta[1]) * (BLOCK // 8), bias_rows, 0)

    for copy in weights:
        copy.wait()

    def project(block, unused):
        rows = rows_at(block)
        x_copy(block).wait()
        part = packed_x[rows, :]
        query = ((dot_nn(part, w_query[...]) + b_query[...]).astype(bf16).astype(f32) * scale).astype(bf16)
        key = dot_nn(part, w_key[...])
        value = dot_nn(part, w_value[...]) + b_value[...]
        key_t[:, rows] = key.T.astype(bf16)
        value_t[:, rows] = value.T.astype(bf16)
        key = key.astype(bf16)
        value = value.astype(bf16)
        for pair in range(pairs):
            lanes = slice(pair * 128, (pair + 1) * 128)
            query3[pair, rows, :] = query[:, lanes]
            key3[pair, rows, :] = key[:, lanes]
            value3[pair, rows, :] = value[:, lanes]
        for maker in outward:
            maker(block).start()
        return unused

    lax.fori_loop(0, meta[4], project, 0)

    def one_sequence(second, unused):
        offset = second * meta[0]
        length = meta[2 + second]

        def sized(blocks):
            count = blocks * BLOCK
            wide = min(count, 256)

            def one_head(head, unused):
                pair = head // 2
                lane = lax.broadcasted_iota(jnp.int32, (count, 128), 1)
                mine = (lane >= 64) == (head % 2 == 1)
                keys = jnp.where(mine, key3[pair, rows_at(offset, blocks), :], jnp.zeros((), bf16))
                values = value_t[pl.ds(pl.multiple_of(head * 64, 64), 64), rows_at(offset, blocks)]
                live = lax.broadcasted_iota(jnp.int32, (count, wide), 0) < length
                for column in range(count // wide):
                    lanes = slice(column * wide, (column + 1) * wide)
                    places = rows_at(offset + column * (wide // BLOCK), wide // BLOCK)
                    scores = dot_nt(keys, query3[pair, places, :]) + bias[head, :count, lanes]
                    scores = jnp.where(live, scores, masked_value)
                    top = jnp.max(scores, axis=0, keepdims=True)
                    powers = jnp.exp(scores - top)
                    total = jnp.sum(powers, axis=0, keepdims=True)
                    probs = (powers * (1.0 / total)).astype(bf16)
                    probs_t[head, rows_at(offset, blocks), lanes] = probs
                    attended_t[pl.ds(pl.multiple_of(head * 64, 64), 64), places] = dot_nn(values, probs)
                probs_copy(probs_t, probs_out, probs_sems, second, head, offset, blocks).start()
                return unused

            lax.fori_loop(0, heads, one_head, 0)

        by_length(meta, second, sized)
        return unused

    lax.fori_loop(0, 2, one_sequence, 0)

    def turn(block, unused):
        attended[rows_at(block), :] = attended_t[:, rows_at(block)].T.astype(bf16)
        return unused

    lax.fori_loop(0, meta[4], turn, 0)
    zero_tail(meta, attended)
    made = piece_copies(meta, (piece0, piece1, piece2, piece3), attended, sems, True)
    start_copies(meta, made)
    over_blocks(0, meta[4], outward, wait)
    over_probs(meta, probs_t, probs_out, probs_sems, wait)
    wait_copies(meta, made)


def feed_forward(
    meta, x, own0, own1, own2, own3, got0, got1, got2, got3, w_out_own_in, w_out_got_in, b_out, gain, shift,
    w_up_in, b_up, w_down_in,
    normed_out, inverse_out, hidden_out, activated_out, slope_out, piece0, piece1, piece2, piece3,
    own, got, part, packed_x, w_out_own, w_out_got, w_up, w_down, normed1, inverse1, hidden_low, activated, slope,
    sems, in_sems, weight_sems, out_sems,
):
    own_copies = piece_copies(meta, (own0, own1, own2, own3), own, sems.at[0], False)
    got_copies = piece_copies(meta, (got0, got1, got2, got3), got, sems.at[1], False)
    start_copies(meta, own_copies)
    start_copies(meta, got_copies)
    sources = (w_out_own_in, w_out_got_in, w_up_in, w_down_in)
    weights = [
        pltpu.make_async_copy(source, target, weight_sems.at[index])
        for index, (source, target) in enumerate(zip(sources, (w_out_own, w_out_got, w_up, w_down)))
    ]
    x_copy = packing_copy(meta, x, packed_x, in_sems)
    weights[0].start()
    weights[1].start()
    over_blocks(0, meta[4], [x_copy], start)
    weights[2].start()
    weights[3].start()
    inverse_copy = rows_copy(inverse1, inverse_out, out_sems.at[0])
    hidden_copy = rows_copy(hidden_low, hidden_out, out_sems.at[1])
    activated_copy = rows_copy(activated, activated_out, out_sems.at[2])
    slope_copy = rows_copy(slope, slope_out, out_sems.at[3])
    normed_copy = rows_copy(normed1, normed_out, out_sems.at[4])
    wait_copies(meta, own_copies)
    wait_copies(meta, got_copies)
    weights[0].wait()
    weights[1].wait()
    width = w_up.shape[1]

    def first_norm(block, unused):
        rows = rows_at(block)
        head_own = dot_nn(own[rows, :], w_out_own[...]).astype(bf16).astype(f32)
        head_got = dot_nn(got[rows, :], w_out_got[...]).astype(bf16).astype(f32)
        branch = (head_own + head_got) + b_out[...]
        x_copy(block).wait()
        base = packed_x[rows, :].astype(f32) + branch
        normed, hidden, inverse = norm_forward(base, gain[...], shift[...])
        normed1[rows, :] = normed
        inverse1[rows, :] = jnp.broadcast_to(inverse, (BLOCK, 128))
        hidden_low[rows, :] = hidden.astype(bf16)
        normed_copy(block).start()
        inverse_copy(block).start()
        hidden_copy(block).start()
        return unused

    lax.fori_loop(0, meta[4], first_norm, 0)
    weights[2].wait()
    weights[3].wait()

    def one_block(block, unused):
        rows = rows_at(block)
        low = hidden_low[rows, :]
        for column in range(width // 512):
            lanes = slice(column * 512, (column + 1) * 512)
            upper = dot_nn(low, w_up[:, lanes]) + b_up[:, lanes]
            normal = 0.5 * (1.0 + lax.erf(upper * inv_root_two))
            activated[rows, lanes] = (upper * normal).astype(bf16)
            slope[rows, lanes] = (
                normal + upper * inv_root_tau * jnp.exp(-0.5 * upper * upper)
            ).astype(bf16)
        activated_copy(block).start()
        slope_copy(block).start()
        part[rows, :] = dot_nn(activated[rows, :], w_down[...]).astype(bf16)
        return unused

    lax.fori_loop(0, meta[4], one_block, 0)
    zero_tail(meta, part)
    made = piece_copies(meta, (piece0, piece1, piece2, piece3), part, sems.at[0], True)
    start_copies(meta, made)
    zero_tail(meta, activated)
    zero_tail(meta, hidden_low)
    over_blocks(meta[4], meta[5], [activated_copy, hidden_copy], start)
    over_blocks(0, meta[5], [activated_copy, hidden_copy], wait)
    over_blocks(0, meta[4], [normed_copy, inverse_copy, slope_copy], wait)
    wait_copies(meta, made)


def second_norm(
    meta, cotangent, own0, own1, own2, own3, got0, got1, got2, got3, normed_in, gain1, shift1, b_down, gain2, shift2,
    w_down_in, w_up_in, slope_in,
    layer_out, grad_y2_out, grad_ffn, grad_upper, sums, sums_up, piece0, piece1, piece2, piece3,
    own, got, part, normed1, packed_grad, w_down, w_up, slope, layer_output, grad_y2,
    sems, in_sems, weight_sems, out_sems, layer_sem,
):
    own_copies = piece_copies(meta, (own0, own1, own2, own3), own, sems.at[0], False)
    got_copies = piece_copies(meta, (got0, got1, got2, got3), got, sems.at[1], False)
    start_copies(meta, own_copies)
    start_copies(meta, got_copies)
    weights = [
        pltpu.make_async_copy(source, target, weight_sems.at[index])
        for index, (source, target) in enumerate(((w_down_in, w_down), (w_up_in, w_up)))
    ]
    grad_copy = packing_copy(meta, cotangent, packed_grad, in_sems.at[0])
    slope_copy = rows_copy(slope_in, slope, in_sems.at[1])
    y2_copy = rows_copy(grad_y2, grad_y2_out, out_sems)
    normed_copy = rows_copy(normed_in, normed1, in_sems.at[2])
    over_blocks(0, meta[4], [normed_copy, grad_copy], start)
    weights[0].start()
    over_blocks(0, meta[4], [slope_copy], start)
    weights[1].start()
    sums[...] = jnp.zeros(sums.shape, f32)
    sums_up[...] = jnp.zeros(sums_up.shape, f32)
    layer_output[...] = jnp.zeros(layer_output.shape, bf16)
    wait_copies(meta, own_copies)
    wait_copies(meta, got_copies)
    width = w_up.shape[1]

    def norm_block(block, unused):
        second, first_row = place_of(meta, block)
        rows = rows_at(block)
        spot = pl.ds(first_row, BLOCK)
        live = live_rows(meta, second, first_row)
        ffn_out = (own[rows, :].astype(f32) + got[rows, :].astype(f32)) + b_down[...]
        normed_copy(block).wait()
        hidden = normed1[rows, :] * gain1[...] + shift1[...]
        normed, result, inverse = norm_forward(hidden + ffn_out, gain2[...], shift2[...])
        layer_output[second, spot, :] = jnp.where(live, result, 0.0).astype(bf16)
        grad_copy(block).wait()
        grad_result = jnp.where(live, packed_grad[rows, :].astype(f32), 0.0)
        sums[0:1, :] += jnp.sum(grad_result * normed, axis=0, keepdims=True)
        sums[1:2, :] += jnp.sum(grad_result, axis=0, keepdims=True)
        grad = norm_back(grad_result, normed, inverse, gain2[...])
        grad_y2[rows, :] = grad
        y2_copy(block).start()
        low = grad.astype(bf16)
        grad_ffn[rows, :] = low
        sums[2:3, :] += jnp.sum(low.astype(f32), axis=0, keepdims=True)
        return unused

    lax.fori_loop(0, meta[4], norm_block, 0)
    layer_copy = pltpu.make_async_copy(layer_output, layer_out, layer_sem.at[0])
    layer_copy.start()
    for copy in weights:
        copy.wait()

    def one_block(block, unused):
        rows = rows_at(block)
        low = grad_ffn[rows, :]
        slope_copy(block).wait()
        for column in range(width // 512):
            lanes = slice(column * 512, (column + 1) * 512)
            back = dot_nt(low, w_down[lanes, :]) * slope[rows, lanes].astype(f32)
            back = back.astype(bf16)
            grad_upper[rows, lanes] = back
            sums_up[:, lanes] += jnp.sum(back.astype(f32), axis=0, keepdims=True)
        part[rows, :] = dot_nt(grad_upper[rows, :], w_up[...]).astype(bf16)
        return unused

    lax.fori_loop(0, meta[4], one_block, 0)
    zero_tail(meta, part)
    made = piece_copies(meta, (piece0, piece1, piece2, piece3), part, sems.at[0], True)
    start_copies(meta, made)
    zero_tail(meta, grad_ffn)
    zero_tail(meta, grad_upper)
    over_blocks(0, meta[4], [y2_copy], wait)
    layer_copy.wait()
    wait_copies(meta, made)


def ffn_weights(meta, slots, activated, grad_ffn, hidden_low, grad_upper, keep, give, stacked):
    width = grad_ffn.shape[1]
    units = activated.shape[1]

    def sized(count):
        def down(tile, unused):
            lanes = pl.ds(pl.multiple_of(tile * 256, 256), 256)
            stacked[lanes, :] = dot_tn(activated[:count, lanes], grad_ffn[:count, :])
            return unused

        lax.fori_loop(0, units // 256, down, 0)

        def up(tile, unused):
            lanes = pl.ds(pl.multiple_of(tile * 256, 256), 256)
            product = dot_tn(hidden_low[:count, lanes], grad_upper[:count, :])
            for half in range(units // width):
                spot = pl.ds(pl.multiple_of(units + half * width + tile * 256, 256), 256)
                stacked[spot, :] = product[:, half * width : (half + 1) * width]
            return unused

        lax.fori_loop(0, width // 256, up, 0)

    by_cap(meta, sized)
    scatter_chunks(slots, keep, give, stacked)


def scatter_chunks(slots, keep, give, stacked):
    chips, rows, unused = keep.shape

    def move(index, unused):
        for first, target in ((0, keep), (chips, give)):
            spot = pl.ds(pl.multiple_of(slots[first + index] * rows, 8), rows)
            target[index] = stacked[spot, :].astype(bf16)
        return unused

    lax.fori_loop(0, chips, move, 0)


def add_halves(keep, got, *outs):
    count = outs[0].shape[0]
    for index in range(keep.shape[0]):
        total = keep[index].astype(f32) + got[index].astype(f32)
        outs[index // count][index % count] = total.astype(bf16)


def attention_backward(
    meta, own0, own1, own2, own3, got0, got1, got2, got3, grad_y2_in, normed_in, inverse_in, gain1,
    w_out_in, w_query_in, w_key_in, w_value_in, query_in, value_in, key_t_in, probs_in,
    grad_y1, grad_branch, grad_qkv, grad_scores_out, sums, sums_qv, part,
    own, got, grad_attended, grad_query_t, grad_key, grad_value,
    grad_y2, normed1, inverse1, w_out, w_query, w_key, w_value, query3, value3, key_t, probs_t,
    sems, in_sems, weight_sems, probs_sems, scores_sems,
):
    own_copies = piece_copies(meta, (own0, own1, own2, own3), own, sems.at[0], False)
    got_copies = piece_copies(meta, (got0, got1, got2, got3), got, sems.at[1], False)
    start_copies(meta, own_copies)
    start_copies(meta, got_copies)
    sources = (w_out_in, w_query_in, w_key_in, w_value_in)
    weights = [
        pltpu.make_async_copy(source, target, weight_sems.at[index])
        for index, (source, target) in enumerate(zip(sources, (w_out, w_query, w_key, w_value)))
    ]
    weights[0].start()
    row_copies = [
        rows_copy(grad_y2_in, grad_y2, in_sems.at[0]),
        rows_copy(inverse_in, inverse1, in_sems.at[1]),
        rows_copy(normed_in, normed1, in_sems.at[5]),
    ]
    over_blocks(0, meta[4], row_copies, start)
    inward = [
        pairs_copy(value_in, value3, in_sems.at[2]),
        lanes_copy(key_t_in, key_t, in_sems.at[3]),
        pairs_copy(query_in, query3, in_sems.at[4]),
    ]
    over_blocks(0, meta[4], inward, start)
    over_probs(meta, probs_in, probs_t, probs_sems, start)
    for copy in weights[1:]:
        copy.start()
    sums[...] = jnp.zeros(sums.shape, f32)
    sums_qv[...] = jnp.zeros(sums_qv.shape, f32)
    wait_copies(meta, own_copies)
    wait_copies(meta, got_copies)
    weights[0].wait()
    heads = probs_t.shape[0]
    pairs = heads // 2
    local = heads * 64
    scale = 0.125

    def first_norm(block, unused):
        rows = rows_at(block)
        for maker in row_copies:
            maker(block).wait()
        grad_hidden = (own[rows, :].astype(f32) + got[rows, :].astype(f32)) + grad_y2[rows, :]
        normed = normed1[rows, :]
        sums[0:1, :] += jnp.sum(grad_hidden * normed, axis=0, keepdims=True)
        sums[1:2, :] += jnp.sum(grad_hidden, axis=0, keepdims=True)
        grad = norm_back(grad_hidden, normed, inverse1[rows, 0:1], gain1[...])
        grad_y1[rows, :] = grad
        low = grad.astype(bf16)
        grad_branch[rows, :] = low
        sums[2:3, :] += jnp.sum(low.astype(f32), axis=0, keepdims=True)
        back = dot_nt(low, w_out[...]).astype(bf16)
        for pair in range(pairs):
            grad_attended[pair, rows, :] = back[:, pair * 128 : (pair + 1) * 128]
            grad_key[pair, rows, :] = jnp.zeros((BLOCK, 128), f32)
            grad_value[pair, rows, :] = jnp.zeros((BLOCK, 128), f32)
        return unused

    lax.fori_loop(0, meta[4], first_norm, 0)
    over_blocks(0, meta[4], inward, wait)

    def one_sequence(second, unused):
        offset = second * meta[0]

        def sized(blocks):
            count = blocks * BLOCK
            wide = min(count, 256)
            every = rows_at(offset, blocks)

            def one_head(head, unused):
                pair = head // 2
                lane = lax.broadcasted_iota(jnp.int32, (wide, 128), 1)
                mine = (lane >= 64) == (head % 2 == 1)
                head_rows = pl.ds(pl.multiple_of(head * 64, 64), 64)
                values = value3[pair, every, :]
                keys = key_t[head_rows, every]
                probs_copy(probs_in, probs_t, probs_sems, second, head, offset, blocks).wait()
                for column in range(count // wide):
                    lanes = slice(column * wide, (column + 1) * wide)
                    places = rows_at(offset + column * (wide // BLOCK), wide // BLOCK)
                    zero = jnp.zeros((), bf16)
                    back = jnp.where(mine, grad_attended[pair, places, :], zero)
                    queries = jnp.where(mine, query3[pair, places, :], zero)
                    grad_probs = dot_nt(values, back)
                    probs_low = probs_t[head, every, lanes]
                    probs = probs_low.astype(f32)
                    mean = jnp.sum(probs * grad_probs, axis=0, keepdims=True)
                    grad_scores = (probs * (grad_probs - mean)).astype(bf16)
                    probs_t[head, every, lanes] = grad_scores
                    grad_value[pair, every, :] += dot_nn(probs_low, back)
                    grad_key[pair, every, :] += dot_nn(grad_scores, queries)
                    grad_query_t[head_rows, places] = dot_nn(keys, grad_scores)
                probs_copy(probs_t, grad_scores_out, scores_sems, second, head, offset, blocks).start()
                return unused

            lax.fori_loop(0, heads, one_head, 0)

        by_length(meta, second, sized)
        return unused

    lax.fori_loop(0, 2, one_sequence, 0)
    for copy in weights[1:]:
        copy.wait()

    def gather_grads(block, unused):
        rows = rows_at(block)
        query = (grad_query_t[:, rows].T * scale).astype(bf16)
        grad_qkv[rows, :local] = query
        for pair in range(pairs):
            lanes = slice(pair * 128, (pair + 1) * 128)
            grad_qkv[rows, local + pair * 128 : local + (pair + 1) * 128] = grad_key[pair, rows, :].astype(bf16)
            value = grad_value[pair, rows, :].astype(bf16)
            grad_qkv[rows, 2 * local + pair * 128 : 2 * local + (pair + 1) * 128] = value
            sums_qv[1:2, lanes] += jnp.sum(value.astype(f32), axis=0, keepdims=True)
        sums_qv[0:1, :] += jnp.sum(query.astype(f32), axis=0, keepdims=True)
        total = dot_nt(query, w_query[...])
        total = total + dot_nt(grad_qkv[rows, local : 2 * local], w_key[...])
        total = total + dot_nt(grad_qkv[rows, 2 * local :], w_value[...])
        part[rows, :] = total.astype(bf16)
        return unused

    lax.fori_loop(0, meta[4], gather_grads, 0)
    zero_tail(meta, grad_qkv)
    zero_tail(meta, grad_branch)
    over_probs(meta, probs_t, grad_scores_out, scores_sems, wait)


def attention_weights(
    meta, slots, x, grad_qkv, own0, own1, own2, own3, grad_branch, keep, give, stacked, attended, packed_x, sems, in_sems
):
    x_copy = packing_copy(meta, x, packed_x, in_sems)
    over_blocks(0, meta[4], [x_copy], start)
    zero_tail(meta, packed_x)
    copies = piece_copies(meta, (own0, own1, own2, own3), attended, sems, False)
    start_copies(meta, copies)
    width = packed_x.shape[1]
    local = attended.shape[1]
    wait_copies(meta, copies)
    over_blocks(0, meta[4], [x_copy], wait)

    def sized(count):
        def project(tile, unused):
            lanes = pl.ds(pl.multiple_of(tile * 256, 256), 256)
            product = dot_tn(packed_x[:count, lanes], grad_qkv[:count, :])
            for part in range(3):
                spot = pl.ds(pl.multiple_of(part * width + tile * 256, 256), 256)
                stacked[spot, :] = product[:, part * local : (part + 1) * local]
            return unused

        lax.fori_loop(0, width // 256, project, 0)
        product = dot_tn(attended[:count, :], grad_branch[:count, :])
        for half in range(width // local):
            first = 3 * width + half * local
            stacked[first : first + local, :] = product[:, half * local : (half + 1) * local]

    by_cap(meta, sized)
    scatter_chunks(slots, keep, give, stacked)


def table_histogram(part, meta, grad_scores_t, buckets, total, left, right):
    heads = grad_scores_t.shape[0]
    group = 16
    total[...] = jnp.zeros(total.shape, f32)

    def one_sequence(second, unused):
        offset = second * meta[0]

        def sized(blocks):
            count = blocks * BLOCK
            upper_digit = lax.broadcasted_iota(jnp.int32, (32, count), 0)
            lower_digit = lax.broadcasted_iota(jnp.int32, (8, count), 0)

            def one_group(index, unused):
                rows = pl.ds(pl.multiple_of(index * group, group), group)
                spots = pl.ds(pl.multiple_of(offset * BLOCK + index * group, group), group)
                bucket = buckets[rows, :count]
                upper = bucket >> 3
                lower = bucket & 7
                grads = [grad_scores_t[head, spots, :count].astype(f32) for head in range(heads)]
                for row in range(group):
                    lanes = slice(row * count, (row + 1) * count)
                    left[:, lanes] = jnp.where(upper_digit == upper[row : row + 1, :], 1.0, 0.0).astype(bf16)
                    chosen = lower_digit == lower[row : row + 1, :]
                    for head in range(0, heads, 2):
                        spread = jnp.concatenate(
                            [jnp.where(chosen, grads[head + odd][row : row + 1, :], 0.0) for odd in range(2)], axis=0
                        )
                        right[head * 8 : (head + 2) * 8, lanes] = spread.astype(bf16)
                total[...] += dot_nt(right[:, : group * count], left[:, : group * count])
                return unused

            groups = count // group
            lax.fori_loop(groups * part // TABLE_PARTS, groups * (part + 1) // TABLE_PARTS, one_group, 0)

        by_length(meta, second, sized)
        return unused

    lax.fori_loop(0, 2, one_sequence, 0)


def input_gradient(meta, grad_y1, own, got, out):
    out[...] = jnp.zeros(out.shape, f32)

    def one_block(block, unused):
        second, first_row = place_of(meta, block)
        rows = rows_at(block)
        live = live_rows(meta, second, first_row)
        total = (own[rows, :].astype(f32) + got[rows, :].astype(f32)) + grad_y1[rows, :]
        out[second, pl.ds(first_row, BLOCK), :] = jnp.where(live, total, 0.0)
        return unused

    lax.fori_loop(0, meta[4], one_block, 0)


def pack_small(sums2, sums_up, sums1, sums_qv, *refs):
    tables, out = refs[:-1], refs[-1]
    out[...] = jnp.zeros(out.shape, f32)
    row = 0
    for source, count in ((sums2, 3), (sums_up, 1), (sums1, 3), (sums_qv, 2)):
        for line in range(count):
            for column in range(source.shape[1] // 128):
                out[row : row + 1, :] = source[line : line + 1, column * 128 : (column + 1) * 128]
                row += 1
    height, wide = tables[0].shape
    first = out.shape[0] - height
    out[first:, :wide] = sum(table[...] for table in tables)


def unpack(first_place, count, targets_of, places, *refs):
    chunks, (wide, sems) = refs[:count], refs[-2:]
    outs, token = refs[-3 - targets_of.outs : -3], refs[-3]
    token[...] = jnp.zeros(token.shape, f32)
    rows = chunks[0].shape[0]
    copies = []
    for index, chunk in enumerate(chunks):
        wide[index] = chunk[...].astype(f32)
        first = places[first_place + index] * rows
        for low, high, target in targets_of(outs, rows):
            inside = (first >= low) & (first < high)
            copy = pltpu.make_async_copy(
                wide.at[index], target(pl.ds(pl.multiple_of(first - low, 8), rows)), sems.at[index]
            )
            copies.append((inside, copy))

            @pl.when(inside)
            def _():
                copy.start()

    for inside, copy in copies:
        @pl.when(inside)
        def _():
            copy.wait()


def ffn_targets(outs, rows):
    grad_up, grad_down = outs
    units, width = grad_down.shape
    found = [(0, units, lambda spot: grad_down.at[spot, :])]
    for half in range(units // width):
        lanes = pl.ds(half * width, width)
        low = units + half * width
        found.append((low, low + width, lambda spot, lanes=lanes: grad_up.at[spot, lanes]))
    return found


def attention_targets(outs, rows):
    width, local = outs[0].shape
    found = []
    for part in range(3):
        found.append((part * width, (part + 1) * width, lambda spot, part=part: outs[part].at[spot, :]))
    for half in range(width // local):
        lanes = pl.ds(half * local, local)
        low = 3 * width + half * local
        found.append((low, low + local, lambda spot, lanes=lanes: outs[3].at[spot, lanes]))
    return found


ffn_targets.outs = 2
attention_targets.outs = 4


spaces = {"s": in_smem, "v": in_vmem, "a": in_any, "h": in_hbm}


def run(kernel, specs, outs, scratch, name, room, aliases={}):
    params = pltpu.CompilerParams(vmem_limit_bytes=room * 1024 * 1024)

    def call(*args):
        return pl.pallas_call(
            kernel,
            in_specs=[spaces[kind] for kind in specs],
            out_specs=[spaces[kind] for kind, unused in outs],
            out_shape=[pltpu.HBM(shape.shape, shape.dtype) if kind == "h" else shape for kind, shape in outs],
            scratch_shapes=scratch,
            compiler_params=params,
            input_output_aliases=aliases,
            name=name,
        )(
            *[
                pltpu.with_memory_space_constraint(arg, pltpu.HBM) if kind == "h" else arg
                for kind, arg in zip(specs, args)
            ]
        )

    return call


class Unpacker:
    def __init__(self, places, targets_of, shapes, name, parts, dp_count):
        chips = dp_count // 2
        self.places = jnp.stack([places[:chips], places[chips:]], axis=1).reshape(-1)
        self.targets_of, self.shapes, self.name = targets_of, shapes, name
        self.ends = [chips * (part + 1) // parts for part in range(parts)]
        self.done, self.made, self.tokens = 0, [], []
        self.pairs = siblings(dp_count)

    def next(self, own, earlier=()):
        first, last = self.done, self.ends[len(self.tokens)]
        pieces = []
        for piece in own[first:last]:
            pieces += [piece, lax.ppermute(piece, "dp", self.pairs)]
        rows, columns = own[0].shape
        count = len(pieces)
        *self.made, token = run(
            functools.partial(unpack, 2 * first, count, self.targets_of),
            "s" + "v" * count + "a" * (len(self.made) + len(earlier)),
            [("a", shape) for shape in self.shapes] + [("v", shape_of((8, 128), f32))],
            [pltpu.VMEM((count, rows, columns), f32), pltpu.SemaphoreType.DMA((count,))],
            f"{self.name}{len(self.tokens)}",
            8,
            {1 + count + index: index for index in range(len(self.made))},
        )(self.places, *pieces, *self.made, *earlier)
        self.tokens.append(token)
        self.done = last
        return token


def swap_tensor(value):
    return lax.ppermute(value, "tensor", ((0, 1), (1, 0)))


def exchange_within(pieces, level, least=1):
    def branch(swapped):
        return lambda *given: tuple(
            swap_tensor(piece) if index < swapped else piece for index, piece in enumerate(given)
        )

    return lax.switch(level, [branch(least + step) for step in range(len(CAPS))], *pieces)


def exchange(pieces, level):
    return swap_tensor(pieces[0]), *exchange_within(pieces[1:], level, 0)


def ring_pairs(dp_count):
    chips = dp_count // 2
    order = list(range(0, chips, 2)) + list(range(chips - 1, 0, -2))
    pairs = []
    for place, chip in enumerate(order):
        after = order[(place + 1) % chips]
        pairs.append((2 * chip, 2 * after))
        pairs.append((2 * after + 1, 2 * chip + 1))
    return tuple(pairs)


def fold_bits(chips):
    bits = [1]
    bit = chips // 2
    while bit > 1:
        bits.append(bit)
        bit //= 2
    return bits


def ring_places(dp_count):
    chips = dp_count // 2
    index = lax.axis_index("dp")
    chip, core = index // 2, index % 2
    position = lambda at: jnp.where(at % 2 == 0, at // 2, chips - 1 - at // 2)
    steps = jnp.arange(chips, dtype=jnp.int32)
    mine, theirs = core * chips, (1 - core) * chips
    offsets = [
        sum(bit for step, bit in enumerate(fold_bits(chips)) if slot & (chips >> (step + 1))) for slot in range(chips)
    ]
    targets = position(chip ^ jnp.array(offsets, jnp.int32))
    turn = steps * (1 - 2 * core)
    own_chunks = mine + (position(chip) - turn) % chips
    other_chunks = theirs + (position(chip) + turn) % chips
    slots = jnp.concatenate([mine + targets, theirs + targets])
    return slots.astype(jnp.int32), jnp.concatenate([own_chunks, other_chunks]).astype(jnp.int32)


def siblings(dp_count):
    return tuple((i, i ^ 1) for i in range(dp_count))


def fold(parts, stage, dp_count, room, name):
    keep, give = parts
    if stage == 0:
        pairs = siblings(dp_count)
    else:
        distance = 2 * fold_bits(dp_count // 2)[stage - 1]
        pairs = tuple((i, i ^ distance) for i in range(dp_count))
    got = lax.ppermute(give, "dp", pairs)
    count = keep.shape[0]
    halves = [count // 2, count // 2] if count > 1 else [1]
    outs = [("v", shape_of((half, *keep.shape[1:]), bf16)) for half in halves]
    return run(add_halves, "vv", outs, [], f"{name}{stage}", room)(keep, got)


def gather_both(first, second, dp_count, fill):
    pairs = ring_pairs(dp_count)
    one, two = [first], [second]
    for step in range(dp_count // 2 - 1):
        moving = after(one[step], *two[: step][-1:], *fill(step, one, two))
        one.append(lax.ppermute(moving, "dp", pairs))
        moving = after(two[step], one[step])
        two.append(lax.ppermute(moving, "dp", pairs))
    return one, two


def later(parts, *earlier):
    return after(parts[0], *earlier), parts[1]


def after(value, *earlier):
    return lax.optimization_barrier((value, earlier))[0]


def add_small(value, bit, mark, dp_count):
    got = lax.ppermute(value, "dp", tuple((i, i ^ bit) for i in range(dp_count)))
    return value + after(got, mark)


def per_device(dp_count, *arrays):
    (
        inputs, lengths, buckets, w_query, b_query, w_key, w_value, b_value, w_out, b_out, norm1_gain, norm1_shift,
        w_up, b_up, w_down, b_down, norm2_gain, norm2_shift, position_table, cotangent,
    ) = arrays
    micro, seqs, seq_len, width = inputs.shape
    bucket_count, heads = position_table.shape
    local = w_query.shape[1]
    units = w_up.shape[1]
    chips = dp_count // 2
    rows = micro * seq_len
    x = inputs.reshape(micro, seq_len, width)
    grad_out = cotangent.reshape(micro, seq_len, width)
    sizes = lengths[:, 0]
    blocks = jnp.where(sizes <= BLOCK, 1, jnp.where(sizes <= 2 * BLOCK, 2, 4))
    used = blocks[0] + blocks[1]
    level = sum((used > most).astype(jnp.int32) for most in CAPS[:-1])
    cap = CAPS[0]
    for step, most in enumerate(CAPS):
        cap = jnp.where(level >= step, most, cap)
    meta = jnp.stack([blocks[0], blocks[1], sizes[0], sizes[1], used, cap, cap, cap]).astype(jnp.int32)
    slots, places = ring_places(dp_count)
    buckets_t = buckets.T
    table = position_table.T
    row = lambda vector: vector.reshape(1, -1)
    ends = [0, *(most * BLOCK for most in CAPS[:-1]), rows]
    piece_rows = [last - first for first, last in zip(ends, ends[1:])]
    pieces = lambda columns: [("a", shape_of((count, columns), bf16)) for count in piece_rows]
    vmem = pltpu.VMEM
    dma = pltpu.SemaphoreType.DMA

    w_out_got = swap_tensor(w_out)
    blocks_most = rows // BLOCK
    query3, value3, key_t, probs_t, *attended = run(
        attention_forward,
        "shhvhhvvv",
        [
            ("h", shape_of((heads // 2, rows, 128), bf16)),
            ("h", shape_of((heads // 2, rows, 128), bf16)),
            ("h", shape_of((local, rows), bf16)),
            ("h", shape_of((heads, rows, seq_len), bf16)),
            *pieces(local),
        ],
        [
            vmem((rows, width), bf16),
            *[vmem((width, local), bf16)] * 3,
            *[vmem((heads // 2, rows, 128), bf16)] * 3,
            vmem((local, rows), bf16),
            vmem((heads, rows, seq_len), bf16),
            vmem((heads, seq_len, seq_len), f32),
            vmem((local, rows), bf16),
            vmem((local, rows), f32),
            vmem((rows, local), bf16),
            dma((len(CAPS),)),
            dma((blocks_most,)),
            dma((3,)),
            dma((3, blocks_most)),
            dma((2, heads)),
        ],
        "attention_forward",
        27,
    )(meta, x, w_query, row(b_query), w_key, w_value, row(b_value), buckets_t, table)
    attended_got = exchange(attended, level)

    normed1, inverse1, hidden_low, activated, slope, *unit_part = run(
        feed_forward,
        "shaaaaaaaahhvvvhvh",
        [
            ("h", shape_of((rows, width), f32)),
            ("h", shape_of((rows, 128), f32)),
            ("h", shape_of((rows, width), bf16)),
            ("h", shape_of((rows, units), bf16)),
            ("h", shape_of((rows, units), bf16)),
            *pieces(width),
        ],
        [
            vmem((rows, local), bf16),
            vmem((rows, local), bf16),
            vmem((rows, width), bf16),
            vmem((rows, width), bf16),
            vmem((local, width), bf16),
            vmem((local, width), bf16),
            vmem((width, units), bf16),
            vmem((units, width), bf16),
            vmem((rows, width), f32),
            vmem((rows, 128), f32),
            vmem((rows, width), bf16),
            vmem((rows, units), bf16),
            vmem((rows, units), bf16),
            dma((2, len(CAPS))),
            dma((blocks_most,)),
            dma((4,)),
            dma((5, blocks_most)),
        ],
        "feed_forward",
        26,
    )(
        meta, x, *attended, *attended_got, w_out, w_out_got, row(b_out), row(norm1_gain), row(norm1_shift),
        w_up, row(b_up), w_down,
    )
    unit_got = exchange(unit_part, level)

    layer_output, grad_y2, grad_ffn, grad_upper, sums2, sums_up, *hidden_part = run(
        second_norm,
        "shaaaaaaaahvvvvvhhh",
        [
            ("h", shape_of((micro, seq_len, width), bf16)),
            ("h", shape_of((rows, width), f32)),
            ("v", shape_of((rows, width), bf16)),
            ("v", shape_of((rows, units), bf16)),
            ("v", shape_of((8, width), f32)),
            ("v", shape_of((1, units), f32)),
            *pieces(width),
        ],
        [
            vmem((rows, width), bf16),
            vmem((rows, width), bf16),
            vmem((rows, width), bf16),
            vmem((rows, width), f32),
            vmem((rows, width), bf16),
            vmem((units, width), bf16),
            vmem((width, units), bf16),
            vmem((rows, units), bf16),
            vmem((micro, seq_len, width), bf16),
            vmem((rows, width), f32),
            dma((2, len(CAPS))),
            dma((3, blocks_most)),
            dma((2,)),
            dma((blocks_most,)),
            dma((1,)),
        ],
        "second_norm",
        26,
    )(
        meta, grad_out, *unit_part, *unit_got, normed1, row(norm1_gain), row(norm1_shift), row(b_down),
        row(norm2_gain), row(norm2_shift), w_down, w_up, slope,
    )
    stacked_ffn = 2 * units
    ffn_parts = run(
        ffn_weights,
        "ssvvvv",
        [("v", shape_of((chips, stacked_ffn // (2 * chips), width), bf16))] * 2,
        [vmem((stacked_ffn, width), f32)],
        "ffn_weights",
        14,
    )(meta, slots, activated, grad_ffn, hidden_low, grad_upper)
    hidden_got = exchange_within(hidden_part, after(level, ffn_parts[0]))
    ffn_parts = fold(later(ffn_parts, hidden_got[0]), 0, dp_count, 8, "ffn_fold")

    grad_y1, grad_branch, grad_qkv, grad_scores_t, sums1, sums_qv, input_part = run(
        attention_backward,
        "saaaaaaaahhhvhhhhhhhh",
        [
            ("v", shape_of((rows, width), f32)),
            ("v", shape_of((rows, width), bf16)),
            ("v", shape_of((rows, 3 * local), bf16)),
            ("h", shape_of((heads, rows, seq_len), bf16)),
            ("v", shape_of((8, width), f32)),
            ("v", shape_of((8, local), f32)),
            ("v", shape_of((rows, width), bf16)),
        ],
        [
            vmem((rows, width), bf16),
            vmem((rows, width), bf16),
            vmem((heads // 2, rows, 128), bf16),
            vmem((local, rows), f32),
            vmem((heads // 2, rows, 128), f32),
            vmem((heads // 2, rows, 128), f32),
            vmem((rows, width), f32),
            vmem((rows, width), f32),
            vmem((rows, 128), f32),
            vmem((local, width), bf16),
            *[vmem((width, local), bf16)] * 3,
            *[vmem((heads // 2, rows, 128), bf16)] * 2,
            vmem((local, rows), bf16),
            vmem((heads, rows, seq_len), bf16),
            dma((2, len(CAPS))),
            dma((6, blocks_most)),
            dma((4,)),
            dma((2, heads)),
            dma((2, heads)),
        ],
        "attention_backward",
        32,
    )(
        after(meta, ffn_parts[0]), *hidden_part, *hidden_got, grad_y2, normed1, inverse1, row(norm1_gain), w_out, w_query, w_key, w_value,
        query3, value3, key_t, probs_t,
    )
    input_got = swap_tensor(input_part)

    stacked_attention = 3 * width + width * local // local
    attention_parts = run(
        attention_weights,
        "sshvaaaav",
        [("v", shape_of((chips, stacked_attention // (2 * chips), local), bf16))] * 2,
        [
            vmem((stacked_attention, local), f32),
            vmem((rows, local), bf16),
            vmem((rows, width), bf16),
            dma((len(CAPS),)),
            dma((blocks_most,)),
        ],
        "attention_weights",
        11,
    )(meta, slots, x, grad_qkv, *attended, grad_branch)

    table_sums = []

    def add_table(earlier):
        part = len(table_sums)
        table_sums.extend(
            run(
                functools.partial(table_histogram, part),
                "svv",
                [("v", shape_of((8 * heads, 32), f32))],
                [vmem((32, 16 * seq_len), bf16), vmem((8 * heads, 16 * seq_len), bf16)],
                f"table_histogram{part}",
                10,
            )(after(meta, *earlier), grad_scores_t, buckets_t)
        )

    stages = len(fold_bits(chips)) + 1
    ffn_parts = fold(later(ffn_parts, attention_parts[0]), 1, dp_count, 8, "ffn_fold")
    attention_parts = later(attention_parts, ffn_parts[0])
    for stage in range(stages):
        attention_parts = fold(later(attention_parts, *table_sums[-1:]), stage, dp_count, 4, "attention_fold")
        if stage == 0:
            add_table(attention_parts)
        elif stage + 1 < stages:
            ffn_parts = fold(later(ffn_parts, attention_parts[0]), stage + 1, dp_count, 8, "ffn_fold")
        for unused in range((3, 2)[stage] if stage < 2 else 0):
            add_table([*attention_parts, table_sums[-1]])
    attention_own = attention_parts[0][0]
    unpack_up = Unpacker(
        places,
        ffn_targets,
        [shape_of((width, units), f32), shape_of((units, width), f32)],
        "unpack_ffn",
        UNPACK_PARTS,
        dp_count,
    )
    unpack_heads = Unpacker(
        places,
        attention_targets,
        [shape_of((width, local), f32)] * 3 + [shape_of((local, width), f32)],
        "unpack_attention",
        2,
        dp_count,
    )

    table_rows = 8 * heads
    vector_rows = (6 * width + units + 2 * local) // 128
    small_rows = -(-vector_rows // 8) * 8 + table_rows
    (small,) = run(
        pack_small,
        "v" * (4 + TABLE_PARTS),
        [("v", shape_of((small_rows, 128), f32))],
        [],
        "pack_small",
        4,
    )(sums2, sums_up, sums1, sums_qv, *table_sums)
    sums = [small]
    small_steps = dp_count.bit_length() - 1

    def fill(step, pieces, gathered):
        waits = []
        if 0 < step <= small_steps:
            sums.append(add_small(sums[-1], 1 << (step - 1), gathered[step - 1], dp_count))
        if step <= small_steps:
            waits.append(sums[-1])
        if step in (3 * chips // 8, 5 * chips // 8, 6 * chips // 8):
            waits.append(unpack_up.next(pieces))
        return waits

    ffn_pieces, attention_pieces = gather_both(ffn_parts[0][0], attention_own, dp_count, fill)
    unpack_up.next(ffn_pieces)
    unpack_heads.next(attention_pieces, unpack_up.tokens)
    unpack_heads.next(attention_pieces)
    grad_w_up, grad_w_down = unpack_up.made
    grad_w_query, grad_w_key, grad_w_value, grad_w_out = unpack_heads.made

    (grad_inputs,) = run(
        input_gradient,
        "svvv",
        [("v", shape_of((micro, seq_len, width), f32))],
        [],
        "input_gradient",
        12,
    )(meta, grad_y1, input_part, input_got)

    small = sums[-1]
    table_grad = small[small_rows - table_rows :, :32].reshape(heads, 8, 32).transpose(2, 1, 0)
    small = small[:vector_rows].reshape(-1)
    cuts = []
    start = 0
    for count in (width, width, width, units, width, width, width, local, local):
        cuts.append(small[start : start + count])
        start += count
    grad_gain2, grad_shift2, grad_b_down, grad_b_up, grad_gain1, grad_shift1, grad_b_out, grad_b_query, grad_b_value = cuts
    return (
        layer_output.reshape(inputs.shape),
        grad_inputs.reshape(inputs.shape),
        grad_w_query,
        grad_b_query,
        grad_w_key,
        grad_w_value,
        grad_b_value,
        grad_w_out,
        grad_b_out,
        grad_gain1,
        grad_shift1,
        grad_w_up,
        grad_b_up,
        grad_w_down,
        grad_b_down,
        grad_gain2,
        grad_shift2,
        table_grad.reshape(bucket_count, heads),
    )


def solution(mesh):
    placed = (
        P(None, "dp", None, None),
        P(None, "dp"),
        P(),
        P(None, "tensor"),
        P("tensor"),
        P(None, "tensor"),
        P(None, "tensor"),
        P("tensor"),
        P("tensor", None),
        P(),
        P(),
        P(),
        P(None, "tensor"),
        P("tensor"),
        P("tensor", None),
        P(),
        P(),
        P(),
        P(None, "tensor"),
        P(None, "dp", None, None),
    )
    dp_count = mesh.shape["dp"]
    return jax.shard_map(
        lambda *arrays: per_device(dp_count, *arrays),
        mesh=mesh,
        in_specs=placed,
        out_specs=(
            P(None, "dp", None, None),
            P(None, "dp", None, None),
            P(None, "tensor"),
            P("tensor"),
            P(None, "tensor"),
            P(None, "tensor"),
            P("tensor"),
            P("tensor", None),
            P(),
            P(),
            P(),
            P(None, "tensor"),
            P("tensor"),
            P("tensor", None),
            P(),
            P(),
            P(),
            P(None, "tensor"),
        ),
        check_vma=False,
    )
```

```python
import functools

import jax
import jax.numpy as jnp
from jax import lax
from jax.experimental import pallas as pl
from jax.experimental.pallas import tpu as pltpu
from jax.sharding import PartitionSpec as P

epsilon = 1e-05
masked_value = -1e30
inv_root_two = 0.7071067811865476
inv_root_tau = 0.3989422804014327

BLOCK = 128
CAPS = (2, 5, 6, 8)
TABLE_PARTS = 6
UNPACK_PARTS = 4
bf16 = jnp.bfloat16
f32 = jnp.float32
shape_of = jax.ShapeDtypeStruct

in_vmem = pl.BlockSpec(memory_space=pltpu.VMEM)
in_smem = pl.BlockSpec(memory_space=pltpu.SMEM)
in_any = pl.BlockSpec(memory_space=pl.ANY)
in_hbm = pl.BlockSpec(memory_space=pltpu.HBM)


def rows_at(block, count=1):
    return pl.ds(pl.multiple_of(block * BLOCK, BLOCK), count * BLOCK)


def dot_nn(left, right):
    return lax.dot_general(left, right, (((1,), (0,)), ((), ())), preferred_element_type=f32)


def dot_nt(left, right):
    return lax.dot_general(left, right, (((1,), (1,)), ((), ())), preferred_element_type=f32)


def dot_tn(left, right):
    return lax.dot_general(left, right, (((0,), (0,)), ((), ())), preferred_element_type=f32)


def block_table(lengths, meta):
    used = jnp.int32(0)
    for second in range(2):
        size = lengths[second, 0]
        blocks = jnp.where(size <= BLOCK, 1, jnp.where(size <= 2 * BLOCK, 2, 4)).astype(jnp.int32)
        meta[second] = blocks
        meta[2 + second] = size
        used = used + blocks
    level, cap = jnp.int32(0), jnp.int32(CAPS[0])
    for step, most in enumerate(CAPS[:-1]):
        over = used > most
        level = jnp.where(over, step + 1, level).astype(jnp.int32)
        cap = jnp.where(over, CAPS[step + 1], cap).astype(jnp.int32)
    meta[4] = used
    meta[5] = cap
    meta[6] = level
    meta[7] = cap


def place_of(meta, block):
    second = (block >= meta[0]).astype(jnp.int32)
    return second, pl.multiple_of((block - second * meta[0]) * BLOCK, BLOCK)


def live_rows(meta, second, first_row):
    rows = lax.broadcasted_iota(jnp.int32, (BLOCK, 1), 0) + first_row
    return rows < meta[2 + second]


def zero_tail(meta, ref):
    def clear(block, unused):
        ref[rows_at(block), :] = jnp.zeros((BLOCK, ref.shape[1]), ref.dtype)
        return unused

    lax.fori_loop(meta[4], meta[5], clear, 0)


def piece_copies(meta, pieces, whole, sems, to_pieces):
    start = 0
    made = []
    for index, piece in enumerate(pieces):
        rows = piece.shape[0]
        part = whole.at[pl.ds(start, rows), :]
        pair = (part, piece) if to_pieces else (piece, part)
        made.append((start // BLOCK, pltpu.make_async_copy(pair[0], pair[1], sems.at[index])))
        start += rows
    return made


def start_copies(meta, made):
    for first, copy in made:
        @pl.when(meta[5] > first)
        def _():
            copy.start()


def wait_copies(meta, made):
    for first, copy in made:
        @pl.when(meta[5] > first)
        def _():
            copy.wait()


def over_blocks(first, last, makers, act):
    def one(block, unused):
        for maker in makers:
            act(maker(block))
        return unused

    lax.fori_loop(first, last, one, 0)


def start(copy):
    copy.start()


def wait(copy):
    copy.wait()


def rows_copy(source, target, sems):
    return lambda block: pltpu.make_async_copy(source.at[rows_at(block), :], target.at[rows_at(block), :], sems.at[block])


def pairs_copy(source, target, sems):
    return lambda block: pltpu.make_async_copy(
        source.at[:, rows_at(block), :], target.at[:, rows_at(block), :], sems.at[block]
    )


def lanes_copy(source, target, sems):
    return lambda block: pltpu.make_async_copy(source.at[:, rows_at(block)], target.at[:, rows_at(block)], sems.at[block])


def packing_copy(meta, source, target, sems):
    def maker(block):
        second, first_row = place_of(meta, block)
        return pltpu.make_async_copy(
            source.at[second, pl.ds(first_row, BLOCK), :], target.at[rows_at(block), :], sems.at[block]
        )

    return maker


def probs_copy(source, target, sems, second, head, offset, blocks):
    spot = rows_at(offset, blocks)
    lanes = pl.ds(0, blocks * BLOCK)
    return pltpu.make_async_copy(
        source.at[head, spot, lanes], target.at[head, spot, lanes], sems.at[second, head]
    )


def over_probs(meta, source, target, sems, act):
    def one_sequence(second, unused):
        def sized(blocks):
            def one_head(head, unused):
                act(probs_copy(source, target, sems, second, head, second * meta[0], blocks))
                return unused

            lax.fori_loop(0, source.shape[0], one_head, 0)

        by_length(meta, second, sized)
        return unused

    lax.fori_loop(0, 2, one_sequence, 0)


def by_length(meta, second, body):
    for blocks in (1, 2, 4):
        @pl.when(meta[second] == blocks)
        def _():
            body(blocks)


def by_cap(meta, body):
    for blocks in CAPS:
        @pl.when(meta[5] == blocks)
        def _():
            body(blocks * BLOCK)


def norm_forward(rows, gain, shift):
    centre = rows - jnp.mean(rows, axis=-1, keepdims=True)
    inverse = lax.rsqrt(jnp.mean(centre * centre, axis=-1, keepdims=True) + epsilon)
    normed = centre * inverse
    return normed, normed * gain + shift, inverse


def norm_back(grad_rows, normed, inverse, gain):
    scaled = grad_rows * gain
    first_mean = jnp.mean(scaled, axis=-1, keepdims=True)
    second_mean = jnp.mean(scaled * normed, axis=-1, keepdims=True)
    return inverse * (scaled - first_mean - normed * second_mean)


def attention_forward(
    meta, x, w_query_in, b_query, w_key_in, w_value_in, b_value, buckets, table,
    query_out, value_out, key_t_out, probs_out, piece0, piece1, piece2, piece3,
    packed_x, w_query, w_key, w_value, query3, key3, value3, key_t, probs_t,
    bias, value_t, attended_t, attended, sems, in_sems, weight_sems, out_sems, probs_sems,
):
    weights = [
        pltpu.make_async_copy(source, target, weight_sems.at[index])
        for index, (source, target) in enumerate(((w_query_in, w_query), (w_key_in, w_key), (w_value_in, w_value)))
    ]
    for copy in weights:
        copy.start()
    x_copy = packing_copy(meta, x, packed_x, in_sems)
    over_blocks(0, meta[4], [x_copy], start)
    outward = [
        pairs_copy(query3, query_out, out_sems.at[0]),
        pairs_copy(value3, value_out, out_sems.at[1]),
        lanes_copy(key_t, key_t_out, out_sems.at[2]),
    ]
    heads = probs_t.shape[0]
    pairs = heads // 2
    scale = 0.125
    seq_len = buckets.shape[1]
    columns = seq_len // BLOCK

    def bias_rows(group, unused):
        rows = pl.ds(pl.multiple_of(group * 8, 8), 8)
        for column in range(columns):
            lanes = slice(column * BLOCK, (column + 1) * BLOCK)
            bucket = buckets[rows, lanes]
            low = bucket & 127
            upper = bucket >= 128
            for head in range(heads):
                first = jnp.broadcast_to(table[head : head + 1, :128], (8, 128))
                second = jnp.broadcast_to(table[head : head + 1, 128:], (8, 128))
                bias[head, rows, lanes] = jnp.where(
                    upper,
                    jnp.take_along_axis(second, low, axis=1, mode="promise_in_bounds"),
                    jnp.take_along_axis(first, low, axis=1, mode="promise_in_bounds"),
                )
        return unused

    lax.fori_loop(0, jnp.maximum(meta[0], meta[1]) * (BLOCK // 8), bias_rows, 0)

    for copy in weights:
        copy.wait()

    def project(block, unused):
        rows = rows_at(block)
        x_copy(block).wait()
        part = packed_x[rows, :]
        query = ((dot_nn(part, w_query[...]) + b_query[...]).astype(bf16).astype(f32) * scale).astype(bf16)
        key = dot_nn(part, w_key[...])
        value = dot_nn(part, w_value[...]) + b_value[...]
        key_t[:, rows] = key.T.astype(bf16)
        value_t[:, rows] = value.T.astype(bf16)
        key = key.astype(bf16)
        value = value.astype(bf16)
        for pair in range(pairs):
            lanes = slice(pair * 128, (pair + 1) * 128)
            query3[pair, rows, :] = query[:, lanes]
            key3[pair, rows, :] = key[:, lanes]
            value3[pair, rows, :] = value[:, lanes]
        for maker in outward:
            maker(block).start()
        return unused

    lax.fori_loop(0, meta[4], project, 0)

    def one_sequence(second, unused):
        offset = second * meta[0]
        length = meta[2 + second]

        def sized(blocks):
            count = blocks * BLOCK
            wide = min(count, 256)

            def one_head(head, unused):
                pair = head // 2
                lane = lax.broadcasted_iota(jnp.int32, (count, 128), 1)
                mine = (lane >= 64) == (head % 2 == 1)
                keys = jnp.where(mine, key3[pair, rows_at(offset, blocks), :], jnp.zeros((), bf16))
                values = value_t[pl.ds(pl.multiple_of(head * 64, 64), 64), rows_at(offset, blocks)]
                live = lax.broadcasted_iota(jnp.int32, (count, wide), 0) < length
                for column in range(count // wide):
                    lanes = slice(column * wide, (column + 1) * wide)
                    places = rows_at(offset + column * (wide // BLOCK), wide // BLOCK)
                    scores = dot_nt(keys, query3[pair, places, :]) + bias[head, :count, lanes]
                    scores = jnp.where(live, scores, masked_value)
                    top = jnp.max(scores, axis=0, keepdims=True)
                    powers = jnp.exp(scores - top)
                    total = jnp.sum(powers, axis=0, keepdims=True)
                    probs = (powers * (1.0 / total)).astype(bf16)
                    probs_t[head, rows_at(offset, blocks), lanes] = probs
                    attended_t[pl.ds(pl.multiple_of(head * 64, 64), 64), places] = dot_nn(values, probs)
                probs_copy(probs_t, probs_out, probs_sems, second, head, offset, blocks).start()
                return unused

            lax.fori_loop(0, heads, one_head, 0)

        by_length(meta, second, sized)
        return unused

    lax.fori_loop(0, 2, one_sequence, 0)

    def turn(block, unused):
        attended[rows_at(block), :] = attended_t[:, rows_at(block)].T.astype(bf16)
        return unused

    lax.fori_loop(0, meta[4], turn, 0)
    zero_tail(meta, attended)
    made = piece_copies(meta, (piece0, piece1, piece2, piece3), attended, sems, True)
    start_copies(meta, made)
    over_blocks(0, meta[4], outward, wait)
    over_probs(meta, probs_t, probs_out, probs_sems, wait)
    wait_copies(meta, made)


def feed_forward(
    meta, x, own0, own1, own2, own3, got0, got1, got2, got3, w_out_own_in, w_out_got_in, b_out, gain, shift,
    w_up_in, b_up, w_down_in,
    normed_out, inverse_out, hidden_out, activated_out, slope_out, piece0, piece1, piece2, piece3,
    own, got, part, packed_x, w_out_own, w_out_got, w_up, w_down, normed1, inverse1, hidden_low, activated, slope,
    sems, in_sems, weight_sems, out_sems,
):
    own_copies = piece_copies(meta, (own0, own1, own2, own3), own, sems.at[0], False)
    got_copies = piece_copies(meta, (got0, got1, got2, got3), got, sems.at[1], False)
    start_copies(meta, own_copies)
    start_copies(meta, got_copies)
    sources = (w_out_own_in, w_out_got_in, w_up_in, w_down_in)
    weights = [
        pltpu.make_async_copy(source, target, weight_sems.at[index])
        for index, (source, target) in enumerate(zip(sources, (w_out_own, w_out_got, w_up, w_down)))
    ]
    x_copy = packing_copy(meta, x, packed_x, in_sems)
    weights[0].start()
    weights[1].start()
    over_blocks(0, meta[4], [x_copy], start)
    weights[2].start()
    weights[3].start()
    inverse_copy = rows_copy(inverse1, inverse_out, out_sems.at[0])
    hidden_copy = rows_copy(hidden_low, hidden_out, out_sems.at[1])
    activated_copy = rows_copy(activated, activated_out, out_sems.at[2])
    slope_copy = rows_copy(slope, slope_out, out_sems.at[3])
    normed_copy = rows_copy(normed1, normed_out, out_sems.at[4])
    wait_copies(meta, own_copies)
    wait_copies(meta, got_copies)
    weights[0].wait()
    weights[1].wait()
    width = w_up.shape[1]

    def first_norm(block, unused):
        rows = rows_at(block)
        head_own = dot_nn(own[rows, :], w_out_own[...]).astype(bf16).astype(f32)
        head_got = dot_nn(got[rows, :], w_out_got[...]).astype(bf16).astype(f32)
        branch = (head_own + head_got) + b_out[...]
        x_copy(block).wait()
        base = packed_x[rows, :].astype(f32) + branch
        normed, hidden, inverse = norm_forward(base, gain[...], shift[...])
        normed1[rows, :] = normed
        inverse1[rows, :] = jnp.broadcast_to(inverse, (BLOCK, 128))
        hidden_low[rows, :] = hidden.astype(bf16)
        normed_copy(block).start()
        inverse_copy(block).start()
        hidden_copy(block).start()
        return unused

    lax.fori_loop(0, meta[4], first_norm, 0)
    weights[2].wait()
    weights[3].wait()

    def one_block(block, unused):
        rows = rows_at(block)
        low = hidden_low[rows, :]
        for column in range(width // 512):
            lanes = slice(column * 512, (column + 1) * 512)
            upper = dot_nn(low, w_up[:, lanes]) + b_up[:, lanes]
            normal = 0.5 * (1.0 + lax.erf(upper * inv_root_two))
            activated[rows, lanes] = (upper * normal).astype(bf16)
            slope[rows, lanes] = (
                normal + upper * inv_root_tau * jnp.exp(-0.5 * upper * upper)
            ).astype(bf16)
        activated_copy(block).start()
        slope_copy(block).start()
        part[rows, :] = dot_nn(activated[rows, :], w_down[...]).astype(bf16)
        return unused

    lax.fori_loop(0, meta[4], one_block, 0)
    zero_tail(meta, part)
    made = piece_copies(meta, (piece0, piece1, piece2, piece3), part, sems.at[0], True)
    start_copies(meta, made)
    zero_tail(meta, activated)
    zero_tail(meta, hidden_low)
    over_blocks(meta[4], meta[5], [activated_copy, hidden_copy], start)
    over_blocks(0, meta[5], [activated_copy, hidden_copy], wait)
    over_blocks(0, meta[4], [normed_copy, inverse_copy, slope_copy], wait)
    wait_copies(meta, made)


def second_norm(
    meta, cotangent, own0, own1, own2, own3, got0, got1, got2, got3, normed_in, gain1, shift1, b_down, gain2, shift2,
    w_down_in, w_up_in, slope_in,
    layer_out, grad_y2_out, grad_ffn, grad_upper, sums, sums_up, piece0, piece1, piece2, piece3,
    own, got, part, normed1, packed_grad, w_down, w_up, slope, layer_output, grad_y2,
    sems, in_sems, weight_sems, out_sems, layer_sem,
):
    own_copies = piece_copies(meta, (own0, own1, own2, own3), own, sems.at[0], False)
    got_copies = piece_copies(meta, (got0, got1, got2, got3), got, sems.at[1], False)
    start_copies(meta, own_copies)
    start_copies(meta, got_copies)
    weights = [
        pltpu.make_async_copy(source, target, weight_sems.at[index])
        for index, (source, target) in enumerate(((w_down_in, w_down), (w_up_in, w_up)))
    ]
    grad_copy = packing_copy(meta, cotangent, packed_grad, in_sems.at[0])
    slope_copy = rows_copy(slope_in, slope, in_sems.at[1])
    y2_copy = rows_copy(grad_y2, grad_y2_out, out_sems)
    normed_copy = rows_copy(normed_in, normed1, in_sems.at[2])
    over_blocks(0, meta[4], [normed_copy, grad_copy], start)
    weights[0].start()
    over_blocks(0, meta[4], [slope_copy], start)
    weights[1].start()
    sums[...] = jnp.zeros(sums.shape, f32)
    sums_up[...] = jnp.zeros(sums_up.shape, f32)
    layer_output[...] = jnp.zeros(layer_output.shape, bf16)
    wait_copies(meta, own_copies)
    wait_copies(meta, got_copies)
    width = w_up.shape[1]

    def norm_block(block, unused):
        second, first_row = place_of(meta, block)
        rows = rows_at(block)
        spot = pl.ds(first_row, BLOCK)
        live = live_rows(meta, second, first_row)
        ffn_out = (own[rows, :].astype(f32) + got[rows, :].astype(f32)) + b_down[...]
        normed_copy(block).wait()
        hidden = normed1[rows, :] * gain1[...] + shift1[...]
        normed, result, inverse = norm_forward(hidden + ffn_out, gain2[...], shift2[...])
        layer_output[second, spot, :] = jnp.where(live, result, 0.0).astype(bf16)
        grad_copy(block).wait()
        grad_result = jnp.where(live, packed_grad[rows, :].astype(f32), 0.0)
        sums[0:1, :] += jnp.sum(grad_result * normed, axis=0, keepdims=True)
        sums[1:2, :] += jnp.sum(grad_result, axis=0, keepdims=True)
        grad = norm_back(grad_result, normed, inverse, gain2[...])
        grad_y2[rows, :] = grad
        y2_copy(block).start()
        low = grad.astype(bf16)
        grad_ffn[rows, :] = low
        sums[2:3, :] += jnp.sum(low.astype(f32), axis=0, keepdims=True)
        return unused

    lax.fori_loop(0, meta[4], norm_block, 0)
    layer_copy = pltpu.make_async_copy(layer_output, layer_out, layer_sem.at[0])
    layer_copy.start()
    for copy in weights:
        copy.wait()

    def one_block(block, unused):
        rows = rows_at(block)
        low = grad_ffn[rows, :]
        slope_copy(block).wait()
        for column in range(width // 512):
            lanes = slice(column * 512, (column + 1) * 512)
            back = dot_nt(low, w_down[lanes, :]) * slope[rows, lanes].astype(f32)
            back = back.astype(bf16)
            grad_upper[rows, lanes] = back
            sums_up[:, lanes] += jnp.sum(back.astype(f32), axis=0, keepdims=True)
        part[rows, :] = dot_nt(grad_upper[rows, :], w_up[...]).astype(bf16)
        return unused

    lax.fori_loop(0, meta[4], one_block, 0)
    zero_tail(meta, part)
    made = piece_copies(meta, (piece0, piece1, piece2, piece3), part, sems.at[0], True)
    start_copies(meta, made)
    zero_tail(meta, grad_ffn)
    zero_tail(meta, grad_upper)
    over_blocks(0, meta[4], [y2_copy], wait)
    layer_copy.wait()
    wait_copies(meta, made)


def ffn_weights(meta, slots, activated, grad_ffn, hidden_low, grad_upper, keep, give, stacked):
    width = grad_ffn.shape[1]
    units = activated.shape[1]

    def sized(count):
        def down(tile, unused):
            lanes = pl.ds(pl.multiple_of(tile * 256, 256), 256)
            stacked[lanes, :] = dot_tn(activated[:count, lanes], grad_ffn[:count, :])
            return unused

        lax.fori_loop(0, units // 256, down, 0)

        def up(tile, unused):
            lanes = pl.ds(pl.multiple_of(tile * 256, 256), 256)
            product = dot_tn(hidden_low[:count, lanes], grad_upper[:count, :])
            for half in range(units // width):
                spot = pl.ds(pl.multiple_of(units + half * width + tile * 256, 256), 256)
                stacked[spot, :] = product[:, half * width : (half + 1) * width]
            return unused

        lax.fori_loop(0, width // 256, up, 0)

    by_cap(meta, sized)
    scatter_chunks(slots, keep, give, stacked)


def scatter_chunks(slots, keep, give, stacked):
    chips, rows, unused = keep.shape

    def move(index, unused):
        for first, target in ((0, keep), (chips, give)):
            spot = pl.ds(pl.multiple_of(slots[first + index] * rows, 8), rows)
            target[index] = stacked[spot, :].astype(bf16)
        return unused

    lax.fori_loop(0, chips, move, 0)


def add_halves(keep, got, *outs):
    count = outs[0].shape[0]
    for index in range(keep.shape[0]):
        total = keep[index].astype(f32) + got[index].astype(f32)
        outs[index // count][index % count] = total.astype(bf16)


def attention_backward(
    meta, own0, own1, own2, own3, got0, got1, got2, got3, grad_y2_in, normed_in, inverse_in, gain1,
    w_out_in, w_query_in, w_key_in, w_value_in, query_in, value_in, key_t_in, probs_in,
    grad_y1, grad_branch, grad_qkv, grad_scores_out, sums, sums_qv, part,
    own, got, grad_attended, grad_query_t, grad_key, grad_value,
    grad_y2, normed1, inverse1, w_out, w_query, w_key, w_value, query3, value3, key_t, probs_t,
    sems, in_sems, weight_sems, probs_sems, scores_sems,
):
    own_copies = piece_copies(meta, (own0, own1, own2, own3), own, sems.at[0], False)
    got_copies = piece_copies(meta, (got0, got1, got2, got3), got, sems.at[1], False)
    start_copies(meta, own_copies)
    start_copies(meta, got_copies)
    sources = (w_out_in, w_query_in, w_key_in, w_value_in)
    weights = [
        pltpu.make_async_copy(source, target, weight_sems.at[index])
        for index, (source, target) in enumerate(zip(sources, (w_out, w_query, w_key, w_value)))
    ]
    weights[0].start()
    row_copies = [
        rows_copy(grad_y2_in, grad_y2, in_sems.at[0]),
        rows_copy(inverse_in, inverse1, in_sems.at[1]),
        rows_copy(normed_in, normed1, in_sems.at[5]),
    ]
    over_blocks(0, meta[4], row_copies, start)
    inward = [
        pairs_copy(value_in, value3, in_sems.at[2]),
        lanes_copy(key_t_in, key_t, in_sems.at[3]),
        pairs_copy(query_in, query3, in_sems.at[4]),
    ]
    over_blocks(0, meta[4], inward, start)
    over_probs(meta, probs_in, probs_t, probs_sems, start)
    for copy in weights[1:]:
        copy.start()
    sums[...] = jnp.zeros(sums.shape, f32)
    sums_qv[...] = jnp.zeros(sums_qv.shape, f32)
    wait_copies(meta, own_copies)
    wait_copies(meta, got_copies)
    weights[0].wait()
    heads = probs_t.shape[0]
    pairs = heads // 2
    local = heads * 64
    scale = 0.125

    def first_norm(block, unused):
        rows = rows_at(block)
        for maker in row_copies:
            maker(block).wait()
        grad_hidden = (own[rows, :].astype(f32) + got[rows, :].astype(f32)) + grad_y2[rows, :]
        normed = normed1[rows, :]
        sums[0:1, :] += jnp.sum(grad_hidden * normed, axis=0, keepdims=True)
        sums[1:2, :] += jnp.sum(grad_hidden, axis=0, keepdims=True)
        grad = norm_back(grad_hidden, normed, inverse1[rows, 0:1], gain1[...])
        grad_y1[rows, :] = grad
        low = grad.astype(bf16)
        grad_branch[rows, :] = low
        sums[2:3, :] += jnp.sum(low.astype(f32), axis=0, keepdims=True)
        back = dot_nt(low, w_out[...]).astype(bf16)
        for pair in range(pairs):
            grad_attended[pair, rows, :] = back[:, pair * 128 : (pair + 1) * 128]
            grad_key[pair, rows, :] = jnp.zeros((BLOCK, 128), f32)
            grad_value[pair, rows, :] = jnp.zeros((BLOCK, 128), f32)
        return unused

    lax.fori_loop(0, meta[4], first_norm, 0)
    over_blocks(0, meta[4], inward, wait)

    def one_sequence(second, unused):
        offset = second * meta[0]

        def sized(blocks):
            count = blocks * BLOCK
            wide = min(count, 256)
            every = rows_at(offset, blocks)

            def one_head(head, unused):
                pair = head // 2
                lane = lax.broadcasted_iota(jnp.int32, (wide, 128), 1)
                mine = (lane >= 64) == (head % 2 == 1)
                head_rows = pl.ds(pl.multiple_of(head * 64, 64), 64)
                values = value3[pair, every, :]
                keys = key_t[head_rows, every]
                probs_copy(probs_in, probs_t, probs_sems, second, head, offset, blocks).wait()
                for column in range(count // wide):
                    lanes = slice(column * wide, (column + 1) * wide)
                    places = rows_at(offset + column * (wide // BLOCK), wide // BLOCK)
                    zero = jnp.zeros((), bf16)
                    back = jnp.where(mine, grad_attended[pair, places, :], zero)
                    queries = jnp.where(mine, query3[pair, places, :], zero)
                    grad_probs = dot_nt(values, back)
                    probs_low = probs_t[head, every, lanes]
                    probs = probs_low.astype(f32)
                    mean = jnp.sum(probs * grad_probs, axis=0, keepdims=True)
                    grad_scores = (probs * (grad_probs - mean)).astype(bf16)
                    probs_t[head, every, lanes] = grad_scores
                    grad_value[pair, every, :] += dot_nn(probs_low, back)
                    grad_key[pair, every, :] += dot_nn(grad_scores, queries)
                    grad_query_t[head_rows, places] = dot_nn(keys, grad_scores)
                probs_copy(probs_t, grad_scores_out, scores_sems, second, head, offset, blocks).start()
                return unused

            lax.fori_loop(0, heads, one_head, 0)

        by_length(meta, second, sized)
        return unused

    lax.fori_loop(0, 2, one_sequence, 0)
    for copy in weights[1:]:
        copy.wait()

    def gather_grads(block, unused):
        rows = rows_at(block)
        query = (grad_query_t[:, rows].T * scale).astype(bf16)
        grad_qkv[rows, :local] = query
        for pair in range(pairs):
            lanes = slice(pair * 128, (pair + 1) * 128)
            grad_qkv[rows, local + pair * 128 : local + (pair + 1) * 128] = grad_key[pair, rows, :].astype(bf16)
            value = grad_value[pair, rows, :].astype(bf16)
            grad_qkv[rows, 2 * local + pair * 128 : 2 * local + (pair + 1) * 128] = value
            sums_qv[1:2, lanes] += jnp.sum(value.astype(f32), axis=0, keepdims=True)
        sums_qv[0:1, :] += jnp.sum(query.astype(f32), axis=0, keepdims=True)
        total = dot_nt(query, w_query[...])
        total = total + dot_nt(grad_qkv[rows, local : 2 * local], w_key[...])
        total = total + dot_nt(grad_qkv[rows, 2 * local :], w_value[...])
        part[rows, :] = total.astype(bf16)
        return unused

    lax.fori_loop(0, meta[4], gather_grads, 0)
    zero_tail(meta, grad_qkv)
    zero_tail(meta, grad_branch)
    over_probs(meta, probs_t, grad_scores_out, scores_sems, wait)


def attention_weights(
    meta, slots, x, grad_qkv, own0, own1, own2, own3, grad_branch, keep, give, stacked, attended, packed_x, sems, in_sems
):
    x_copy = packing_copy(meta, x, packed_x, in_sems)
    over_blocks(0, meta[4], [x_copy], start)
    zero_tail(meta, packed_x)
    copies = piece_copies(meta, (own0, own1, own2, own3), attended, sems, False)
    start_copies(meta, copies)
    width = packed_x.shape[1]
    local = attended.shape[1]
    wait_copies(meta, copies)
    over_blocks(0, meta[4], [x_copy], wait)

    def sized(count):
        def project(tile, unused):
            lanes = pl.ds(pl.multiple_of(tile * 256, 256), 256)
            product = dot_tn(packed_x[:count, lanes], grad_qkv[:count, :])
            for part in range(3):
                spot = pl.ds(pl.multiple_of(part * width + tile * 256, 256), 256)
                stacked[spot, :] = product[:, part * local : (part + 1) * local]
            return unused

        lax.fori_loop(0, width // 256, project, 0)
        product = dot_tn(attended[:count, :], grad_branch[:count, :])
        for half in range(width // local):
            first = 3 * width + half * local
            stacked[first : first + local, :] = product[:, half * local : (half + 1) * local]

    by_cap(meta, sized)
    scatter_chunks(slots, keep, give, stacked)


def table_histogram(part, meta, grad_scores_t, buckets, total, left, right):
    heads = grad_scores_t.shape[0]
    group = 16
    total[...] = jnp.zeros(total.shape, f32)

    def one_sequence(second, unused):
        offset = second * meta[0]

        def sized(blocks):
            count = blocks * BLOCK
            upper_digit = lax.broadcasted_iota(jnp.int32, (32, count), 0)
            lower_digit = lax.broadcasted_iota(jnp.int32, (8, count), 0)

            def one_group(index, unused):
                rows = pl.ds(pl.multiple_of(index * group, group), group)
                spots = pl.ds(pl.multiple_of(offset * BLOCK + index * group, group), group)
                bucket = buckets[rows, :count]
                upper = bucket >> 3
                lower = bucket & 7
                grads = [grad_scores_t[head, spots, :count].astype(f32) for head in range(heads)]
                for row in range(group):
                    lanes = slice(row * count, (row + 1) * count)
                    left[:, lanes] = jnp.where(upper_digit == upper[row : row + 1, :], 1.0, 0.0).astype(bf16)
                    chosen = lower_digit == lower[row : row + 1, :]
                    for head in range(0, heads, 2):
                        spread = jnp.concatenate(
                            [jnp.where(chosen, grads[head + odd][row : row + 1, :], 0.0) for odd in range(2)], axis=0
                        )
                        right[head * 8 : (head + 2) * 8, lanes] = spread.astype(bf16)
                total[...] += dot_nt(right[:, : group * count], left[:, : group * count])
                return unused

            groups = count // group
            lax.fori_loop(groups * part // TABLE_PARTS, groups * (part + 1) // TABLE_PARTS, one_group, 0)

        by_length(meta, second, sized)
        return unused

    lax.fori_loop(0, 2, one_sequence, 0)


def input_gradient(meta, grad_y1, own, got, out):
    out[...] = jnp.zeros(out.shape, f32)

    def one_block(block, unused):
        second, first_row = place_of(meta, block)
        rows = rows_at(block)
        live = live_rows(meta, second, first_row)
        total = (own[rows, :].astype(f32) + got[rows, :].astype(f32)) + grad_y1[rows, :]
        out[second, pl.ds(first_row, BLOCK), :] = jnp.where(live, total, 0.0)
        return unused

    lax.fori_loop(0, meta[4], one_block, 0)


def pack_small(sums2, sums_up, sums1, sums_qv, *refs):
    tables, out = refs[:-1], refs[-1]
    out[...] = jnp.zeros(out.shape, f32)
    row = 0
    for source, count in ((sums2, 3), (sums_up, 1), (sums1, 3), (sums_qv, 2)):
        for line in range(count):
            for column in range(source.shape[1] // 128):
                out[row : row + 1, :] = source[line : line + 1, column * 128 : (column + 1) * 128]
                row += 1
    height, wide = tables[0].shape
    first = out.shape[0] - height
    out[first:, :wide] = sum(table[...] for table in tables)


def unpack(first_place, count, targets_of, places, *refs):
    chunks, (wide, sems) = refs[:count], refs[-2:]
    outs, token = refs[-3 - targets_of.outs : -3], refs[-3]
    token[...] = jnp.zeros(token.shape, f32)
    rows = chunks[0].shape[0]
    copies = []
    for index, chunk in enumerate(chunks):
        wide[index] = chunk[...].astype(f32)
        first = places[first_place + index] * rows
        for low, high, target in targets_of(outs, rows):
            inside = (first >= low) & (first < high)
            copy = pltpu.make_async_copy(
                wide.at[index], target(pl.ds(pl.multiple_of(first - low, 8), rows)), sems.at[index]
            )
            copies.append((inside, copy))

            @pl.when(inside)
            def _():
                copy.start()

    for inside, copy in copies:
        @pl.when(inside)
        def _():
            copy.wait()


def ffn_targets(outs, rows):
    grad_up, grad_down = outs
    units, width = grad_down.shape
    found = [(0, units, lambda spot: grad_down.at[spot, :])]
    for half in range(units // width):
        lanes = pl.ds(half * width, width)
        low = units + half * width
        found.append((low, low + width, lambda spot, lanes=lanes: grad_up.at[spot, lanes]))
    return found


def attention_targets(outs, rows):
    width, local = outs[0].shape
    found = []
    for part in range(3):
        found.append((part * width, (part + 1) * width, lambda spot, part=part: outs[part].at[spot, :]))
    for half in range(width // local):
        lanes = pl.ds(half * local, local)
        low = 3 * width + half * local
        found.append((low, low + local, lambda spot, lanes=lanes: outs[3].at[spot, lanes]))
    return found


ffn_targets.outs = 2
attention_targets.outs = 4


spaces = {"s": in_smem, "v": in_vmem, "a": in_any, "h": in_hbm}


def run(kernel, specs, outs, scratch, name, room, aliases={}):
    params = pltpu.CompilerParams(vmem_limit_bytes=room * 1024 * 1024)

    def call(*args):
        return pl.pallas_call(
            kernel,
            in_specs=[spaces[kind] for kind in specs],
            out_specs=[spaces[kind] for kind, unused in outs],
            out_shape=[pltpu.HBM(shape.shape, shape.dtype) if kind == "h" else shape for kind, shape in outs],
            scratch_shapes=scratch,
            compiler_params=params,
            input_output_aliases=aliases,
            name=name,
        )(
            *[
                pltpu.with_memory_space_constraint(arg, pltpu.HBM) if kind == "h" else arg
                for kind, arg in zip(specs, args)
            ]
        )

    return call


class Unpacker:
    def __init__(self, places, targets_of, shapes, name, parts, dp_count):
        chips = dp_count // 2
        self.places = jnp.stack([places[:chips], places[chips:]], axis=1).reshape(-1)
        self.targets_of, self.shapes, self.name = targets_of, shapes, name
        self.ends = [chips * (part + 1) // parts for part in range(parts)]
        self.done, self.made, self.tokens = 0, [], []
        self.pairs = siblings(dp_count)

    def next(self, own, earlier=()):
        first, last = self.done, self.ends[len(self.tokens)]
        pieces = []
        for piece in own[first:last]:
            pieces += [piece, lax.ppermute(piece, "dp", self.pairs)]
        rows, columns = own[0].shape
        count = len(pieces)
        *self.made, token = run(
            functools.partial(unpack, 2 * first, count, self.targets_of),
            "s" + "v" * count + "a" * (len(self.made) + len(earlier)),
            [("a", shape) for shape in self.shapes] + [("v", shape_of((8, 128), f32))],
            [pltpu.VMEM((count, rows, columns), f32), pltpu.SemaphoreType.DMA((count,))],
            f"{self.name}{len(self.tokens)}",
            8,
            {1 + count + index: index for index in range(len(self.made))},
        )(self.places, *pieces, *self.made, *earlier)
        self.tokens.append(token)
        self.done = last
        return token


def swap_tensor(value):
    return lax.ppermute(value, "tensor", ((0, 1), (1, 0)))


def exchange_within(pieces, level, least=1):
    def branch(swapped):
        return lambda *given: tuple(
            swap_tensor(piece) if index < swapped else piece for index, piece in enumerate(given)
        )

    return lax.switch(level, [branch(least + step) for step in range(len(CAPS))], *pieces)


def exchange(pieces, level):
    return swap_tensor(pieces[0]), *exchange_within(pieces[1:], level, 0)


def ring_pairs(dp_count):
    chips = dp_count // 2
    order = list(range(0, chips, 2)) + list(range(chips - 1, 0, -2))
    pairs = []
    for place, chip in enumerate(order):
        after = order[(place + 1) % chips]
        pairs.append((2 * chip, 2 * after))
        pairs.append((2 * after + 1, 2 * chip + 1))
    return tuple(pairs)


def fold_bits(chips):
    bits = [1]
    bit = chips // 2
    while bit > 1:
        bits.append(bit)
        bit //= 2
    return bits


def ring_places(dp_count):
    chips = dp_count // 2
    index = lax.axis_index("dp")
    chip, core = index // 2, index % 2
    position = lambda at: jnp.where(at % 2 == 0, at // 2, chips - 1 - at // 2)
    steps = jnp.arange(chips, dtype=jnp.int32)
    mine, theirs = core * chips, (1 - core) * chips
    offsets = [
        sum(bit for step, bit in enumerate(fold_bits(chips)) if slot & (chips >> (step + 1))) for slot in range(chips)
    ]
    targets = position(chip ^ jnp.array(offsets, jnp.int32))
    turn = steps * (1 - 2 * core)
    own_chunks = mine + (position(chip) - turn) % chips
    other_chunks = theirs + (position(chip) + turn) % chips
    slots = jnp.concatenate([mine + targets, theirs + targets])
    return slots.astype(jnp.int32), jnp.concatenate([own_chunks, other_chunks]).astype(jnp.int32)


def siblings(dp_count):
    return tuple((i, i ^ 1) for i in range(dp_count))


def fold(parts, stage, dp_count, room, name):
    keep, give = parts
    if stage == 0:
        pairs = siblings(dp_count)
    else:
        distance = 2 * fold_bits(dp_count // 2)[stage - 1]
        pairs = tuple((i, i ^ distance) for i in range(dp_count))
    got = lax.ppermute(give, "dp", pairs)
    count = keep.shape[0]
    halves = [count // 2, count // 2] if count > 1 else [1]
    outs = [("v", shape_of((half, *keep.shape[1:]), bf16)) for half in halves]
    return run(add_halves, "vv", outs, [], f"{name}{stage}", room)(keep, got)


def gather_both(first, second, dp_count, fill):
    pairs = ring_pairs(dp_count)
    one, two = [first], [second]
    for step in range(dp_count // 2 - 1):
        moving = after(one[step], *two[: step][-1:], *fill(step, one, two))
        one.append(lax.ppermute(moving, "dp", pairs))
        moving = after(two[step], one[step])
        two.append(lax.ppermute(moving, "dp", pairs))
    return one, two


def later(parts, *earlier):
    return after(parts[0], *earlier), parts[1]


def after(value, *earlier):
    return lax.optimization_barrier((value, earlier))[0]


def add_small(value, bit, mark, dp_count):
    got = lax.ppermute(value, "dp", tuple((i, i ^ bit) for i in range(dp_count)))
    return value + after(got, mark)


def per_device(dp_count, *arrays):
    (
        inputs, lengths, buckets, w_query, b_query, w_key, w_value, b_value, w_out, b_out, norm1_gain, norm1_shift,
        w_up, b_up, w_down, b_down, norm2_gain, norm2_shift, position_table, cotangent,
    ) = arrays
    micro, seqs, seq_len, width = inputs.shape
    bucket_count, heads = position_table.shape
    local = w_query.shape[1]
    units = w_up.shape[1]
    chips = dp_count // 2
    rows = micro * seq_len
    x = inputs.reshape(micro, seq_len, width)
    grad_out = cotangent.reshape(micro, seq_len, width)
    (meta,) = run(block_table, "s", [("s", shape_of((8,), jnp.int32))], [], "block_table", 1)(lengths)
    level = meta[6]
    slots, places = ring_places(dp_count)
    buckets_t = buckets.T
    table = position_table.T
    row = lambda vector: vector.reshape(1, -1)
    ends = [0, *(most * BLOCK for most in CAPS[:-1]), rows]
    piece_rows = [last - first for first, last in zip(ends, ends[1:])]
    pieces = lambda columns: [("a", shape_of((count, columns), bf16)) for count in piece_rows]
    vmem = pltpu.VMEM
    dma = pltpu.SemaphoreType.DMA

    w_out_got = swap_tensor(w_out)
    blocks_most = rows // BLOCK
    query3, value3, key_t, probs_t, *attended = run(
        attention_forward,
        "shhvhhvvv",
        [
            ("h", shape_of((heads // 2, rows, 128), bf16)),
            ("h", shape_of((heads // 2, rows, 128), bf16)),
            ("h", shape_of((local, rows), bf16)),
            ("h", shape_of((heads, rows, seq_len), bf16)),
            *pieces(local),
        ],
        [
            vmem((rows, width), bf16),
            *[vmem((width, local), bf16)] * 3,
            *[vmem((heads // 2, rows, 128), bf16)] * 3,
            vmem((local, rows), bf16),
            vmem((heads, rows, seq_len), bf16),
            vmem((heads, seq_len, seq_len), f32),
            vmem((local, rows), bf16),
            vmem((local, rows), f32),
            vmem((rows, local), bf16),
            dma((len(CAPS),)),
            dma((blocks_most,)),
            dma((3,)),
            dma((3, blocks_most)),
            dma((2, heads)),
        ],
        "attention_forward",
        27,
    )(meta, x, w_query, row(b_query), w_key, w_value, row(b_value), buckets_t, table)
    attended_got = exchange(attended, level)

    normed1, inverse1, hidden_low, activated, slope, *unit_part = run(
        feed_forward,
        "shaaaaaaaahhvvvhvh",
        [
            ("h", shape_of((rows, width), f32)),
            ("h", shape_of((rows, 128), f32)),
            ("h", shape_of((rows, width), bf16)),
            ("h", shape_of((rows, units), bf16)),
            ("h", shape_of((rows, units), bf16)),
            *pieces(width),
        ],
        [
            vmem((rows, local), bf16),
            vmem((rows, local), bf16),
            vmem((rows, width), bf16),
            vmem((rows, width), bf16),
            vmem((local, width), bf16),
            vmem((local, width), bf16),
            vmem((width, units), bf16),
            vmem((units, width), bf16),
            vmem((rows, width), f32),
            vmem((rows, 128), f32),
            vmem((rows, width), bf16),
            vmem((rows, units), bf16),
            vmem((rows, units), bf16),
            dma((2, len(CAPS))),
            dma((blocks_most,)),
            dma((4,)),
            dma((5, blocks_most)),
        ],
        "feed_forward",
        26,
    )(
        meta, x, *attended, *attended_got, w_out, w_out_got, row(b_out), row(norm1_gain), row(norm1_shift),
        w_up, row(b_up), w_down,
    )
    unit_got = exchange(unit_part, level)

    layer_output, grad_y2, grad_ffn, grad_upper, sums2, sums_up, *hidden_part = run(
        second_norm,
        "shaaaaaaaahvvvvvhhh",
        [
            ("h", shape_of((micro, seq_len, width), bf16)),
            ("h", shape_of((rows, width), f32)),
            ("v", shape_of((rows, width), bf16)),
            ("v", shape_of((rows, units), bf16)),
            ("v", shape_of((8, width), f32)),
            ("v", shape_of((1, units), f32)),
            *pieces(width),
        ],
        [
            vmem((rows, width), bf16),
            vmem((rows, width), bf16),
            vmem((rows, width), bf16),
            vmem((rows, width), f32),
            vmem((rows, width), bf16),
            vmem((units, width), bf16),
            vmem((width, units), bf16),
            vmem((rows, units), bf16),
            vmem((micro, seq_len, width), bf16),
            vmem((rows, width), f32),
            dma((2, len(CAPS))),
            dma((3, blocks_most)),
            dma((2,)),
            dma((blocks_most,)),
            dma((1,)),
        ],
        "second_norm",
        26,
    )(
        meta, grad_out, *unit_part, *unit_got, normed1, row(norm1_gain), row(norm1_shift), row(b_down),
        row(norm2_gain), row(norm2_shift), w_down, w_up, slope,
    )
    stacked_ffn = 2 * units
    ffn_parts = run(
        ffn_weights,
        "ssvvvv",
        [("v", shape_of((chips, stacked_ffn // (2 * chips), width), bf16))] * 2,
        [vmem((stacked_ffn, width), f32)],
        "ffn_weights",
        14,
    )(meta, slots, activated, grad_ffn, hidden_low, grad_upper)
    hidden_got = exchange_within(hidden_part, after(level, ffn_parts[0]))
    ffn_parts = fold(later(ffn_parts, hidden_got[0]), 0, dp_count, 8, "ffn_fold")

    grad_y1, grad_branch, grad_qkv, grad_scores_t, sums1, sums_qv, input_part = run(
        attention_backward,
        "saaaaaaaahhhvhhhhhhhh",
        [
            ("v", shape_of((rows, width), f32)),
            ("v", shape_of((rows, width), bf16)),
            ("v", shape_of((rows, 3 * local), bf16)),
            ("h", shape_of((heads, rows, seq_len), bf16)),
            ("v", shape_of((8, width), f32)),
            ("v", shape_of((8, local), f32)),
            ("v", shape_of((rows, width), bf16)),
        ],
        [
            vmem((rows, width), bf16),
            vmem((rows, width), bf16),
            vmem((heads // 2, rows, 128), bf16),
            vmem((local, rows), f32),
            vmem((heads // 2, rows, 128), f32),
            vmem((heads // 2, rows, 128), f32),
            vmem((rows, width), f32),
            vmem((rows, width), f32),
            vmem((rows, 128), f32),
            vmem((local, width), bf16),
            *[vmem((width, local), bf16)] * 3,
            *[vmem((heads // 2, rows, 128), bf16)] * 2,
            vmem((local, rows), bf16),
            vmem((heads, rows, seq_len), bf16),
            dma((2, len(CAPS))),
            dma((6, blocks_most)),
            dma((4,)),
            dma((2, heads)),
            dma((2, heads)),
        ],
        "attention_backward",
        32,
    )(
        after(meta, ffn_parts[0]), *hidden_part, *hidden_got, grad_y2, normed1, inverse1, row(norm1_gain), w_out, w_query, w_key, w_value,
        query3, value3, key_t, probs_t,
    )
    input_got = swap_tensor(input_part)

    stacked_attention = 3 * width + width * local // local
    attention_parts = run(
        attention_weights,
        "sshvaaaav",
        [("v", shape_of((chips, stacked_attention // (2 * chips), local), bf16))] * 2,
        [
            vmem((stacked_attention, local), f32),
            vmem((rows, local), bf16),
            vmem((rows, width), bf16),
            dma((len(CAPS),)),
            dma((blocks_most,)),
        ],
        "attention_weights",
        11,
    )(meta, slots, x, grad_qkv, *attended, grad_branch)

    table_sums = []

    def add_table(earlier):
        part = len(table_sums)
        table_sums.extend(
            run(
                functools.partial(table_histogram, part),
                "svv",
                [("v", shape_of((8 * heads, 32), f32))],
                [vmem((32, 16 * seq_len), bf16), vmem((8 * heads, 16 * seq_len), bf16)],
                f"table_histogram{part}",
                10,
            )(after(meta, *earlier), grad_scores_t, buckets_t)
        )

    stages = len(fold_bits(chips)) + 1
    ffn_parts = fold(later(ffn_parts, attention_parts[0]), 1, dp_count, 8, "ffn_fold")
    attention_parts = later(attention_parts, ffn_parts[0])
    for stage in range(stages):
        attention_parts = fold(later(attention_parts, *table_sums[-1:]), stage, dp_count, 4, "attention_fold")
        if stage == 0:
            add_table(attention_parts)
        elif stage + 1 < stages:
            ffn_parts = fold(later(ffn_parts, attention_parts[0]), stage + 1, dp_count, 8, "ffn_fold")
        for unused in range((3, 2)[stage] if stage < 2 else 0):
            add_table([*attention_parts, table_sums[-1]])
    attention_own = attention_parts[0][0]
    unpack_up = Unpacker(
        places,
        ffn_targets,
        [shape_of((width, units), f32), shape_of((units, width), f32)],
        "unpack_ffn",
        UNPACK_PARTS,
        dp_count,
    )
    unpack_heads = Unpacker(
        places,
        attention_targets,
        [shape_of((width, local), f32)] * 3 + [shape_of((local, width), f32)],
        "unpack_attention",
        2,
        dp_count,
    )

    table_rows = 8 * heads
    vector_rows = (6 * width + units + 2 * local) // 128
    small_rows = -(-vector_rows // 8) * 8 + table_rows
    (small,) = run(
        pack_small,
        "v" * (4 + TABLE_PARTS),
        [("v", shape_of((small_rows, 128), f32))],
        [],
        "pack_small",
        4,
    )(sums2, sums_up, sums1, sums_qv, *table_sums)
    sums = [small]
    small_steps = dp_count.bit_length() - 1

    def fill(step, pieces, gathered):
        waits = []
        if 0 < step <= small_steps:
            sums.append(add_small(sums[-1], 1 << (step - 1), gathered[step - 1], dp_count))
        if step <= small_steps:
            waits.append(sums[-1])
        if step in (3 * chips // 8, 5 * chips // 8, 6 * chips // 8):
            waits.append(unpack_up.next(pieces))
        return waits

    ffn_pieces, attention_pieces = gather_both(ffn_parts[0][0], attention_own, dp_count, fill)
    unpack_up.next(ffn_pieces)
    unpack_heads.next(attention_pieces, unpack_up.tokens)
    unpack_heads.next(attention_pieces)
    grad_w_up, grad_w_down = unpack_up.made
    grad_w_query, grad_w_key, grad_w_value, grad_w_out = unpack_heads.made

    (grad_inputs,) = run(
        input_gradient,
        "svvv",
        [("v", shape_of((micro, seq_len, width), f32))],
        [],
        "input_gradient",
        12,
    )(meta, grad_y1, input_part, input_got)

    small = sums[-1]
    table_grad = small[small_rows - table_rows :, :32].reshape(heads, 8, 32).transpose(2, 1, 0)
    small = small[:vector_rows].reshape(-1)
    cuts = []
    start = 0
    for count in (width, width, width, units, width, width, width, local, local):
        cuts.append(small[start : start + count])
        start += count
    grad_gain2, grad_shift2, grad_b_down, grad_b_up, grad_gain1, grad_shift1, grad_b_out, grad_b_query, grad_b_value = cuts
    return (
        layer_output.reshape(inputs.shape),
        grad_inputs.reshape(inputs.shape),
        grad_w_query,
        grad_b_query,
        grad_w_key,
        grad_w_value,
        grad_b_value,
        grad_w_out,
        grad_b_out,
        grad_gain1,
        grad_shift1,
        grad_w_up,
        grad_b_up,
        grad_w_down,
        grad_b_down,
        grad_gain2,
        grad_shift2,
        table_grad.reshape(bucket_count, heads),
    )


def solution(mesh):
    placed = (
        P(None, "dp", None, None),
        P(None, "dp"),
        P(),
        P(None, "tensor"),
        P("tensor"),
        P(None, "tensor"),
        P(None, "tensor"),
        P("tensor"),
        P("tensor", None),
        P(),
        P(),
        P(),
        P(None, "tensor"),
        P("tensor"),
        P("tensor", None),
        P(),
        P(),
        P(),
        P(None, "tensor"),
        P(None, "dp", None, None),
    )
    dp_count = mesh.shape["dp"]
    return jax.shard_map(
        lambda *arrays: per_device(dp_count, *arrays),
        mesh=mesh,
        in_specs=placed,
        out_specs=(
            P(None, "dp", None, None),
            P(None, "dp", None, None),
            P(None, "tensor"),
            P("tensor"),
            P(None, "tensor"),
            P(None, "tensor"),
            P("tensor"),
            P("tensor", None),
            P(),
            P(),
            P(),
            P(None, "tensor"),
            P("tensor"),
            P("tensor", None),
            P(),
            P(),
            P(),
            P(None, "tensor"),
        ),
        check_vma=False,
    )
```
